32 devices in a mesh: dp: 8 (over z, x), expert: 4 (over y, core).
Axes of the slice: x: 2, y: 2, z: 4, core: 2. Of those that a mesh axis runs over, the one named last changes fastest.
Arguments:
- tokens: bfloat16 [24576, 768], P(('dp', 'expert')), may hold values from -6 to 6
- prev_logits: bfloat16 [24576, 8], P(('dp', 'expert')), may hold values from -3 to 3
- segment_ids: int32 [32, 768], P(('dp', 'expert')), may hold values from 0 to 7, never falling along the last dimension, each value on 1 to 384 neighbouring positions
- pad_mask: int32 [32, 768], P(('dp', 'expert')), may hold values 0 or 1
- routes: int32 [32, 768, 2], P(('dp', 'expert')), may hold values from 0 to 7, all different within a row
- slot_order: int32 [32, 1536], P(('dp', 'expert')), may hold values from 0 to 1535, each once within a row
- cotangent: bfloat16 [24576, 768], P(('dp', 'expert')), may hold values from -6 to 6
- attn_gain: bfloat16 [768], P('dp'), may hold values from 0.5 to 1.5
- qkv_weight: bfloat16 [768, 2304], P('dp'), may hold values from -0.21875 to 0.21875
- out_weight: bfloat16 [768, 768], P('dp'), may hold values from -0.875 to 0.875
- ffn_gain: bfloat16 [768], P('dp'), may hold values from 0.5 to 1.5
- router_weight: bfloat16 [768, 8], P('dp'), may hold values from -0.109375 to 0.109375
- mix_weight: bfloat16 [768, 4], P('dp'), may hold values from -0.21875 to 0.21875
- const_weight: bfloat16 [768, 2], P('dp'), may hold values from -5 to 5
- gate_up_weight: bfloat16 [4, 768, 4096], P('expert', 'dp'), may hold values from -0.21875 to 0.21875
- down_weight: bfloat16 [4, 2048, 768], P('expert', 'dp'), may hold values from -0.25 to 0.25
Outputs:
- layer_out: bfloat16 [24576, 768], P(('dp', 'expert'))
- tokens_grad: float32 [24576, 768], P(('dp', 'expert'))
- prev_grad: float32 [24576, 8], P(('dp', 'expert'))
- attn_gain_grad: float32 [768], P('dp')
- qkv_weight_grad: float32 [768, 2304], P('dp')
- out_weight_grad: float32 [768, 768], P('dp')
- ffn_gain_grad: float32 [768], P('dp')
- router_weight_grad: float32 [768, 8], P('dp')
- mix_weight_grad: float32 [768, 4], P('dp')
- const_weight_grad: float32 [768, 2], P('dp')
- gate_up_grad: float32 [4, 768, 4096], P('expert', 'dp')
- down_grad: float32 [4, 2048, 768], P('expert', 'dp')
The draws below stay inside these ranges and needn't reach their ends.
Inputs may be any that keep to these rules, and one draw needn't show every extreme that they name: Each token names two different routes; below 4 the SwiGLU experts, 4 the zero expert, 5 the copy expert, 6 and 7 the constant experts. `slot_order`: each row is a permutation; entry 2 t + k ranks route k of token t. `segment_ids`: never falling along a row. `pad_mask`: 1 marks a real token, 0 padding.
All inputs are finite; a program needn't handle non-finite values. No bound on the sum of `pad_mask` on one device may be relied on, other than what follows from the above.
Results may differ from the reference program's by a relative error of at most 0.02.
Values may be sent and summed in bfloat16 or wider, within the bound.
A program may use at most 192 MiB of HBM per device.

```python
import math
import jax
import jax.numpy as jnp
import numpy as np
from jax import lax

D = 768
HEADS = 12
HEAD_DIM = 64
FF = 2048
TOK_DEV = 768
EXPERTS = 4
ROUTES = 8
SEQS = 32
TOKENS = 24576
CAP = 192


def place_ends(array, key, smallest, top_value):
    longest = array.shape.index(max(array.shape))
    spots = []
    for shift in (0, 1):
        where = [jax.random.randint(jax.random.fold_in(key, axis), (), 0, length) for axis, length in enumerate(array.shape)]
        where[longest] = (where[longest] + shift) % array.shape[longest]
        spots.append(tuple(where))
    return array.at[spots[0]].set(smallest).at[spots[1]].set(top_value)


def level_of(own_key, extent, cuts, least, largest):
    level, own = 1.0, jax.random.fold_in(own_key, 6)
    for position, parts in cuts:
        steps = jnp.exp(jax.random.uniform(jax.random.fold_in(own, position), (parts,), jnp.float32, least / len(cuts), largest / len(cuts)))
        level = level * jnp.repeat(steps, extent[position] // parts).reshape([-1 if axis == position else 1 for axis in range(len(extent))])
    return level


def different_ones(key, rows, number_of, top, lift):
    sequence = jax.random.permutation(jax.random.fold_in(key, 1), number_of)
    boost = sequence
    for power in range(3):
        boost = boost * boost // number_of
    boost = boost * lift // number_of
    chance = jax.random.randint(jax.random.fold_in(key, 2), (rows, number_of), 0, 4096) + boost
    fixed_rows = jax.random.permutation(jax.random.fold_in(key, 3), rows)[jnp.arange(number_of) % rows]
    chance = jnp.where(jnp.arange(rows)[:, None] == fixed_rows[None, :], 1 << 14, chance)
    score = chance * number_of + jnp.arange(number_of)
    return lax.top_k(score.astype(jnp.int32), top)[1].astype(jnp.int32)


def length_profile(count, total, most, skew):
    loads = [(1 << 20) // math.isqrt(standing ** skew) + 1 for standing in range(2, count + 1)]
    surplus, holding = total - most - (count - 1), [1] * (count - 1)
    while surplus > 0:
        movable = [i for i in range(count - 1) if holding[i] < most]
        whole, remaining = sum([loads[i] for i in movable]), surplus
        for i in movable:
            extra = min(most - holding[i], max(1, remaining * loads[i] // whole), surplus)
            holding[i] = holding[i] + extra
            surplus = surplus - extra
    return np.array([most] + holding)


def uneven_parts(key, amount, total, most, lean):
    if amount == 2:
        one = jax.random.randint(key, (), max(1, total - most), min(most, total - 1) + 1)
        return jnp.stack([one, total - one])
    lengths = jnp.asarray(length_profile(amount, total, most, lean), jnp.int32)
    pairs = (amount - 1) // 2
    source_of, taker = lengths[1:1 + 2 * pairs:2], lengths[2:2 + 2 * pairs:2]
    room = jnp.minimum(source_of - 1, most - taker)
    shifted = jax.random.randint(jax.random.fold_in(key, 1), (pairs,), 0, 1 << 20) % (room + 1)
    lengths = lengths.at[1:1 + 2 * pairs:2].set(source_of - shifted).at[2:2 + 2 * pairs:2].set(taker + shifted)
    return lengths[jax.random.permutation(jax.random.fold_in(key, 2), amount)]


def noise(own_key, shape, deviation, reach, cuts=(), dtype=jnp.bfloat16):
    values = deviation * jax.random.normal(own_key, shape, jnp.float32)
    if cuts:
        values = values * level_of(own_key, shape, cuts, -0.22, 0.18)
    return jnp.clip(values, -reach, reach).astype(dtype)


def setup_inputs(seed: int = 0) -> dict:
    arg_keys = jax.random.split(jax.random.key(seed), 17)
    return {
        "tokens": noise(arg_keys[0], (TOKENS, D), 1.0, 6.0, ((0, 32),)),
        "prev_logits": noise(arg_keys[1], (TOKENS, ROUTES), 0.5, 3.0, ((0, 32),)),
        "segment_ids": jax.vmap(lambda own: jnp.searchsorted(jnp.cumsum(uneven_parts(own, 8, TOK_DEV, TOK_DEV // 2, 2)), jnp.arange(TOK_DEV), side="right"))(jax.random.split(arg_keys[2], SEQS)).reshape((SEQS, TOK_DEV)).astype(jnp.int32),
        "pad_mask": place_ends((jax.random.randint(arg_keys[3], (SEQS, TOK_DEV), 0, 8) < 7).astype(jnp.int32), jax.random.fold_in(arg_keys[3], 1), 0, 1),
        "routes": different_ones(arg_keys[4], SEQS * TOK_DEV, ROUTES, 2, 2048).reshape((SEQS, TOK_DEV, 2)),
        "slot_order": jax.vmap(lambda own: jax.random.permutation(own, 2 * TOK_DEV))(jax.random.split(arg_keys[5], SEQS)).reshape((SEQS, 2 * TOK_DEV)).astype(jnp.int32),
        "cotangent": noise(arg_keys[6], (TOKENS, D), 1.0, 6.0, ((0, 32),)),
        "attn_gain": jnp.clip(1.0 + 0.1 * jax.random.normal(arg_keys[7], (D,), jnp.float32), 0.5, 1.5).astype(jnp.bfloat16),
        "qkv_weight": noise(arg_keys[8], (D, 3 * D), D ** -0.5, 0.21875, ((0, 8),)),
        "out_weight": noise(arg_keys[9], (D, D), (D // 16) ** -0.5, 0.875, ((0, 8),)),
        "ffn_gain": jnp.clip(1.0 + 0.1 * jax.random.normal(arg_keys[10], (D,), jnp.float32), 0.5, 1.5).astype(jnp.bfloat16),
        "router_weight": noise(arg_keys[11], (D, ROUTES), (4 * D) ** -0.5, 0.109375, ((0, 8),)),
        "mix_weight": noise(arg_keys[12], (D, 4), D ** -0.5, 0.21875, ((0, 8),)),
        "const_weight": noise(arg_keys[13], (D, 2), 1.0, 5.0, ((0, 8),)),
        "gate_up_weight": noise(arg_keys[14], (EXPERTS, D, 2 * FF), D ** -0.5, 0.21875, ((0, 4), (1, 8))),
        "down_weight": noise(arg_keys[15], (EXPERTS, FF, D), (FF // 4) ** -0.5, 0.25, ((0, 4), (1, 8))),
    }


@jax.custom_vjp
def low(v):
    return lax.optimization_barrier(v.astype(jnp.bfloat16)).astype(jnp.float32)

@jax.custom_vjp
def low_back(v):
    return v

def low_keep(v):
    return (low(v), None)

def low_pass(kept, grad):
    return (grad,)

def back_keep(v):
    return (v, None)

def back_low(kept, grad):
    return (low(grad),)
low.defvjp(low_keep, low_pass)
low_back.defvjp(back_keep, back_low)
epsilon = 1e-06
highest = lax.Precision.HIGHEST

def matmul_high(left, right):
    return jnp.dot(left, right, precision=highest, preferred_element_type=jnp.float32)

def rms_norm(values, gain):
    return values * lax.rsqrt(lax.optimization_barrier(jnp.mean(values * values, axis=-1, keepdims=True)) + epsilon) * gain

def rope_tables(length, half):
    positions = jnp.arange(length).astype(jnp.float32)[:, None]
    inverse = 10000.0 ** (-(jnp.arange(half).astype(jnp.float32) / half))
    angles = positions * inverse[None, :]
    return (jnp.cos(angles)[:, None, :], jnp.sin(angles)[:, None, :])

def rotate(values, cosine, sine):
    half = values.shape[-1] // 2
    first = values[..., :half]
    second = values[..., half:]
    return jnp.concatenate([first * cosine - second * sine, second * cosine + first * sine], axis=-1)

def attend_sequence(normed, qkv_weight, out_weight, segments, padding, cosine, sine):
    length = normed.shape[0]
    qkv = low_back(matmul_high(normed, qkv_weight)).reshape(length, 3, HEADS, HEAD_DIM)
    queries = low(rotate(qkv[:, 0], cosine, sine) * HEAD_DIM ** (-0.5))
    key_rows = low(rotate(qkv[:, 1], cosine, sine))
    value_rows = low(qkv[:, 2])
    scores = low_back(jnp.einsum('qhd,khd->hqk', queries, key_rows, precision=highest))
    row_index = jnp.arange(length)
    allowed = (row_index[None, :] <= row_index[:, None]) & (segments[:, None] == segments[None, :]) & ((padding[None, :] == 1) | (row_index[None, :] == row_index[:, None]))
    scores = jnp.where(allowed[None], scores, -1e+30)
    probabilities = low(jax.nn.softmax(scores, axis=-1))
    attended = jnp.einsum('hqk,khd->qhd', probabilities, value_rows, precision=highest).reshape(length, -1)
    attended = low_back(low(attended))
    return low_back(matmul_high(attended, out_weight))

def expert_rows(rows, gate_up, down):
    projected = low_back(matmul_high(rows, gate_up))
    activated = low(jax.nn.silu(projected[:, :FF]) * projected[:, FF:])
    return low_back(low(matmul_high(activated, down)))

def slot_plan(routes, slot_order):

    def one_row(pair_expert, order):
        expert_range = jnp.arange(EXPERTS).astype(jnp.int32)
        onehot = (pair_expert[:, None] == expert_range[None, :]).astype(jnp.int32)
        placed = jnp.zeros_like(onehot).at[order].set(onehot)
        before = (jnp.cumsum(placed, axis=0) - placed).astype(jnp.int32)
        slot_rank = lax.optimization_barrier(jnp.sum(before[order] * onehot, axis=1)).astype(jnp.int32)
        is_kept = (pair_expert < EXPERTS) & (slot_rank < CAP)
        flat_slot = jnp.where(is_kept, pair_expert * CAP + slot_rank, EXPERTS * CAP).astype(jnp.int32)
        pair_token = (jnp.arange(2 * TOK_DEV) // 2).astype(jnp.int32)
        slot_token = jnp.zeros(EXPERTS * CAP + 1, jnp.int32).at[flat_slot].set(pair_token)[:-1]
        slot_valid = jnp.zeros(EXPERTS * CAP + 1, jnp.float32).at[flat_slot].set(1.0)[:-1]
        return (flat_slot, slot_token, slot_valid)
    return jax.vmap(one_row)(routes.reshape(SEQS, 2 * TOK_DEV), slot_order)

def forward(weights, tokens, prev_logits, plan, segment_ids, pad_mask, routes):
    gain_one, qkv_weight, out_weight, gain_two, router_weight, mix_weight, const_weight, gate_up, down = weights
    flat_slot, slot_token, slot_valid = plan
    cosine, sine = rope_tables(TOK_DEV, HEAD_DIM // 2)
    normed = low(rms_norm(tokens, gain_one))

    def one_sequence(pieces):
        return attend_sequence(pieces[0], qkv_weight, out_weight, pieces[1], pieces[2], cosine, sine)
    attn_out = lax.map(jax.checkpoint(one_sequence), (normed.reshape(SEQS, TOK_DEV, D), segment_ids, pad_mask)).reshape(TOKENS, D)
    hidden_state = tokens + attn_out
    ffn_normed = low(rms_norm(hidden_state, gain_two))
    logits = low_back(matmul_high(ffn_normed, router_weight)) + prev_logits
    route_rows = routes.reshape(TOKENS, 2)
    picked = jnp.take_along_axis(logits, route_rows, axis=1)
    gate_weights = jax.nn.softmax(picked, axis=-1)
    mix = jax.nn.softmax(low_back(matmul_high(ffn_normed, mix_weight)).reshape(TOKENS, 2, 2), axis=-1)
    is_copy = (route_rows == EXPERTS + 1).astype(jnp.float32)
    const_ids = (EXPERTS + 2 + jnp.arange(2)).astype(jnp.int32)
    is_const = (route_rows[:, :, None] == const_ids[None, None, :]).astype(jnp.float32)
    copy_coef = lax.optimization_barrier(jnp.sum(gate_weights * (is_copy + lax.optimization_barrier(jnp.sum(is_const * mix[:, None, :, 0], axis=-1))), axis=-1))
    const_coef = lax.optimization_barrier(jnp.sum(gate_weights[:, :, None] * is_const, axis=1)) * mix[:, :, 1]
    normed_seq = ffn_normed.reshape(SEQS, TOK_DEV, D)
    slots = jnp.take_along_axis(normed_seq, slot_token[:, :, None], axis=1) * slot_valid[:, :, None]
    slots = low_back(slots)
    by_expert = slots.reshape(SEQS, EXPERTS, CAP, D).transpose(1, 0, 2, 3).reshape(EXPERTS, SEQS * CAP, D)

    def one_expert(pieces):
        return expert_rows(pieces[0], pieces[1], pieces[2])
    expert_out = lax.map(jax.checkpoint(one_expert), (by_expert, gate_up, down))
    expert_out = expert_out.reshape(EXPERTS, SEQS, CAP, D).transpose(1, 0, 2, 3).reshape(SEQS, EXPERTS * CAP, D)
    padded = jnp.concatenate([expert_out, jnp.zeros((SEQS, 1, D), jnp.float32)], axis=1)
    pair_rows = jnp.take_along_axis(padded, flat_slot[:, :, None], axis=1).reshape(TOKENS, 2, D)
    branch_out = lax.optimization_barrier(jnp.sum(gate_weights[:, :, None] * pair_rows, axis=1)) + copy_coef[:, None] * ffn_normed + matmul_high(const_coef, const_weight.T)
    return hidden_state + branch_out

def reference(tokens, prev_logits, segment_ids, pad_mask, routes, slot_order, cotangent, attn_gain, qkv_weight, out_weight, ffn_gain, router_weight, mix_weight, const_weight, gate_up_weight, down_weight):
    plan = slot_plan(routes, slot_order)
    weights = (attn_gain.astype(jnp.float32), qkv_weight.astype(jnp.float32), out_weight.astype(jnp.float32), ffn_gain.astype(jnp.float32), router_weight.astype(jnp.float32), mix_weight.astype(jnp.float32), const_weight.astype(jnp.float32), gate_up_weight.astype(jnp.float32), down_weight.astype(jnp.float32))

    def wrapped(weight_set, tokens_float, prev_float):
        return forward(weight_set, tokens_float, prev_float, plan, segment_ids, pad_mask, routes)
    result, pullback = jax.vjp(wrapped, weights, tokens.astype(jnp.float32), prev_logits.astype(jnp.float32))
    weight_grads, tokens_grad, prev_grad = pullback(cotangent.astype(jnp.float32))
    return (result.astype(jnp.bfloat16), tokens_grad, prev_grad, weight_grads[0], weight_grads[1], weight_grads[2], weight_grads[3], weight_grads[4], weight_grads[5], weight_grads[6], weight_grads[7], weight_grads[8])
```

```python
import functools
import jax
import jax.numpy as jnp
from jax import lax
from jax.experimental import pallas as pl
from jax.experimental.pallas import tpu as pltpu
from jax.sharding import PartitionSpec as P

HEAD_DIM = 64

MESH = pl.DeviceIdType.MESH


class Spot:
    def __init__(self, sizes):
        self.nz, self.nx, self.ny, self.nc = sizes
        self.dp, self.ex = lax.axis_index("dp"), lax.axis_index("expert")
        self.z, self.x = lax.div(self.dp, self.nx), lax.rem(self.dp, self.nx)
        self.y, self.core = lax.div(self.ex, self.nc), lax.rem(self.ex, self.nc)

    def device(self, z=None, x=None, y=None, core=None):
        z, x = self.z if z is None else z, self.x if x is None else x
        y, core = self.y if y is None else y, self.core if core is None else core
        return {"dp": z * self.nx + x, "expert": y * self.nc + core}


def between(value, size):
    return jnp.logical_and(value >= 0, value < size)


class Flood:
    def __init__(self, spot, number, own, view, sends, recvs, z_first, mate=None):
        self.s, self.n, self.own, self.view = spot, number, own, view
        self.sends, self.recvs, self.z_first, self.mate = sends, recvs, z_first, mate
        if z_first:
            self.na, self.nb, self.a, self.b = spot.nz, spot.nx, spot.z, spot.x
        else:
            self.na, self.nb, self.a, self.b = spot.nx, spot.nz, spot.x, spot.z
        self.drains = []

    def origin(self, a, b):
        return a * self.s.nx + b if self.z_first else b * self.s.nx + a

    def along(self, which, value):
        zed = (which == 0) == self.z_first
        return self.s.device(z=value) if zed else self.s.device(x=value)

    def push(self, cond, src, o, way, device, recvs=None):
        copy = pltpu.make_async_remote_copy(
            src_ref=src, dst_ref=self.view(o),
            send_sem=self.sends.at[way, self.n, o],
            recv_sem=(self.recvs if recvs is None else recvs).at[self.n, o],
            device_id=device, device_id_type=MESH)
        if cond is None:
            copy.start()
            self.drains.append(copy.wait_send)
        else:
            pl.when(cond)(lambda: copy.start())
            self.drains.append(lambda: pl.when(cond)(lambda: copy.wait_send()))

    def share(self, cond, src, o):
        if self.mate is not None:
            self.push(cond, src, o, 4, self.s.device(core=1 - self.s.core), self.mate)

    def mates(self, view):
        def one(o, carry):
            pltpu.make_async_remote_copy(
                src_ref=view(o), dst_ref=view(o), send_sem=self.sends.at[0, self.n, o], recv_sem=self.mate.at[self.n, o],
                device_id=self.s.device(), device_id_type=MESH).wait_recv()
            return carry
        lax.fori_loop(0, self.s.nz * self.s.nx, one, 0)

    def arrive(self, o):
        pltpu.make_async_remote_copy(
            src_ref=self.view(o), dst_ref=self.view(o),
            send_sem=self.sends.at[0, self.n, o], recv_sem=self.recvs.at[self.n, o],
            device_id=self.s.device(), device_id_type=MESH).wait_recv()

    def second(self, cond, src, o):
        for j, sign in enumerate((1, -1)):
            to = self.b + sign
            if self.nb > 1:
                ok = between(to, self.nb)
                self.push(ok if cond is None else jnp.logical_and(cond, ok), src, o, 2 + j, self.along(1, to))

    def levels(self):
        out = [[] for _ in range(self.na + self.nb - 1)]

        def begin():
            o = self.origin(self.a, self.b)
            for j, sign in enumerate((1, -1)):
                if self.na > 1:
                    self.push(between(self.a + sign, self.na), self.own, o, j, self.along(0, self.a + sign))
            self.second(None, self.own, o)
            self.share(None, self.own, o)

        out[0].append(begin)
        for k in range(1, self.na):
            for j, sign in enumerate((1, -1)):
                def step(k=k, j=j, sign=sign):
                    a = self.a - sign * k
                    here = between(a, self.na)
                    o = self.origin(a, self.b)
                    pl.when(here)(lambda: self.arrive(o))
                    on = jnp.logical_and(here, between(self.a + sign, self.na))
                    if self.na > 2 or k == 0:
                        self.push(on, self.view(o), o, j, self.along(0, self.a + sign))
                    self.second(here, self.view(o), o)
                    self.share(here, self.view(o), o)
                out[k].append(step)
        for d in range(1, self.nb):
            for da in range(-(self.na - 1), self.na):
                for j, sign in enumerate((1, -1)):
                    def step(d=d, da=da, j=j, sign=sign):
                        a, b = self.a + da, self.b - sign * d
                        here = jnp.logical_and(between(a, self.na), between(b, self.nb))
                        o = self.origin(a, b)
                        pl.when(here)(lambda: self.arrive(o))
                        if self.nb > 2:
                            on = jnp.logical_and(here, between(self.b + sign, self.nb))
                            self.push(on, self.view(o), o, 2 + j, self.along(1, self.b + sign))
                        self.share(here, self.view(o), o)
                    out[abs(da) + d].append(step)
        return out


def enter(spot, devices):
    barrier = pltpu.get_barrier_semaphore()
    count = jnp.int32(0)
    for cond, device in devices:
        def hail(device=device):
            pl.semaphore_signal(barrier, inc=1, device_id=device, device_id_type=MESH)
        if cond is None:
            hail()
            count = count + 1
        else:
            pl.when(cond)(hail)
            count = count + cond.astype(jnp.int32)
    pl.semaphore_wait(barrier, count)


def line_neighbours(spot):
    out = []
    for sign in (1, -1):
        out.append((between(spot.z + sign, spot.nz), spot.device(z=spot.z + sign)))
        out.append((between(spot.x + sign, spot.nx), spot.device(x=spot.x + sign)))
    return out


def gather_kernel(sizes, chunks, qkv_ref, rest_ref, gu_ref, dn_ref, qkv_out, rest_out, gu_out, dn_out,
                  sends, recvs, mates, local):
    spot = Spot(sizes)
    enter(spot, line_neighbours(spot) + [(None, spot.device(core=1 - spot.core))])
    rows = qkv_ref.shape[0]
    rows_d, width = dn_ref.shape
    first, later = [], []
    for src, out in ((qkv_ref, qkv_out), (rest_ref, rest_out)):
        part = src.shape[1] // 2
        def half(o, core, out=out, part=part):
            return out.at[pl.ds(pl.multiple_of(o * rows, 8), rows), pl.ds(pl.multiple_of(core * part, 128), part)]
        first.append((src.at[:, pl.ds(pl.multiple_of(spot.core * part, 128), part)],
                      lambda o, half=half: half(o, spot.core), True, lambda o, half=half: half(o, 1 - spot.core)))
    part = rows_d // 2
    for p, zf in ((0, True), (1, False)):
        later.append((dn_ref.at[pl.ds(p * part, part)],
                      lambda o, p=p: dn_out.at[pl.ds(pl.multiple_of(o * rows_d + p * part, 8), part)], zf, None))
    wide = gu_ref.shape[1] // chunks
    for c in range(chunks):
        later.append((gu_ref.at[:, pl.ds(c * wide, wide)],
                      lambda o, c=c: gu_out.at[pl.ds(pl.multiple_of(o * rows, 8), rows), pl.ds(c * wide, wide)], True, None))
    keeps = []
    for n, (own, view, zf, other) in enumerate(first + later):
        keep = pltpu.make_async_copy(own, view(spot.dp), local.at[n])
        keep.start()
        keeps.append(keep)
    number = 0
    drains = []
    for group in (first, later):
        floods = []
        for own, view, zf, other in group:
            floods.append(Flood(spot, number, own, view, sends, recvs, zf, None if other is None else mates))
            number += 1
        levels = [f.levels() for f in floods]
        for level in range(max(map(len, levels))):
            for ls in levels:
                if level < len(ls):
                    for step in ls[level]:
                        step()
        for f, (own, view, zf, other) in zip(floods, group):
            if other is not None:
                f.mates(other)
            drains += f.drains
    for drain in drains:
        drain()
    for keep in keeps:
        keep.wait()


def gather_weights(sizes, qkv, rest, gu, dn, chunks=4):
    n_dp = sizes[0] * sizes[1]
    items = 4 + chunks
    arrays = (qkv, rest, gu, dn)
    return pl.pallas_call(
        functools.partial(gather_kernel, sizes, chunks),
        out_shape=tuple(jax.ShapeDtypeStruct((a.shape[0] * n_dp, a.shape[1]), a.dtype) for a in arrays),
        in_specs=[pl.BlockSpec(memory_space=pltpu.VMEM)] * 4,
        out_specs=(pl.BlockSpec(memory_space=pl.ANY),) * 4,
        scratch_shapes=[pltpu.SemaphoreType.DMA((5, items, n_dp)), pltpu.SemaphoreType.DMA((items, n_dp)),
                        pltpu.SemaphoreType.DMA((2, n_dp)), pltpu.SemaphoreType.DMA((items,))],
        compiler_params=pltpu.CompilerParams(collective_id=1, has_side_effects=True),
    )(*arrays)


def add_into(view, more):
    view[...] = (view[...].astype(jnp.float32) + more[...].astype(jnp.float32)).astype(view.dtype)


class Reduce:
    def __init__(self, spot, number, view, one, two, sends, recv_one, recv_two, x_first):
        self.s, self.n, self.view, self.one, self.two = spot, number, view, one, two
        self.sends, self.recv_one, self.recv_two, self.x_first = sends, recv_one, recv_two, x_first
        if x_first:
            self.np, self.nq, self.p, self.q = spot.nx, spot.nz, spot.x, spot.z
        else:
            self.np, self.nq, self.p, self.q = spot.nz, spot.nx, spot.z, spot.x
        self.drains = []

    def owner(self, p, q):
        return q * self.s.nx + p if self.x_first else p * self.s.nx + q

    def along(self, first, value):
        return self.s.device(x=value) if first == self.x_first else self.s.device(z=value)

    def push(self, cond, o, dst, recv, device):
        copy = pltpu.make_async_remote_copy(
            src_ref=self.view(o), dst_ref=dst, send_sem=self.sends.at[self.n, o], recv_sem=recv,
            device_id=device, device_id_type=MESH)
        pl.when(cond)(lambda: copy.start())
        self.drains.append(lambda: pl.when(cond)(lambda: copy.wait_send()))

    def take(self, cond, o, slot, recv):
        def run():
            pltpu.make_async_remote_copy(
                src_ref=slot, dst_ref=slot, send_sem=self.sends.at[self.n, o], recv_sem=recv,
                device_id=self.s.device(), device_id_type=MESH).wait_recv()
            add_into(self.view(o), slot)
        pl.when(cond)(run)

    def order(self):
        return sorted(range(-(self.nq - 1), self.nq), key=lambda d: (-abs(d), d))

    def phase_one(self):
        steps = []
        for turn in range(2):
            sign = jnp.where(self.p * 2 < self.np, 1, -1) * (1 if turn == 0 else -1)
            for k in range(self.np - 1, 0, -1):
                for dq in self.order():
                    def step(sign=sign, k=k, dq=dq):
                        p, q = self.p + sign * k, self.q + dq
                        here = jnp.logical_and(between(p, self.np), between(q, self.nq))
                        o = self.owner(p, q)
                        if self.np > 2:
                            behind = jnp.logical_and(here, between(self.p - sign, self.np))
                            self.take(behind, o, self.one.at[p, q], self.recv_one.at[self.n, p, q])
                        last = jnp.logical_and(k == 1, sign < 0)
                        slot = jnp.where(last, self.np, p)
                        self.push(here, o, self.one.at[slot, q], self.recv_one.at[self.n, slot, q],
                                  self.along(True, self.p + sign))
                    steps.append(step)
        return steps

    def settle(self, cond, q):
        o = self.owner(self.p, q)
        below = self.p > 0
        above = self.p < self.np - 1
        if cond is not None:
            below, above = jnp.logical_and(cond, below), jnp.logical_and(cond, above)
        self.take(below, o, self.one.at[self.p, q], self.recv_one.at[self.n, self.p, q])
        self.take(above, o, self.one.at[self.np, q], self.recv_one.at[self.n, self.np, q])

    def phase_two(self):
        steps = []
        for turn in range(2):
            sign = jnp.where(self.q * 2 < self.nq, 1, -1) * (1 if turn == 0 else -1)
            for k in range(self.nq - 1, 0, -1):
                def step(sign=sign, k=k):
                    q = self.q + sign * k
                    here = between(q, self.nq)
                    o = self.owner(self.p, q)
                    self.settle(here, q)
                    behind = jnp.logical_and(here, between(self.q - sign, self.nq))
                    self.take(behind, o, self.two.at[q], self.recv_two.at[self.n, q])
                    last = jnp.logical_and(k == 1, sign < 0)
                    slot = jnp.where(last, self.nq, q)
                    self.push(here, o, self.two.at[slot], self.recv_two.at[self.n, slot], self.along(False, self.q + sign))
                steps.append(step)
        return steps

    def finish(self, out):
        o = self.owner(self.p, self.q)
        self.settle(None, self.q)
        out[...] = self.view(o)[...].astype(jnp.float32)
        for cond, slot in ((self.q > 0, self.q), (self.q < self.nq - 1, self.nq)):
            def run(slot=slot):
                two = self.two.at[slot]
                pltpu.make_async_remote_copy(
                    src_ref=two, dst_ref=two, send_sem=self.sends.at[self.n, o], recv_sem=self.recv_two.at[self.n, slot],
                    device_id=self.s.device(), device_id_type=MESH).wait_recv()
                out[...] += two[...].astype(jnp.float32)
            pl.when(cond)(run)


def reduce_kernel(sizes, chunks, gu_in, dn_in, gu_out, dn_out, gu_ref, dn_ref, g1, g2, d1a, d2a, d1b, d2b,
                  sends, r1, r2, local):
    spot = Spot(sizes)
    loads = [pltpu.make_async_copy(dn_in, dn_ref, local.at[0]), pltpu.make_async_copy(gu_in, gu_ref, local.at[1])]
    for l in loads:
        l.start()
    enter(spot, line_neighbours(spot))
    n_dp, rows_g, cols = gu_ref.shape
    _, rows_d, width = dn_ref.shape
    half = rows_d // 2
    wide = cols // chunks
    items, outs = [], []
    for p, xf in ((0, True), (1, False)):
        one, two = (d1a, d2a) if p == 0 else (d1b, d2b)
        items.append(Reduce(spot, p, lambda o, p=p: dn_ref.at[o, pl.ds(p * half, half)], one, two, sends, r1, r2, xf))
        outs.append(dn_out.at[pl.ds(p * half, half)])
    for c in range(chunks):
        cut = pl.ds(c * wide, wide)
        items.append(Reduce(spot, 2 + c, lambda o, c=c: gu_ref.at[o, :, pl.ds(c * wide, wide)],
                            g1.at[c], g2.at[c], sends, r1, r2, True))
        outs.append(gu_out.at[:, cut])
    for l in loads:
        l.wait()
    for item in items:
        for step in item.phase_one():
            step()
    lists = [item.phase_two() for item in items]
    for turn in range(2):
        for l in lists:
            for step in l[turn * len(l) // 2:(turn + 1) * len(l) // 2]:
                step()
    for item, out in zip(items, outs):
        item.finish(out)
    for item in items:
        for drain in item.drains:
            drain()


def reduce_experts(sizes, gu, dn, chunks=4):
    nz, nx = sizes[:2]
    n_dp = nz * nx
    big = max(nz, nx)
    gu = gu.reshape(n_dp, gu.shape[0] // n_dp, gu.shape[1])
    dn = dn.reshape(n_dp, dn.shape[0] // n_dp, dn.shape[1])
    items = 2 + chunks
    half = (dn.shape[1] // 2, dn.shape[2])
    wide = (gu.shape[1], gu.shape[2] // chunks)
    bf = gu.dtype
    return pl.pallas_call(
        functools.partial(reduce_kernel, sizes, chunks),
        out_shape=(jax.ShapeDtypeStruct(gu.shape[1:], jnp.float32), jax.ShapeDtypeStruct(dn.shape[1:], jnp.float32)),
        in_specs=[pl.BlockSpec(memory_space=pl.ANY)] * 2,
        out_specs=(pl.BlockSpec(memory_space=pltpu.VMEM),) * 2,
        scratch_shapes=[
            pltpu.VMEM(gu.shape, bf), pltpu.VMEM(dn.shape, bf),
            pltpu.VMEM((chunks, nx + 1, nz) + wide, bf), pltpu.VMEM((chunks, nz + 1) + wide, bf),
            pltpu.VMEM((nx + 1, nz) + half, bf), pltpu.VMEM((nz + 1,) + half, bf),
            pltpu.VMEM((nz + 1, nx) + half, bf), pltpu.VMEM((nx + 1,) + half, bf),
            pltpu.SemaphoreType.DMA((items, n_dp)), pltpu.SemaphoreType.DMA((items, big + 1, big)),
            pltpu.SemaphoreType.DMA((items, big + 1)), pltpu.SemaphoreType.DMA((2,))],
        compiler_params=pltpu.CompilerParams(collective_id=2, has_side_effects=True, vmem_limit_bytes=60 << 20),
    )(gu, dn)


def dense_kernel(sizes, cuts, *refs):
    n_in = len(cuts)
    ins, outs, rest = refs[:n_in], refs[n_in:2 * n_in], list(refs[2 * n_in:])
    spot = Spot(sizes)
    mate = spot.device(core=1 - spot.core)
    others = []
    for d in range(1, spot.ny):
        others.append((None, spot.device(y=lax.rem(spot.y + d, spot.ny))))
    enter(spot, line_neighbours(spot) + [(None, mate)] + others)
    sends, r1, r2, mate_sem, y_sem, out_sem, local = rest[-7:]
    pieces, drains = [], []
    number = 0
    for a in range(n_in):
        mine, one, two, ybuf, final = rest[5 * a:5 * a + 5]
        chunks = cuts[a]
        half = ins[a].shape[2] // 2
        wide = half // chunks
        for c in range(chunks):
            def cols(core, half=half, wide=wide, c=c):
                return pl.ds(pl.multiple_of(core * half + c * wide, 128), wide)
            pieces.append((number, a, c, wide, cols, mine, one, two, ybuf, final))
            number += 1
    reduces = []
    n_dp = spot.nz * spot.nx

    def to_mate(number, a, c, wide, cols, mine):
        return pltpu.make_async_remote_copy(
            src_ref=ins[a].at[:, :, cols(1 - spot.core)], dst_ref=mine.at[c], send_sem=mate_sem.at[0, number],
            recv_sem=mate_sem.at[1, number], device_id=mate, device_id_type=MESH)

    for number, a, c, wide, cols, mine, one, two, ybuf, final in pieces:
        to_mate(number, a, c, wide, cols, mine).start()
    for number, a, c, wide, cols, mine, one, two, ybuf, final in pieces:
        to_mate(number, a, c, wide, cols, mine).wait()
        own = ins[a]

        def add(o, carry, own=own, mine=mine, c=c, cols=cols):
            mine[c, o] = (mine[c, o].astype(jnp.float32) + own[o, :, cols(spot.core)].astype(jnp.float32)).astype(mine.dtype)
            return carry
        lax.fori_loop(0, n_dp, add, 0)
        r = Reduce(spot, number, lambda o, mine=mine, c=c: mine.at[c, o], one.at[c], two.at[c], sends, r1, r2, True)
        reduces.append(r)
        for step in r.phase_one():
            step()
    lists = [r.phase_two() for r in reduces]
    for turn in range(2):
        for l in lists:
            for step in l[turn * len(l) // 2:(turn + 1) * len(l) // 2]:
                step()
    for r, (number, a, c, wide, cols, mine, one, two, ybuf, final) in zip(reduces, pieces):
        r.finish(final.at[c])
        ybuf[c, spot.y] = final[c].astype(ybuf.dtype)
        for d in range(1, spot.ny):
            copy = pltpu.make_async_remote_copy(
                src_ref=ybuf.at[c, spot.y], dst_ref=ybuf.at[c, spot.y], send_sem=y_sem.at[0, number, d],
                recv_sem=y_sem.at[1, number, spot.y], device_id=spot.device(y=lax.rem(spot.y + d, spot.ny)),
                device_id_type=MESH)
            copy.start()
            drains.append(copy.wait_send)
    for number, a, c, wide, cols, mine, one, two, ybuf, final in pieces:
        for d in range(1, spot.ny):
            y = lax.rem(spot.y + d, spot.ny)
            pltpu.make_async_remote_copy(
                src_ref=ybuf.at[c, y], dst_ref=ybuf.at[c, y], send_sem=y_sem.at[0, number, d],
                recv_sem=y_sem.at[1, number, y], device_id=mate, device_id_type=MESH).wait_recv()
        total = ybuf[c, 0].astype(jnp.float32)
        for y in range(1, spot.ny):
            total = total + ybuf[c, y].astype(jnp.float32)
        final[c] = total
        outs[a][:, cols(spot.core)] = total
        copy = pltpu.make_async_remote_copy(
            src_ref=final.at[c], dst_ref=outs[a].at[:, cols(spot.core)], send_sem=out_sem.at[0, number],
            recv_sem=out_sem.at[1, number], device_id=mate, device_id_type=MESH)
        copy.start()
        drains.append(copy.wait_send)
    for number, a, c, wide, cols, mine, one, two, ybuf, final in pieces:
        pltpu.make_async_remote_copy(
            src_ref=final.at[c], dst_ref=outs[a].at[:, cols(1 - spot.core)], send_sem=out_sem.at[0, number],
            recv_sem=out_sem.at[1, number], device_id=mate, device_id_type=MESH).wait_recv()
    for r in reduces:
        drains += r.drains
    for drain in drains:
        drain()


def reduce_dense(sizes, arrays, cuts):
    nz, nx, ny = sizes[:3]
    n_dp = nz * nx
    big = max(nz, nx)
    arrays = [a.reshape(n_dp, a.shape[0] // n_dp, a.shape[1]) for a in arrays]
    items = sum(cuts)
    scratch = []
    for a, cut in zip(arrays, cuts):
        block = (a.shape[1], a.shape[2] // 2 // cut)
        scratch += [pltpu.VMEM((cut, n_dp) + block, a.dtype), pltpu.VMEM((cut, nx + 1, nz) + block, a.dtype),
                    pltpu.VMEM((cut, nz + 1) + block, a.dtype), pltpu.VMEM((cut, ny) + block, a.dtype),
                    pltpu.VMEM((cut,) + block, jnp.float32)]
    scratch += [pltpu.SemaphoreType.DMA((items, n_dp)), pltpu.SemaphoreType.DMA((items, big + 1, big)),
                pltpu.SemaphoreType.DMA((items, big + 1)), pltpu.SemaphoreType.DMA((2, items)),
                pltpu.SemaphoreType.DMA((2, items, ny)), pltpu.SemaphoreType.DMA((2, items)),
                pltpu.SemaphoreType.DMA((2,))]
    return pl.pallas_call(
        functools.partial(dense_kernel, sizes, tuple(cuts)),
        out_shape=tuple(jax.ShapeDtypeStruct(a.shape[1:], jnp.float32) for a in arrays),
        in_specs=[pl.BlockSpec(memory_space=pltpu.VMEM)] * len(arrays),
        out_specs=(pl.BlockSpec(memory_space=pltpu.VMEM),) * len(arrays),
        scratch_shapes=scratch,
        compiler_params=pltpu.CompilerParams(collective_id=3, has_side_effects=True, vmem_limit_bytes=60 << 20),
    )(*arrays)


epsilon = 1e-06
highest = lax.Precision.HIGHEST


def rope_tables(length, half):
    positions = jnp.arange(length).astype(jnp.float32)[:, None]
    inverse = 10000.0 ** (-(jnp.arange(half).astype(jnp.float32) / half))
    angles = positions * inverse[None, :]
    return (jnp.cos(angles)[:, None, :], jnp.sin(angles)[:, None, :])


def rotate(values, cosine, sine):
    half = values.shape[-1] // 2
    first = values[..., :half]
    second = values[..., half:]
    return jnp.concatenate(
        [first * cosine - second * sine, second * cosine + first * sine], axis=-1
    )


def rotate_back(grads, cosine, sine):
    half = grads.shape[-1] // 2
    first = grads[..., :half]
    second = grads[..., half:]
    return jnp.concatenate(
        [first * cosine + second * sine, second * cosine - first * sine], axis=-1
    )


def masked_scores(query_block, key_rows, block_start, segments, padding):
    block_rows = query_block.shape[0]
    scores = jnp.einsum("qhd,khd->hqk", query_block, key_rows, preferred_element_type=jnp.float32)
    row_index = block_start + jnp.arange(block_rows)
    col_index = jnp.arange(key_rows.shape[0])
    allowed = (
        (col_index[None, :] <= row_index[:, None])
        & (segments[:, None] == segments[None, :])
        & ((padding[None, :] == 1) | (col_index[None, :] == row_index[:, None]))
    )
    return jnp.where(allowed[None], scores, -1e30)


def norm_backward(values, inverse, gain, grad_normed):
    scaled = gain * grad_normed
    correction = jnp.sum(scaled * values, axis=-1, keepdims=True) / values.shape[-1]
    return (
        inverse * scaled - values * inverse * inverse * inverse * correction,
        jnp.sum(grad_normed * values * inverse, axis=0),
    )


def per_device(
    sizes,
    tokens,
    prev_logits,
    segment_ids,
    pad_mask,
    routes,
    slot_order,
    cotangent,
    attn_gain,
    qkv_weight,
    out_weight,
    ffn_gain,
    router_weight,
    mix_weight,
    const_weight,
    gate_up_weight,
    down_weight,
):
    length, width = tokens.shape
    owners = lax.axis_size("expert")
    real_count = owners * gate_up_weight.shape[0]
    capacity = 2 * length // (real_count + 4)
    hidden_units = gate_up_weight.shape[2] // 2
    heads = width // HEAD_DIM
    block_rows = min(length, 768)
    starts = jnp.arange(length // block_rows) * block_rows
    query_scale = HEAD_DIM ** (-0.5)
    rows = qkv_weight.shape[0]
    small = jnp.concatenate(
        [attn_gain[:, None], ffn_gain[:, None], mix_weight, const_weight, router_weight], axis=1
    )
    rest = jnp.concatenate([out_weight, jnp.pad(small, ((0, 0), (0, 256 - small.shape[1])))], axis=1)
    qkv_full, rest_full, gate_up_local, down_local = gather_weights(
        sizes, qkv_weight, rest, gate_up_weight[0], down_weight[0]
    )
    out_full = rest_full[:, :width]
    small_full = rest_full[:, width:]
    gain_one, gain_two = small_full[:, 0], small_full[:, 1]
    mix_full, const_full = small_full[:, 2:6], small_full[:, 6:8]
    router_full = small_full[:, 8 : 8 + router_weight.shape[1]]
    inputs = tokens.astype(jnp.float32)
    inverse_one = lax.rsqrt(jnp.mean(inputs * inputs, axis=-1, keepdims=True) + epsilon)
    normed = (inputs * inverse_one * gain_one.astype(jnp.float32)).astype(jnp.bfloat16)
    qkv = jnp.dot(normed, qkv_full, preferred_element_type=jnp.float32).reshape(
        length, 3, heads, HEAD_DIM
    )
    cosine, sine = rope_tables(length, HEAD_DIM // 2)
    queries = (rotate(qkv[:, 0], cosine, sine) * query_scale).astype(jnp.bfloat16)
    key_rows = rotate(qkv[:, 1], cosine, sine).astype(jnp.bfloat16)
    value_rows = qkv[:, 2].astype(jnp.bfloat16)
    segments = segment_ids[0]
    padding = pad_mask[0]

    def forward_block(block_start):
        scores = masked_scores(queries, key_rows, block_start, segments, padding)
        highest_score = jnp.max(scores, axis=-1, keepdims=True)
        exponent = jnp.exp(scores - highest_score)
        denominator = jnp.sum(exponent, axis=-1, keepdims=True)
        probabilities = (exponent / denominator).astype(jnp.bfloat16)
        attended_block = jnp.einsum(
            "hqk,khd->qhd", probabilities, value_rows, preferred_element_type=jnp.float32
        )
        return (attended_block.astype(jnp.bfloat16), (highest_score + jnp.log(denominator))[..., 0])

    attended_blocks, log_totals = lax.map(forward_block, starts)
    attended = attended_blocks.reshape(length, width)
    hidden_state = inputs + jnp.dot(attended, out_full, preferred_element_type=jnp.float32)
    inverse_two = lax.rsqrt(jnp.mean(hidden_state * hidden_state, axis=-1, keepdims=True) + epsilon)
    gain_float = gain_two.astype(jnp.float32)
    ffn_normed = (hidden_state * inverse_two * gain_float).astype(jnp.bfloat16)
    ffn_float = ffn_normed.astype(jnp.float32)
    logits = jnp.dot(
        ffn_normed, router_full, preferred_element_type=jnp.float32
    ) + prev_logits.astype(jnp.float32)
    route_rows = routes[0]
    route_ids = jnp.arange(real_count + 4)
    chosen = (route_rows[:, :, None] == route_ids[None, None, :]).astype(jnp.float32)
    picked = jnp.sum(chosen * logits[:, None, :], axis=-1)
    gate_weights = jax.nn.softmax(picked, axis=-1)
    mix = jax.nn.softmax(
        jnp.dot(ffn_normed, mix_full, preferred_element_type=jnp.float32).reshape(length, 2, 2),
        axis=-1,
    )
    is_copy = (route_rows == real_count + 1).astype(jnp.float32)
    const_ids = real_count + 2 + jnp.arange(2)
    is_const = (route_rows[:, :, None] == const_ids[None, None, :]).astype(jnp.float32)
    route_copy = is_copy + jnp.sum(is_const * mix[:, None, :, 0], axis=-1)
    copy_coef = jnp.sum(gate_weights * route_copy, axis=-1)
    const_select = jnp.sum(gate_weights[:, :, None] * is_const, axis=1)
    const_coef = const_select * mix[:, :, 1]
    pair_expert = route_rows.reshape(2 * length)
    order = slot_order[0]
    expert_range = jnp.arange(real_count)
    onehot = (pair_expert[:, None] == expert_range[None, :]).astype(jnp.int32)
    placed = jnp.zeros_like(onehot).at[order].set(onehot)
    before = jnp.cumsum(placed, axis=0) - placed
    slot_rank = jnp.sum(before[order] * onehot, axis=1)
    is_kept = (pair_expert < real_count) & (slot_rank < capacity)
    flat_slot = jnp.where(is_kept, pair_expert * capacity + slot_rank, real_count * capacity)
    pair_token = jnp.arange(2 * length) // 2
    slot_token = jnp.zeros(real_count * capacity + 1, jnp.int32).at[flat_slot].set(pair_token)[:-1]
    slot_valid = jnp.zeros(real_count * capacity + 1, jnp.int32).at[flat_slot].set(1)[:-1]
    send_rows = jnp.where(
        slot_valid[:, None] > 0, ffn_normed[slot_token], jnp.zeros((), jnp.bfloat16)
    ).reshape(real_count, capacity, width)
    received = lax.all_to_all(send_rows, "expert", split_axis=0, concat_axis=0, tiled=True)
    expert_input = received.reshape(-1, width)
    projected = jnp.dot(expert_input, gate_up_local, preferred_element_type=jnp.float32)
    gate_part = projected[:, :hidden_units]
    up_part = projected[:, hidden_units:]
    activated = (jax.nn.silu(gate_part) * up_part).astype(jnp.bfloat16)
    expert_out = (
        jnp.dot(activated, down_local, preferred_element_type=jnp.float32)
        .astype(jnp.bfloat16)
        .reshape(received.shape)
    )
    returned = lax.all_to_all(expert_out, "expert", split_axis=0, concat_axis=0, tiled=True)
    returned_rows = jnp.concatenate(
        [returned.reshape(-1, width), jnp.zeros((1, width), jnp.bfloat16)], axis=0
    )
    pair_rows = returned_rows[flat_slot].astype(jnp.float32).reshape(length, 2, width)
    const_float = const_full.astype(jnp.float32)
    branch_out = (
        jnp.sum(gate_weights[:, :, None] * pair_rows, axis=1)
        + copy_coef[:, None] * ffn_float
        + jnp.dot(const_coef, const_float.T, precision=highest)
    )
    layer_out = (hidden_state + branch_out).astype(jnp.bfloat16)
    qkv_back, out_back, router_back, mix_back = qkv_full, out_full, router_full, mix_full
    gate_up_back, down_back = gate_up_local, down_local
    out_grad = cotangent.astype(jnp.float32)
    pair_grad = (
        (gate_weights[:, :, None] * out_grad[:, None, :])
        .astype(jnp.bfloat16)
        .reshape(2 * length, width)
    )
    slot_grad = (
        jnp.zeros((real_count * capacity + 1, width), jnp.bfloat16)
        .at[flat_slot]
        .set(pair_grad)[:-1]
    )
    slot_grad = slot_grad.reshape(real_count, capacity, width)
    expert_out_grad = lax.all_to_all(
        slot_grad, "expert", split_axis=0, concat_axis=0, tiled=True
    ).reshape(-1, width)
    activated_grad = jnp.einsum(
        "rd,fd->rf", expert_out_grad, down_back, preferred_element_type=jnp.float32
    )
    sigmoid_gate = jax.nn.sigmoid(gate_part)
    gate_grad = activated_grad * up_part * sigmoid_gate * (1.0 + gate_part * (1.0 - sigmoid_gate))
    up_grad = activated_grad * gate_part * sigmoid_gate
    projected_grad = jnp.concatenate([gate_grad, up_grad], axis=1).astype(jnp.bfloat16)
    down_weight_grad = jnp.einsum(
        "rf,rd->fd", activated, expert_out_grad, preferred_element_type=jnp.float32
    )
    gate_up_weight_grad = jnp.einsum(
        "rd,rf->df", expert_input, projected_grad, preferred_element_type=jnp.float32
    )
    input_grad_rows = jnp.einsum(
        "rf,df->rd", projected_grad, gate_up_back, preferred_element_type=jnp.float32
    ).astype(jnp.bfloat16)
    back_rows = lax.all_to_all(
        input_grad_rows.reshape(received.shape), "expert", split_axis=0, concat_axis=0, tiled=True
    )
    back_padded = jnp.concatenate(
        [back_rows.reshape(-1, width), jnp.zeros((1, width), jnp.bfloat16)], axis=0
    )
    routed_grad = jnp.sum(
        back_padded[flat_slot].astype(jnp.float32).reshape(length, 2, width), axis=1
    )
    gate_up_shard, down_shard = reduce_experts(
        sizes, gate_up_weight_grad.astype(jnp.bfloat16), down_weight_grad.astype(jnp.bfloat16)
    )
    grad_dot_normed = jnp.sum(out_grad * ffn_float, axis=-1)
    grad_dot_const = jnp.dot(out_grad, const_float, precision=highest)
    grad_dot_pairs = jnp.sum(out_grad[:, None, :] * pair_rows, axis=-1)
    gate_grads = (
        grad_dot_pairs
        + route_copy * grad_dot_normed[:, None]
        + jnp.sum(is_const * (mix[:, None, :, 1] * grad_dot_const[:, None, :]), axis=-1)
    )
    picked_grad = gate_weights * (
        gate_grads - jnp.sum(gate_weights * gate_grads, axis=-1, keepdims=True)
    )
    prev_grad = jnp.sum(chosen * picked_grad[:, :, None], axis=1)
    logits_low = prev_grad.astype(jnp.bfloat16)
    router_weight_grad = jnp.einsum(
        "ld,lr->dr", ffn_normed, logits_low, preferred_element_type=jnp.float32
    )
    mix_grad = jnp.stack(
        [const_select * grad_dot_normed[:, None], const_select * grad_dot_const], axis=-1
    )
    mix_logit_grad = (
        (mix * (mix_grad - jnp.sum(mix * mix_grad, axis=-1, keepdims=True)))
        .reshape(length, 4)
        .astype(jnp.bfloat16)
    )
    mix_weight_grad = jnp.einsum(
        "ld,lm->dm", ffn_normed, mix_logit_grad, preferred_element_type=jnp.float32
    )
    const_weight_grad = jnp.einsum("ld,lj->dj", out_grad, const_coef, precision=highest)
    normed_two_grad = routed_grad + copy_coef[:, None] * out_grad
    normed_two_grad = normed_two_grad + jnp.einsum(
        "lr,dr->ld", logits_low, router_back, preferred_element_type=jnp.float32
    )
    normed_two_grad = normed_two_grad + jnp.einsum(
        "lm,dm->ld", mix_logit_grad, mix_back, preferred_element_type=jnp.float32
    )
    hidden_part, gain_two_grad = norm_backward(
        hidden_state, inverse_two, gain_float, normed_two_grad
    )
    hidden_grad = out_grad + hidden_part
    attn_grad = hidden_grad.astype(jnp.bfloat16)
    out_weight_grad = jnp.einsum(
        "ld,le->de", attended, attn_grad, preferred_element_type=jnp.float32
    )
    attended_grad = (
        jnp.einsum("le,de->ld", attn_grad, out_back, preferred_element_type=jnp.float32)
        .astype(jnp.bfloat16)
        .reshape(length, heads, HEAD_DIM)
    )

    def backward_block(carry, block_input):
        key_grad, value_grad = carry
        block_start, log_block = block_input
        scores = masked_scores(queries, key_rows, block_start, segments, padding)
        probs_full = jnp.exp(scores - log_block[..., None])
        probs_low = probs_full.astype(jnp.bfloat16)
        prob_grad = jnp.einsum(
            "qhd,khd->hqk", attended_grad, value_rows, preferred_element_type=jnp.float32
        )
        row_dot = jnp.sum(probs_full * prob_grad, axis=-1, keepdims=True)
        score_grad = (probs_full * (prob_grad - row_dot)).astype(jnp.bfloat16)
        query_grad = jnp.einsum(
            "hqk,khd->qhd", score_grad, key_rows, preferred_element_type=jnp.float32
        )
        key_grad = key_grad + jnp.einsum(
            "hqk,qhd->khd", score_grad, queries, preferred_element_type=jnp.float32
        )
        value_grad = value_grad + jnp.einsum(
            "hqk,qhd->khd", probs_low, attended_grad, preferred_element_type=jnp.float32
        )
        return ((key_grad, value_grad), query_grad)

    zero_heads = jnp.zeros((length, heads, HEAD_DIM), jnp.float32)
    (key_grad, value_grad), query_grads = lax.scan(
        backward_block, (zero_heads, zero_heads), (starts, log_totals)
    )
    query_grad = query_grads.reshape(length, heads, HEAD_DIM)
    qkv_grad = (
        jnp.stack(
            [
                rotate_back(query_grad * query_scale, cosine, sine),
                rotate_back(key_grad, cosine, sine),
                value_grad,
            ],
            axis=1,
        )
        .reshape(length, 3 * width)
        .astype(jnp.bfloat16)
    )
    qkv_weight_grad = jnp.einsum("ld,le->de", normed, qkv_grad, preferred_element_type=jnp.float32)
    normed_one_grad = jnp.einsum(
        "le,de->ld", qkv_grad, qkv_back, preferred_element_type=jnp.float32
    )
    input_part, gain_one_grad = norm_backward(
        inputs, inverse_one, gain_one.astype(jnp.float32), normed_one_grad
    )
    tokens_grad = hidden_grad + input_part
    small_grad = jnp.concatenate(
        [gain_one_grad[:, None], gain_two_grad[:, None], mix_weight_grad, const_weight_grad, router_weight_grad], axis=1
    )
    rest_grad = jnp.concatenate(
        [out_weight_grad, jnp.pad(small_grad, ((0, 0), (0, 256 - small_grad.shape[1])))], axis=1
    )
    qkv_shard, rest_shard = reduce_dense(
        sizes, [qkv_weight_grad.astype(jnp.bfloat16), rest_grad.astype(jnp.bfloat16)], [3, 1]
    )
    small_shard = rest_shard[:, width:]
    return (
        layer_out,
        tokens_grad,
        prev_grad,
        small_shard[:, 0],
        qkv_shard,
        rest_shard[:, :width],
        small_shard[:, 1],
        small_shard[:, 8 : 8 + router_weight.shape[1]],
        small_shard[:, 2:6],
        small_shard[:, 6:8],
        gate_up_shard[None],
        down_shard[None],
    )


def grid_sizes(mesh):
    along_dp, along_expert = mesh.devices[:, 0], mesh.devices[0]
    nx = len({d.coords[0] for d in along_dp})
    ny = len({d.coords[1] for d in along_expert})
    return (len(along_dp) // nx, nx, ny, len(along_expert) // ny)


def solution(mesh):
    in_specs = (
        P(("dp", "expert"), None),
        P(("dp", "expert"), None),
        P(("dp", "expert"), None),
        P(("dp", "expert"), None),
        P(("dp", "expert"), None, None),
        P(("dp", "expert"), None),
        P(("dp", "expert"), None),
        P("dp"),
        P("dp", None),
        P("dp", None),
        P("dp"),
        P("dp", None),
        P("dp", None),
        P("dp", None),
        P("expert", "dp", None),
        P("expert", "dp", None),
    )
    out_specs = (
        P(("dp", "expert"), None),
        P(("dp", "expert"), None),
        P(("dp", "expert"), None),
        P("dp"),
        P("dp", None),
        P("dp", None),
        P("dp"),
        P("dp", None),
        P("dp", None),
        P("dp", None),
        P("expert", "dp", None),
        P("expert", "dp", None),
    )
    return jax.shard_map(
        functools.partial(per_device, grid_sizes(mesh)), mesh=mesh, in_specs=in_specs, out_specs=out_specs, check_vma=False
    )
```

```python
import functools
import jax
import jax.numpy as jnp
from jax import lax
from jax.experimental import pallas as pl
from jax.experimental.pallas import tpu as pltpu
import numpy as np
from jax.sharding import PartitionSpec as P

HEAD_DIM = 64
BLOCK = 256
LONGEST = 384
epsilon = 1e-06


MESH = pl.DeviceIdType.MESH


class Spot:
    def __init__(self, sizes):
        self.nz, self.nx, self.ny, self.nc = sizes
        self.dp, self.ex = lax.axis_index("dp"), lax.axis_index("expert")
        self.z, self.x = lax.div(self.dp, self.nx), lax.rem(self.dp, self.nx)
        self.y, self.core = lax.div(self.ex, self.nc), lax.rem(self.ex, self.nc)

    def device(self, z=None, x=None, y=None, core=None):
        z, x = self.z if z is None else z, self.x if x is None else x
        y, core = self.y if y is None else y, self.core if core is None else core
        return {"dp": z * self.nx + x, "expert": y * self.nc + core}


def between(value, size):
    return jnp.logical_and(value >= 0, value < size)


class Flood:
    def __init__(self, spot, number, own, view, sends, recvs, z_first, mate=None):
        self.s, self.n, self.own, self.view = spot, number, own, view
        self.sends, self.recvs, self.z_first, self.mate = sends, recvs, z_first, mate
        if z_first:
            self.na, self.nb, self.a, self.b = spot.nz, spot.nx, spot.z, spot.x
        else:
            self.na, self.nb, self.a, self.b = spot.nx, spot.nz, spot.x, spot.z
        self.drains = []

    def origin(self, a, b):
        return a * self.s.nx + b if self.z_first else b * self.s.nx + a

    def along(self, which, value):
        zed = (which == 0) == self.z_first
        return self.s.device(z=value) if zed else self.s.device(x=value)

    def push(self, cond, src, o, way, device, recvs=None):
        copy = pltpu.make_async_remote_copy(
            src_ref=src, dst_ref=self.view(o),
            send_sem=self.sends.at[way, self.n, o],
            recv_sem=(self.recvs if recvs is None else recvs).at[self.n, o],
            device_id=device, device_id_type=MESH)
        if cond is None:
            copy.start()
            self.drains.append(copy.wait_send)
        else:
            pl.when(cond)(lambda: copy.start())
            self.drains.append(lambda: pl.when(cond)(lambda: copy.wait_send()))

    def share(self, cond, src, o):
        if self.mate is not None:
            self.push(cond, src, o, 4, self.s.device(core=1 - self.s.core), self.mate)

    def mates(self, view):
        def one(o, carry):
            pltpu.make_async_remote_copy(
                src_ref=view(o), dst_ref=view(o), send_sem=self.sends.at[0, self.n, o], recv_sem=self.mate.at[self.n, o],
                device_id=self.s.device(), device_id_type=MESH).wait_recv()
            return carry
        lax.fori_loop(0, self.s.nz * self.s.nx, one, 0)

    def arrive(self, o):
        pltpu.make_async_remote_copy(
            src_ref=self.view(o), dst_ref=self.view(o),
            send_sem=self.sends.at[0, self.n, o], recv_sem=self.recvs.at[self.n, o],
            device_id=self.s.device(), device_id_type=MESH).wait_recv()

    def second(self, cond, src, o):
        for j, sign in enumerate((1, -1)):
            to = self.b + sign
            if self.nb > 1:
                ok = between(to, self.nb)
                self.push(ok if cond is None else jnp.logical_and(cond, ok), src, o, 2 + j, self.along(1, to))

    def levels(self):
        out = [[] for _ in range(self.na + self.nb - 1)]

        def begin():
            o = self.origin(self.a, self.b)
            for j, sign in enumerate((1, -1)):
                if self.na > 1:
                    self.push(between(self.a + sign, self.na), self.own, o, j, self.along(0, self.a + sign))
            self.second(None, self.own, o)
            self.share(None, self.own, o)

        out[0].append(begin)
        for k in range(1, self.na):
            for j, sign in enumerate((1, -1)):
                def step(k=k, j=j, sign=sign):
                    a = self.a - sign * k
                    here = between(a, self.na)
                    o = self.origin(a, self.b)
                    pl.when(here)(lambda: self.arrive(o))
                    on = jnp.logical_and(here, between(self.a + sign, self.na))
                    if self.na > 2 or k == 0:
                        self.push(on, self.view(o), o, j, self.along(0, self.a + sign))
                    self.second(here, self.view(o), o)
                    self.share(here, self.view(o), o)
                out[k].append(step)
        for d in range(1, self.nb):
            for da in range(-(self.na - 1), self.na):
                for j, sign in enumerate((1, -1)):
                    def step(d=d, da=da, j=j, sign=sign):
                        a, b = self.a + da, self.b - sign * d
                        here = jnp.logical_and(between(a, self.na), between(b, self.nb))
                        o = self.origin(a, b)
                        pl.when(here)(lambda: self.arrive(o))
                        if self.nb > 2:
                            on = jnp.logical_and(here, between(self.b + sign, self.nb))
                            self.push(on, self.view(o), o, 2 + j, self.along(1, self.b + sign))
                        self.share(here, self.view(o), o)
                    out[abs(da) + d].append(step)
        return out


def enter(spot, devices):
    barrier = pltpu.get_barrier_semaphore()
    count = jnp.int32(0)
    for cond, device in devices:
        def hail(device=device):
            pl.semaphore_signal(barrier, inc=1, device_id=device, device_id_type=MESH)
        if cond is None:
            hail()
            count = count + 1
        else:
            pl.when(cond)(hail)
            count = count + cond.astype(jnp.int32)
    pl.semaphore_wait(barrier, count)


def line_neighbours(spot):
    out = []
    for sign in (1, -1):
        out.append((between(spot.z + sign, spot.nz), spot.device(z=spot.z + sign)))
        out.append((between(spot.x + sign, spot.nx), spot.device(x=spot.x + sign)))
    return out


def dot(a, b, ca=1, cb=0):
    return lax.dot_general(a, b, (((ca,), (cb,)), ((), ())), preferred_element_type=jnp.float32)


def turned(columns):
    eye = lax.broadcasted_iota(jnp.int32, (128, 128), 0) == lax.broadcasted_iota(jnp.int32, (128, 128), 1)
    return dot(jnp.where(eye, 1.0, 0.0).astype(jnp.bfloat16), columns, 1, 1)


def spread(columns):
    lane = lax.broadcasted_iota(jnp.int32, (columns[0].shape[0], 128), 1)
    out = jnp.zeros(lane.shape, jnp.float32)
    for j, c in enumerate(columns):
        out = jnp.where(lane == j, c, out)
    return out


def swap_halves(v):
    half = HEAD_DIM // 2
    lane = lax.broadcasted_iota(jnp.int32, v.shape, 1)
    return jnp.where(lax.rem(lane, HEAD_DIM) < half, pltpu.roll(v, v.shape[1] - half, 1), pltpu.roll(v, half, 1))


def head_masks():
    lane = lax.broadcasted_iota(jnp.int32, (1, 128), 1)
    low = jnp.where(lane < HEAD_DIM, 1.0, 0.0).astype(jnp.bfloat16)
    high = jnp.where(lane < HEAD_DIM, 0.0, 1.0).astype(jnp.bfloat16)
    return low, high


def key_range(i):
    return max(0, i * BLOCK - LONGEST), (i + 1) * BLOCK


class Front:
    def __init__(self, spot, experts, r):
        self.spot, self.experts, self.r = spot, experts, r
        self.length, self.width = r["tokens"].shape
        self.capacity = 2 * self.length // (experts + 4)
        self.blocks = self.length // BLOCK

    def ranks(self):
        r, n = self.r, self.length
        order = [r["order"][:, k : k + 1] for k in range(2)]
        route = [r["routes"][:, k : k + 1] for k in range(2)]
        parts = []
        for k in range(2):
            parts += [lax.div(order[k], 256).astype(jnp.float32), lax.rem(order[k], 256).astype(jnp.float32)]
        parts += [route[k].astype(jnp.float32) for k in range(2)]
        side = turned(spread(parts).astype(jnp.bfloat16))
        order_row = [side[2 * k : 2 * k + 1] * 256.0 + side[2 * k + 1 : 2 * k + 2] for k in range(2)]
        route_row = [side[4 + k : 5 + k] for k in range(2)]
        out = []
        for k in range(2):
            for i in range(self.blocks):
                rows = slice(i * BLOCK, (i + 1) * BLOCK)
                mine, kind = order[k][rows].astype(jnp.float32), route[k][rows].astype(jnp.float32)
                ahead = jnp.zeros((BLOCK, n), jnp.float32)
                for other in range(2):
                    ahead += jnp.where(
                        jnp.logical_and(order_row[other] < mine, route_row[other] == kind), 1.0, 0.0)
                rank = jnp.sum(ahead, axis=1, keepdims=True)
                kept = jnp.logical_and(kind < self.experts, rank < self.capacity)
                r["scal"][pl.ds(i * BLOCK, BLOCK), 8 + k : 9 + k] = jnp.where(
                    kept, kind * self.capacity + rank, float(self.experts * self.capacity))
                r["scal"][pl.ds(i * BLOCK, BLOCK), 10 + k : 11 + k] = jnp.where(kept, kind, 255.0)
                r["scal"][pl.ds(i * BLOCK, BLOCK), 12 + k : 13 + k] = jnp.where(kept, rank, 0.0)

    def flat_rows(self):
        r = self.r
        side = turned(r["scal"][...].astype(jnp.bfloat16))
        for k in range(2):
            kind, rank = side[10 + k : 11 + k], side[12 + k : 13 + k]
            r["flat"][k : k + 1] = jnp.where(
                kind < 255.0, kind * self.capacity + rank, float(self.experts * self.capacity))

    def first_norm(self):
        r = self.r
        for i in range(self.blocks):
            rows = pl.ds(i * BLOCK, BLOCK)
            x = r["tokens"][rows].astype(jnp.float32)
            r["scal"][rows, 0:1] = lax.rsqrt(jnp.mean(x * x, axis=1, keepdims=True) + epsilon)

    def masks(self):
        r, n = self.r, self.length
        segment = r["segments"][...].astype(jnp.float32)
        padding = r["padding"][...]
        column = jnp.transpose(jnp.broadcast_to(segment, (128, n)))[:, 0:1]
        for i in range(self.blocks):
            k0, k1 = key_range(i)
            row = lax.broadcasted_iota(jnp.int32, (BLOCK, k1 - k0), 0) + i * BLOCK
            col = lax.broadcasted_iota(jnp.int32, (BLOCK, k1 - k0), 1) + k0
            same = column[i * BLOCK : (i + 1) * BLOCK] == segment[:, k0:k1]
            real = jnp.broadcast_to(padding[:, k0:k1], row.shape) == 1
            fine = jnp.logical_and(jnp.logical_and(col <= row, same), jnp.logical_or(real, col == row))
            r["bias"][pl.ds(i * BLOCK, BLOCK), pl.ds(0, k1 - k0)] = jnp.where(fine, 0.0, -1e30)

    def small_rows(self):
        r = self.r
        side = turned(r["rest"][:, pl.ds(self.width, 128)])
        r["rows"][...] = side[: r["rows"].shape[0]]

    def project(self, i):
        r, w = self.r, self.width
        rows = pl.ds(i * BLOCK, BLOCK)
        x = r["tokens"][rows].astype(jnp.float32)
        normed = (x * r["scal"][rows, 0:1] * r["rows"][0:1]).astype(jnp.bfloat16)
        r["normed"][rows] = normed
        cosine, sine = r["cosine"][rows], r["sine"][rows]
        for part, name in enumerate(("q", "k")):
            full = dot(normed, r["qkv"][:, pl.ds(part * w, w)])
            for pair in range(w // 128):
                v = full[:, pair * 128 : pair * 128 + 128]
                v = v * cosine + swap_halves(v) * sine
                if part == 0:
                    v = v * HEAD_DIM ** (-0.5)
                r[name][rows, pl.ds(pair * 128, 128)] = v.astype(jnp.bfloat16)
        r["v"][rows] = dot(normed, r["qkv"][:, pl.ds(2 * w, w)]).astype(jnp.bfloat16)

    def attend(self, i, pair):
        r = self.r
        k0, k1 = key_range(i)
        rows, keys, lanes = pl.ds(i * BLOCK, BLOCK), pl.ds(k0, k1 - k0), pl.ds(pair * 128, 128)
        q, k, v = r["q"][rows, lanes], r["k"][keys, lanes], r["v"][keys, lanes]
        bias = r["bias"][rows, pl.ds(0, k1 - k0)]
        out = jnp.zeros((BLOCK, 128), jnp.float32)
        for s, mask in enumerate(head_masks()):
            scores = dot(q * mask, k, 1, 1) + bias
            top = jnp.max(scores, axis=1, keepdims=True)
            e = jnp.exp(scores - top)
            total = jnp.sum(e, axis=1, keepdims=True)
            probs = (e * (1.0 / total)).astype(jnp.bfloat16)
            out = out + dot(probs, v * mask)
            r["lse"][rows, 2 * pair + s : 2 * pair + s + 1] = top + jnp.log(total)
        r["attended"][rows, lanes] = out.astype(jnp.bfloat16)

    def gate(self, i):
        r, w, e = self.r, self.width, self.experts
        rows = pl.ds(i * BLOCK, BLOCK)
        h = r["tokens"][rows].astype(jnp.float32) + dot(r["attended"][rows], r["rest"][:, pl.ds(0, w)])
        r["h"][rows] = h
        inverse = lax.rsqrt(jnp.mean(h * h, axis=1, keepdims=True) + epsilon)
        hn = (h * inverse * r["rows"][1:2]).astype(jnp.bfloat16)
        r["hn"][rows] = hn
        small = dot(hn, r["rest"][:, pl.ds(w, 128)])
        lane = lax.broadcasted_iota(jnp.int32, small.shape, 1)
        prev = r["prev"][rows].astype(jnp.float32)
        prev_lane = lax.broadcasted_iota(jnp.int32, prev.shape, 1)
        picked = []
        for k in range(2):
            route = r["routes"][rows, k : k + 1]
            picked.append(jnp.sum(jnp.where(lane == route + 8, small, 0.0), axis=1, keepdims=True)
                          + jnp.sum(jnp.where(prev_lane == route, prev, 0.0), axis=1, keepdims=True))
        def soft(a, b):
            top = jnp.maximum(a, b)
            ea, eb = jnp.exp(a - top), jnp.exp(b - top)
            return ea / (ea + eb), eb / (ea + eb)
        gates = soft(*picked)
        mix = soft(small[:, 2:3], small[:, 3:4]) + soft(small[:, 4:5], small[:, 5:6])
        r["scal"][rows, 1:2] = inverse
        for j, c in enumerate(gates + mix):
            r["scal"][rows, 2 + j : 3 + j] = c
        cot = r["cot"][rows].astype(jnp.float32)
        for k in range(2):
            r["gcot"][k, rows] = (gates[k] * cot).astype(jnp.bfloat16)

    def slots(self, d):
        r, n = self.r, self.length
        e = lax.rem(self.spot.ex + d, self.experts)
        slot = (lax.broadcasted_iota(jnp.int32, (self.capacity, n), 0) + e * self.capacity).astype(jnp.float32)
        at = [jnp.where(r["flat"][k : k + 1] == slot, 1.0, 0.0) for k in range(2)]
        x = dot((at[0] + at[1]).astype(jnp.bfloat16), r["hn"][...]).astype(jnp.bfloat16)
        g = (dot(at[0].astype(jnp.bfloat16), r["gcot"][0]) + dot(at[1].astype(jnp.bfloat16), r["gcot"][1]))
        g = g.astype(jnp.bfloat16)
        if d == 0:
            r["xin"][self.spot.ex], r["gin"][self.spot.ex] = x, g
        else:
            r["sendx"][d - 1], r["sendg"][d - 1] = x, g


def expert_device(spot, e):
    return {"dp": spot.dp, "expert": e}


class Exchange:
    def __init__(self, spot, experts, number, out, into, sems):
        self.spot, self.experts, self.n, self.out, self.into, self.sems = spot, experts, number, out, into, sems

    def send(self, d):
        e = lax.rem(self.spot.ex + d, self.experts)
        pltpu.make_async_remote_copy(
            src_ref=self.out(d), dst_ref=self.into.at[self.spot.ex], send_sem=self.sems.at[0, self.n, d],
            recv_sem=self.sems.at[1, self.n, self.spot.ex], device_id=expert_device(self.spot, e),
            device_id_type=MESH).start()

    def receive(self, d):
        e = lax.rem(self.spot.ex + d, self.experts)
        pltpu.make_async_remote_copy(
            src_ref=self.into.at[e], dst_ref=self.into.at[e], send_sem=self.sems.at[0, self.n, d],
            recv_sem=self.sems.at[1, self.n, e], device_id=expert_device(self.spot, e),
            device_id_type=MESH).wait_recv()

    def drain(self, d):
        pltpu.make_async_remote_copy(
            src_ref=self.out(d), dst_ref=self.into.at[self.spot.ex], send_sem=self.sems.at[0, self.n, d],
            recv_sem=self.sems.at[1, self.n, self.spot.ex], device_id=expert_device(self.spot, self.spot.ex),
            device_id_type=MESH).wait_send()


def woven(work, events):
    done = 0
    for j, piece in enumerate(work):
        piece()
        upto = (j + 1) * len(events) // len(work)
        for event in events[done:upto]:
            event()
        done = upto


FRONT_INS = ("tokens", "prev", "segments", "padding", "routes", "order", "cot", "cosine", "sine",
             "qkv_own", "rest_own", "gu_own", "dn_own")
FRONT_OUTS = ("gu", "dn", "qkv", "rest", "q", "k", "v", "normed", "attended", "hn", "h", "lse", "scal", "rows", "flat",
              "xin", "gin")
FRONT_SCRATCH = ("bias", "gcot", "sendx", "sendg", "sends", "recvs", "mates", "local", "trade")


def front_kernel(sizes, experts, chunks, *refs):
    r = dict(zip(FRONT_INS + FRONT_OUTS + FRONT_SCRATCH, refs))
    spot = Spot(sizes)
    front = Front(spot, experts, r)
    enter(spot, line_neighbours(spot)
          + [(None, expert_device(spot, lax.rem(spot.ex + d, experts))) for d in range(1, experts)])
    rows = r["qkv_own"].shape[0]
    rows_d = r["dn_own"].shape[0]
    first, later = [], []
    for name in ("qkv", "rest"):
        src, out = r[name + "_own"], r[name]
        part = src.shape[1] // 2
        def half(o, core, out=out, part=part):
            return out.at[pl.ds(pl.multiple_of(o * rows, 8), rows), pl.ds(pl.multiple_of(core * part, 128), part)]
        first.append((src.at[:, pl.ds(pl.multiple_of(spot.core * part, 128), part)],
                      lambda o, half=half: half(o, spot.core), True, lambda o, half=half: half(o, 1 - spot.core)))
    part = rows_d // 2
    for p, zf in ((0, True), (1, False)):
        later.append((r["dn_own"].at[pl.ds(p * part, part)],
                      lambda o, p=p: r["dn"].at[pl.ds(pl.multiple_of(o * rows_d + p * part, 8), part)], zf, None))
    wide = r["gu_own"].shape[1] // chunks
    for c in range(chunks):
        later.append((r["gu_own"].at[:, pl.ds(c * wide, wide)],
                      lambda o, c=c: r["gu"].at[pl.ds(pl.multiple_of(o * rows, 8), rows), pl.ds(c * wide, wide)], True, None))
    floods = [Flood(spot, n, own, view, r["sends"], r["recvs"], zf, None if other is None else r["mates"])
              for n, (own, view, zf, other) in enumerate(first + later)]
    levels = [f.levels() for f in floods]
    dense, experts_levels = levels[:2], levels[2:]
    keeps = [pltpu.make_async_copy(own, view(spot.dp), r["local"].at[n])
             for n, (own, view, zf, other) in enumerate(first + later)]
    for ls in dense:
        for step in ls[0]:
            step()
    for keep in keeps:
        keep.start()
    front.ranks()
    front.flat_rows()
    front.first_norm()
    front.masks()
    depth = max(map(len, levels))
    events = [step for level in range(depth) for ls in experts_levels if level < len(ls) for step in ls[level]]
    n_start = sum(len(ls[0]) for ls in experts_levels)
    for level in range(1, depth):
        if level == depth - 1:
            for event in events[:n_start]:
                event()
        for ls in dense:
            if level < len(ls):
                for step in ls[level]:
                    step()
    for keep in keeps[:2]:
        keep.wait()
    for f, (own, view, zf, other) in zip(floods, first):
        f.mates(other)
    trades = [Exchange(spot, experts, 0, lambda d: r["sendx"].at[d - 1], r["xin"], r["trade"]),
              Exchange(spot, experts, 1, lambda d: r["sendg"].at[d - 1], r["gin"], r["trade"])]
    work = [front.small_rows]
    work += [functools.partial(front.project, i) for i in range(front.blocks)]
    for pair in range(front.width // 128):
        work += [functools.partial(front.attend, i, pair) for i in range(front.blocks)]
    work += [functools.partial(front.gate, i) for i in range(front.blocks)]
    def dispatch(d):
        front.slots(d)
        if d:
            for t in trades:
                t.send(d)
    work += [functools.partial(dispatch, d) for d in list(range(1, experts)) + [0]]
    rest = events[n_start:]
    cut = len(rest) * 3 // 5
    woven(work, rest[:cut])
    for event in rest[cut:]:
        event()
    for d in range(1, experts):
        for t in trades:
            t.receive(d)
            t.drain(d)
    for f in floods:
        for drain in f.drains:
            drain()
    for keep in keeps[2:]:
        keep.wait()


def run_front(sizes, experts, ins, chunks=4):
    tokens, qkv, rest, gu, dn = ins[0], ins[9], ins[10], ins[11], ins[12]
    length, width = tokens.shape
    n_dp = sizes[0] * sizes[1]
    capacity = 2 * length // (experts + 4)
    bf, f4 = jnp.bfloat16, jnp.float32
    S = jax.ShapeDtypeStruct
    token = S((length, width), bf)
    outs = [S((a.shape[0] * n_dp, a.shape[1]), bf) for a in (gu, dn, qkv, rest)]
    outs += [token] * 6 + [S((length, width), f4), S((length, 128), f4), S((length, 128), f4), S((16, width), f4),
                           S((8, length), f4)]
    outs += [S((experts, capacity, width), bf)] * 2
    items = 4 + chunks
    dma = pltpu.SemaphoreType.DMA
    vmem = pl.BlockSpec(memory_space=pltpu.VMEM)
    hbm = pl.BlockSpec(memory_space=pl.ANY)
    return pl.pallas_call(
        functools.partial(front_kernel, sizes, experts, chunks),
        out_shape=tuple(outs),
        in_specs=[vmem] * 13,
        out_specs=(hbm, hbm) + (vmem,) * (len(outs) - 2),
        scratch_shapes=[
            pltpu.VMEM((length, BLOCK + LONGEST), f4), pltpu.VMEM((2, length, width), bf),
            pltpu.VMEM((experts - 1, capacity, width), bf), pltpu.VMEM((experts - 1, capacity, width), bf),
            dma((5, items, n_dp)), dma((items, n_dp)), dma((2, n_dp)), dma((items,)), dma((2, 2, experts))],
        compiler_params=pltpu.CompilerParams(collective_id=1, has_side_effects=True, vmem_limit_bytes=62 << 20),
        name="front",
    )(*ins)


def add_into(view, more):
    view[...] = (view[...].astype(jnp.float32) + more[...].astype(jnp.float32)).astype(view.dtype)


class Reduce:
    def __init__(self, spot, number, view, one, two, sends, recv_one, recv_two, x_first):
        self.s, self.n, self.view, self.one, self.two = spot, number, view, one, two
        self.sends, self.recv_one, self.recv_two, self.x_first = sends, recv_one, recv_two, x_first
        if x_first:
            self.np, self.nq, self.p, self.q = spot.nx, spot.nz, spot.x, spot.z
        else:
            self.np, self.nq, self.p, self.q = spot.nz, spot.nx, spot.z, spot.x
        self.drains = []

    def owner(self, p, q):
        return q * self.s.nx + p if self.x_first else p * self.s.nx + q

    def along(self, first, value):
        return self.s.device(x=value) if first == self.x_first else self.s.device(z=value)

    def push(self, cond, o, dst, recv, device):
        copy = pltpu.make_async_remote_copy(
            src_ref=self.view(o), dst_ref=dst, send_sem=self.sends.at[self.n, o], recv_sem=recv,
            device_id=device, device_id_type=MESH)
        pl.when(cond)(lambda: copy.start())
        self.drains.append(lambda: pl.when(cond)(lambda: copy.wait_send()))

    def take(self, cond, o, slot, recv):
        def run():
            pltpu.make_async_remote_copy(
                src_ref=slot, dst_ref=slot, send_sem=self.sends.at[self.n, o], recv_sem=recv,
                device_id=self.s.device(), device_id_type=MESH).wait_recv()
            add_into(self.view(o), slot)
        pl.when(cond)(run)

    def order(self):
        return sorted(range(-(self.nq - 1), self.nq), key=lambda d: (-abs(d), d))

    def phase_one(self):
        steps = []
        for turn in range(2):
            sign = jnp.where(self.p * 2 < self.np, 1, -1) * (1 if turn == 0 else -1)
            for k in range(self.np - 1, 0, -1):
                for dq in self.order():
                    def step(sign=sign, k=k, dq=dq):
                        p, q = self.p + sign * k, self.q + dq
                        here = jnp.logical_and(between(p, self.np), between(q, self.nq))
                        o = self.owner(p, q)
                        if self.np > 2:
                            behind = jnp.logical_and(here, between(self.p - sign, self.np))
                            self.take(behind, o, self.one.at[p, q], self.recv_one.at[self.n, p, q])
                        last = jnp.logical_and(k == 1, sign < 0)
                        slot = jnp.where(last, self.np, p)
                        self.push(here, o, self.one.at[slot, q], self.recv_one.at[self.n, slot, q],
                                  self.along(True, self.p + sign))
                    steps.append(step)
        return steps

    def settle(self, cond, q):
        o = self.owner(self.p, q)
        below = self.p > 0
        above = self.p < self.np - 1
        if cond is not None:
            below, above = jnp.logical_and(cond, below), jnp.logical_and(cond, above)
        self.take(below, o, self.one.at[self.p, q], self.recv_one.at[self.n, self.p, q])
        self.take(above, o, self.one.at[self.np, q], self.recv_one.at[self.n, self.np, q])

    def phase_two(self):
        steps = []
        for turn in range(2):
            sign = jnp.where(self.q * 2 < self.nq, 1, -1) * (1 if turn == 0 else -1)
            for k in range(self.nq - 1, 0, -1):
                def step(sign=sign, k=k):
                    q = self.q + sign * k
                    here = between(q, self.nq)
                    o = self.owner(self.p, q)
                    self.settle(here, q)
                    behind = jnp.logical_and(here, between(self.q - sign, self.nq))
                    self.take(behind, o, self.two.at[q], self.recv_two.at[self.n, q])
                    last = jnp.logical_and(k == 1, sign < 0)
                    slot = jnp.where(last, self.nq, q)
                    self.push(here, o, self.two.at[slot], self.recv_two.at[self.n, slot], self.along(False, self.q + sign))
                steps.append(step)
        return steps

    def finish(self, out):
        o = self.owner(self.p, self.q)
        self.settle(None, self.q)
        out[...] = self.view(o)[...].astype(jnp.float32)
        for cond, slot in ((self.q > 0, self.q), (self.q < self.nq - 1, self.nq)):
            def run(slot=slot):
                two = self.two.at[slot]
                pltpu.make_async_remote_copy(
                    src_ref=two, dst_ref=two, send_sem=self.sends.at[self.n, o], recv_sem=self.recv_two.at[self.n, slot],
                    device_id=self.s.device(), device_id_type=MESH).wait_recv()
                out[...] += two[...].astype(jnp.float32)
            pl.when(cond)(run)


def reduce_kernel(sizes, chunks, gu_in, dn_in, gu_out, dn_out, gu_ref, dn_ref, g1, g2, d1a, d2a, d1b, d2b,
                  sends, r1, r2, local):
    spot = Spot(sizes)
    loads = [pltpu.make_async_copy(dn_in, dn_ref, local.at[0]), pltpu.make_async_copy(gu_in, gu_ref, local.at[1])]
    for l in loads:
        l.start()
    enter(spot, line_neighbours(spot))
    n_dp, rows_g, cols = gu_ref.shape
    _, rows_d, width = dn_ref.shape
    half = rows_d // 2
    wide = cols // chunks
    items, outs = [], []
    for p, xf in ((0, True), (1, False)):
        one, two = (d1a, d2a) if p == 0 else (d1b, d2b)
        items.append(Reduce(spot, p, lambda o, p=p: dn_ref.at[o, pl.ds(p * half, half)], one, two, sends, r1, r2, xf))
        outs.append(dn_out.at[pl.ds(p * half, half)])
    for c in range(chunks):
        cut = pl.ds(c * wide, wide)
        items.append(Reduce(spot, 2 + c, lambda o, c=c: gu_ref.at[o, :, pl.ds(c * wide, wide)],
                            g1.at[c], g2.at[c], sends, r1, r2, True))
        outs.append(gu_out.at[:, cut])
    for l in loads:
        l.wait()
    for item in items:
        for step in item.phase_one():
            step()
    lists = [item.phase_two() for item in items]
    for turn in range(2):
        for l in lists:
            for step in l[turn * len(l) // 2:(turn + 1) * len(l) // 2]:
                step()
    for item, out in zip(items, outs):
        item.finish(out)
    for item in items:
        for drain in item.drains:
            drain()


def reduce_experts(sizes, gu, dn, chunks=4):
    nz, nx = sizes[:2]
    n_dp = nz * nx
    big = max(nz, nx)
    gu = gu.reshape(n_dp, gu.shape[0] // n_dp, gu.shape[1])
    dn = dn.reshape(n_dp, dn.shape[0] // n_dp, dn.shape[1])
    items = 2 + chunks
    half = (dn.shape[1] // 2, dn.shape[2])
    wide = (gu.shape[1], gu.shape[2] // chunks)
    bf = gu.dtype
    return pl.pallas_call(
        functools.partial(reduce_kernel, sizes, chunks),
        out_shape=(jax.ShapeDtypeStruct(gu.shape[1:], jnp.float32), jax.ShapeDtypeStruct(dn.shape[1:], jnp.float32)),
        in_specs=[pl.BlockSpec(memory_space=pl.ANY)] * 2,
        out_specs=(pl.BlockSpec(memory_space=pltpu.VMEM),) * 2,
        scratch_shapes=[
            pltpu.VMEM(gu.shape, bf), pltpu.VMEM(dn.shape, bf),
            pltpu.VMEM((chunks, nx + 1, nz) + wide, bf), pltpu.VMEM((chunks, nz + 1) + wide, bf),
            pltpu.VMEM((nx + 1, nz) + half, bf), pltpu.VMEM((nz + 1,) + half, bf),
            pltpu.VMEM((nz + 1, nx) + half, bf), pltpu.VMEM((nx + 1,) + half, bf),
            pltpu.SemaphoreType.DMA((items, n_dp)), pltpu.SemaphoreType.DMA((items, big + 1, big)),
            pltpu.SemaphoreType.DMA((items, big + 1)), pltpu.SemaphoreType.DMA((2,))],
        compiler_params=pltpu.CompilerParams(collective_id=2, has_side_effects=True, vmem_limit_bytes=60 << 20),
    )(gu, dn)


def dense_kernel(sizes, cuts, *refs):
    n_in = len(cuts)
    ins, outs, rest = refs[:n_in], refs[n_in:2 * n_in], list(refs[2 * n_in:])
    spot = Spot(sizes)
    mate = spot.device(core=1 - spot.core)
    others = []
    for d in range(1, spot.ny):
        others.append((None, spot.device(y=lax.rem(spot.y + d, spot.ny))))
    enter(spot, line_neighbours(spot) + [(None, mate)] + others)
    sends, r1, r2, mate_sem, y_sem, out_sem, local = rest[-7:]
    pieces, drains = [], []
    number = 0
    for a in range(n_in):
        mine, one, two, ybuf, final = rest[5 * a:5 * a + 5]
        chunks = cuts[a]
        half = ins[a].shape[2] // 2
        wide = half // chunks
        for c in range(chunks):
            def cols(core, half=half, wide=wide, c=c):
                return pl.ds(pl.multiple_of(core * half + c * wide, 128), wide)
            pieces.append((number, a, c, wide, cols, mine, one, two, ybuf, final))
            number += 1
    reduces = []
    n_dp = spot.nz * spot.nx

    def to_mate(number, a, c, wide, cols, mine):
        return pltpu.make_async_remote_copy(
            src_ref=ins[a].at[:, :, cols(1 - spot.core)], dst_ref=mine.at[c], send_sem=mate_sem.at[0, number],
            recv_sem=mate_sem.at[1, number], device_id=mate, device_id_type=MESH)

    for number, a, c, wide, cols, mine, one, two, ybuf, final in pieces:
        to_mate(number, a, c, wide, cols, mine).start()
    for number, a, c, wide, cols, mine, one, two, ybuf, final in pieces:
        to_mate(number, a, c, wide, cols, mine).wait()
        own = ins[a]

        def add(o, carry, own=own, mine=mine, c=c, cols=cols):
            mine[c, o] = (mine[c, o].astype(jnp.float32) + own[o, :, cols(spot.core)].astype(jnp.float32)).astype(mine.dtype)
            return carry
        lax.fori_loop(0, n_dp, add, 0)
        r = Reduce(spot, number, lambda o, mine=mine, c=c: mine.at[c, o], one.at[c], two.at[c], sends, r1, r2, True)
        reduces.append(r)
        for step in r.phase_one():
            step()
    lists = [r.phase_two() for r in reduces]
    for turn in range(2):
        for l in lists:
            for step in l[turn * len(l) // 2:(turn + 1) * len(l) // 2]:
                step()
    for r, (number, a, c, wide, cols, mine, one, two, ybuf, final) in zip(reduces, pieces):
        r.finish(final.at[c])
        ybuf[c, spot.y] = final[c].astype(ybuf.dtype)
        for d in range(1, spot.ny):
            copy = pltpu.make_async_remote_copy(
                src_ref=ybuf.at[c, spot.y], dst_ref=ybuf.at[c, spot.y], send_sem=y_sem.at[0, number, d],
                recv_sem=y_sem.at[1, number, spot.y], device_id=spot.device(y=lax.rem(spot.y + d, spot.ny)),
                device_id_type=MESH)
            copy.start()
            drains.append(copy.wait_send)
    for number, a, c, wide, cols, mine, one, two, ybuf, final in pieces:
        for d in range(1, spot.ny):
            y = lax.rem(spot.y + d, spot.ny)
            pltpu.make_async_remote_copy(
                src_ref=ybuf.at[c, y], dst_ref=ybuf.at[c, y], send_sem=y_sem.at[0, number, d],
                recv_sem=y_sem.at[1, number, y], device_id=mate, device_id_type=MESH).wait_recv()
        total = ybuf[c, 0].astype(jnp.float32)
        for y in range(1, spot.ny):
            total = total + ybuf[c, y].astype(jnp.float32)
        final[c] = total
        outs[a][:, cols(spot.core)] = total
        copy = pltpu.make_async_remote_copy(
            src_ref=final.at[c], dst_ref=outs[a].at[:, cols(spot.core)], send_sem=out_sem.at[0, number],
            recv_sem=out_sem.at[1, number], device_id=mate, device_id_type=MESH)
        copy.start()
        drains.append(copy.wait_send)
    for number, a, c, wide, cols, mine, one, two, ybuf, final in pieces:
        pltpu.make_async_remote_copy(
            src_ref=final.at[c], dst_ref=outs[a].at[:, cols(1 - spot.core)], send_sem=out_sem.at[0, number],
            recv_sem=out_sem.at[1, number], device_id=mate, device_id_type=MESH).wait_recv()
    for r in reduces:
        drains += r.drains
    for drain in drains:
        drain()


def reduce_dense(sizes, arrays, cuts):
    nz, nx, ny = sizes[:3]
    n_dp = nz * nx
    big = max(nz, nx)
    arrays = [a.reshape(n_dp, a.shape[0] // n_dp, a.shape[1]) for a in arrays]
    items = sum(cuts)
    scratch = []
    for a, cut in zip(arrays, cuts):
        block = (a.shape[1], a.shape[2] // 2 // cut)
        scratch += [pltpu.VMEM((cut, n_dp) + block, a.dtype), pltpu.VMEM((cut, nx + 1, nz) + block, a.dtype),
                    pltpu.VMEM((cut, nz + 1) + block, a.dtype), pltpu.VMEM((cut, ny) + block, a.dtype),
                    pltpu.VMEM((cut,) + block, jnp.float32)]
    scratch += [pltpu.SemaphoreType.DMA((items, n_dp)), pltpu.SemaphoreType.DMA((items, big + 1, big)),
                pltpu.SemaphoreType.DMA((items, big + 1)), pltpu.SemaphoreType.DMA((2, items)),
                pltpu.SemaphoreType.DMA((2, items, ny)), pltpu.SemaphoreType.DMA((2, items)),
                pltpu.SemaphoreType.DMA((2,))]
    return pl.pallas_call(
        functools.partial(dense_kernel, sizes, tuple(cuts)),
        out_shape=tuple(jax.ShapeDtypeStruct(a.shape[1:], jnp.float32) for a in arrays),
        in_specs=[pl.BlockSpec(memory_space=pltpu.VMEM)] * len(arrays),
        out_specs=(pl.BlockSpec(memory_space=pltpu.VMEM),) * len(arrays),
        scratch_shapes=scratch,
        compiler_params=pltpu.CompilerParams(collective_id=3, has_side_effects=True, vmem_limit_bytes=60 << 20),
    )(*arrays)

def pair_tables(length):
    half = HEAD_DIM // 2
    inverse = np.float32(10000.0) ** (-(np.arange(half, dtype=np.float32) / np.float32(half)))
    angles = (np.arange(length, dtype=np.float32)[:, None] * inverse[None]).astype(np.float64)
    cosine, sine = np.cos(angles).astype(np.float32), np.sin(angles).astype(np.float32)
    return jnp.asarray(np.tile(cosine, (1, 4))), jnp.asarray(np.tile(np.concatenate([-sine, sine], 1), (1, 2)))


highest = lax.Precision.HIGHEST


def rope_tables(length, half):
    positions = jnp.arange(length).astype(jnp.float32)[:, None]
    inverse = 10000.0 ** (-(jnp.arange(half).astype(jnp.float32) / half))
    angles = positions * inverse[None, :]
    return (jnp.cos(angles)[:, None, :], jnp.sin(angles)[:, None, :])


def rotate(values, cosine, sine):
    half = values.shape[-1] // 2
    first = values[..., :half]
    second = values[..., half:]
    return jnp.concatenate(
        [first * cosine - second * sine, second * cosine + first * sine], axis=-1
    )


def rotate_back(grads, cosine, sine):
    half = grads.shape[-1] // 2
    first = grads[..., :half]
    second = grads[..., half:]
    return jnp.concatenate(
        [first * cosine + second * sine, second * cosine - first * sine], axis=-1
    )


def masked_scores(query_block, key_rows, block_start, segments, padding):
    block_rows = query_block.shape[0]
    scores = jnp.einsum("qhd,khd->hqk", query_block, key_rows, preferred_element_type=jnp.float32)
    row_index = block_start + jnp.arange(block_rows)
    col_index = jnp.arange(key_rows.shape[0])
    allowed = (
        (col_index[None, :] <= row_index[:, None])
        & (segments[:, None] == segments[None, :])
        & ((padding[None, :] == 1) | (col_index[None, :] == row_index[:, None]))
    )
    return jnp.where(allowed[None], scores, -1e30)


def norm_backward(values, inverse, gain, grad_normed):
    scaled = gain * grad_normed
    correction = jnp.sum(scaled * values, axis=-1, keepdims=True) / values.shape[-1]
    return (
        inverse * scaled - values * inverse * inverse * inverse * correction,
        jnp.sum(grad_normed * values * inverse, axis=0),
    )


def per_device(
    sizes,
    tokens,
    prev_logits,
    segment_ids,
    pad_mask,
    routes,
    slot_order,
    cotangent,
    attn_gain,
    qkv_weight,
    out_weight,
    ffn_gain,
    router_weight,
    mix_weight,
    const_weight,
    gate_up_weight,
    down_weight,
):
    length, width = tokens.shape
    owners = lax.axis_size("expert")
    real_count = owners * gate_up_weight.shape[0]
    capacity = 2 * length // (real_count + 4)
    hidden_units = gate_up_weight.shape[2] // 2
    heads = width // HEAD_DIM
    block_rows = min(length, 768)
    starts = jnp.arange(length // block_rows) * block_rows
    query_scale = HEAD_DIM ** (-0.5)
    small = jnp.concatenate(
        [attn_gain[:, None], ffn_gain[:, None], mix_weight, const_weight, router_weight], axis=1
    )
    rest = jnp.concatenate([out_weight, jnp.pad(small, ((0, 0), (0, 256 - small.shape[1])))], axis=1)
    cos_table, sin_table = pair_tables(length)
    (gate_up_local, down_local, qkv_full, rest_full, qf, kf, vf, normed, attended, ffn_normed, hidden_state, lse, scal,
     rows, flat, xin, gin) = run_front(
        sizes, real_count,
        (tokens, prev_logits, segment_ids, pad_mask, routes[0], slot_order.reshape(length, 2), cotangent,
         cos_table, sin_table, qkv_weight, rest, gate_up_weight[0], down_weight[0]))
    out_full = rest_full[:, :width]
    small_full = rest_full[:, width:]
    gain_one, gain_two = small_full[:, 0], small_full[:, 1]
    mix_full, const_full = small_full[:, 2:6], small_full[:, 6:8]
    router_full = small_full[:, 8 : 8 + router_weight.shape[1]]
    inputs = tokens.astype(jnp.float32)
    inverse_one = scal[:, 0:1]
    cosine, sine = rope_tables(length, HEAD_DIM // 2)
    queries, key_rows, value_rows = (t.reshape(length, heads, HEAD_DIM) for t in (qf, kf, vf))
    log_totals = lse[:, :heads].T[None]
    segments = segment_ids[0]
    padding = pad_mask[0]

    gain_float = gain_two.astype(jnp.float32)
    inverse_two = scal[:, 1:2]
    ffn_float = ffn_normed.astype(jnp.float32)
    route_rows = routes[0]
    route_ids = jnp.arange(real_count + 4)
    chosen = (route_rows[:, :, None] == route_ids[None, None, :]).astype(jnp.float32)
    gate_weights = scal[:, 2:4]
    mix = scal[:, 4:8].reshape(length, 2, 2)
    is_copy = (route_rows == real_count + 1).astype(jnp.float32)
    const_ids = real_count + 2 + jnp.arange(2)
    is_const = (route_rows[:, :, None] == const_ids[None, None, :]).astype(jnp.float32)
    route_copy = is_copy + jnp.sum(is_const * mix[:, None, :, 0], axis=-1)
    copy_coef = jnp.sum(gate_weights * route_copy, axis=-1)
    const_select = jnp.sum(gate_weights[:, :, None] * is_const, axis=1)
    const_coef = const_select * mix[:, :, 1]
    flat_slot = scal[:, 8:10].astype(jnp.int32).reshape(2 * length)
    received = xin
    expert_input = xin.reshape(-1, width)
    projected = jnp.dot(expert_input, gate_up_local, preferred_element_type=jnp.float32)
    gate_part = projected[:, :hidden_units]
    up_part = projected[:, hidden_units:]
    activated = (jax.nn.silu(gate_part) * up_part).astype(jnp.bfloat16)
    expert_out = (
        jnp.dot(activated, down_local, preferred_element_type=jnp.float32)
        .astype(jnp.bfloat16)
        .reshape(received.shape)
    )
    returned = lax.all_to_all(expert_out, "expert", split_axis=0, concat_axis=0, tiled=True)
    returned_rows = jnp.concatenate(
        [returned.reshape(-1, width), jnp.zeros((1, width), jnp.bfloat16)], axis=0
    )
    pair_rows = returned_rows[flat_slot].astype(jnp.float32).reshape(length, 2, width)
    const_float = const_full.astype(jnp.float32)
    branch_out = (
        jnp.sum(gate_weights[:, :, None] * pair_rows, axis=1)
        + copy_coef[:, None] * ffn_float
        + jnp.dot(const_coef, const_float.T, precision=highest)
    )
    layer_out = (hidden_state + branch_out).astype(jnp.bfloat16)
    qkv_back, out_back, router_back, mix_back = qkv_full, out_full, router_full, mix_full
    gate_up_back, down_back = gate_up_local, down_local
    out_grad = cotangent.astype(jnp.float32)
    expert_out_grad = gin.reshape(-1, width)
    activated_grad = jnp.einsum(
        "rd,fd->rf", expert_out_grad, down_back, preferred_element_type=jnp.float32
    )
    sigmoid_gate = jax.nn.sigmoid(gate_part)
    gate_grad = activated_grad * up_part * sigmoid_gate * (1.0 + gate_part * (1.0 - sigmoid_gate))
    up_grad = activated_grad * gate_part * sigmoid_gate
    projected_grad = jnp.concatenate([gate_grad, up_grad], axis=1).astype(jnp.bfloat16)
    down_weight_grad = jnp.einsum(
        "rf,rd->fd", activated, expert_out_grad, preferred_element_type=jnp.float32
    )
    gate_up_weight_grad = jnp.einsum(
        "rd,rf->df", expert_input, projected_grad, preferred_element_type=jnp.float32
    )
    input_grad_rows = jnp.einsum(
        "rf,df->rd", projected_grad, gate_up_back, preferred_element_type=jnp.float32
    ).astype(jnp.bfloat16)
    back_rows = lax.all_to_all(
        input_grad_rows.reshape(received.shape), "expert", split_axis=0, concat_axis=0, tiled=True
    )
    back_padded = jnp.concatenate(
        [back_rows.reshape(-1, width), jnp.zeros((1, width), jnp.bfloat16)], axis=0
    )
    routed_grad = jnp.sum(
        back_padded[flat_slot].astype(jnp.float32).reshape(length, 2, width), axis=1
    )
    gate_up_shard, down_shard = reduce_experts(
        sizes, gate_up_weight_grad.astype(jnp.bfloat16), down_weight_grad.astype(jnp.bfloat16)
    )
    grad_dot_normed = jnp.sum(out_grad * ffn_float, axis=-1)
    grad_dot_const = jnp.dot(out_grad, const_float, precision=highest)
    grad_dot_pairs = jnp.sum(out_grad[:, None, :] * pair_rows, axis=-1)
    gate_grads = (
        grad_dot_pairs
        + route_copy * grad_dot_normed[:, None]
        + jnp.sum(is_const * (mix[:, None, :, 1] * grad_dot_const[:, None, :]), axis=-1)
    )
    picked_grad = gate_weights * (
        gate_grads - jnp.sum(gate_weights * gate_grads, axis=-1, keepdims=True)
    )
    prev_grad = jnp.sum(chosen * picked_grad[:, :, None], axis=1)
    logits_low = prev_grad.astype(jnp.bfloat16)
    router_weight_grad = jnp.einsum(
        "ld,lr->dr", ffn_normed, logits_low, preferred_element_type=jnp.float32
    )
    mix_grad = jnp.stack(
        [const_select * grad_dot_normed[:, None], const_select * grad_dot_const], axis=-1
    )
    mix_logit_grad = (
        (mix * (mix_grad - jnp.sum(mix * mix_grad, axis=-1, keepdims=True)))
        .reshape(length, 4)
        .astype(jnp.bfloat16)
    )
    mix_weight_grad = jnp.einsum(
        "ld,lm->dm", ffn_normed, mix_logit_grad, preferred_element_type=jnp.float32
    )
    const_weight_grad = jnp.einsum("ld,lj->dj", out_grad, const_coef, precision=highest)
    normed_two_grad = routed_grad + copy_coef[:, None] * out_grad
    normed_two_grad = normed_two_grad + jnp.einsum(
        "lr,dr->ld", logits_low, router_back, preferred_element_type=jnp.float32
    )
    normed_two_grad = normed_two_grad + jnp.einsum(
        "lm,dm->ld", mix_logit_grad, mix_back, preferred_element_type=jnp.float32
    )
    hidden_part, gain_two_grad = norm_backward(
        hidden_state, inverse_two, gain_float, normed_two_grad
    )
    hidden_grad = out_grad + hidden_part
    attn_grad = hidden_grad.astype(jnp.bfloat16)
    out_weight_grad = jnp.einsum(
        "ld,le->de", attended, attn_grad, preferred_element_type=jnp.float32
    )
    attended_grad = (
        jnp.einsum("le,de->ld", attn_grad, out_back, preferred_element_type=jnp.float32)
        .astype(jnp.bfloat16)
        .reshape(length, heads, HEAD_DIM)
    )

    def backward_block(carry, block_input):
        key_grad, value_grad = carry
        block_start, log_block = block_input
        scores = masked_scores(queries, key_rows, block_start, segments, padding)
        probs_full = jnp.exp(scores - log_block[..., None])
        probs_low = probs_full.astype(jnp.bfloat16)
        prob_grad = jnp.einsum(
            "qhd,khd->hqk", attended_grad, value_rows, preferred_element_type=jnp.float32
        )
        row_dot = jnp.sum(probs_full * prob_grad, axis=-1, keepdims=True)
        score_grad = (probs_full * (prob_grad - row_dot)).astype(jnp.bfloat16)
        query_grad = jnp.einsum(
            "hqk,khd->qhd", score_grad, key_rows, preferred_element_type=jnp.float32
        )
        key_grad = key_grad + jnp.einsum(
            "hqk,qhd->khd", score_grad, queries, preferred_element_type=jnp.float32
        )
        value_grad = value_grad + jnp.einsum(
            "hqk,qhd->khd", probs_low, attended_grad, preferred_element_type=jnp.float32
        )
        return ((key_grad, value_grad), query_grad)

    zero_heads = jnp.zeros((length, heads, HEAD_DIM), jnp.float32)
    (key_grad, value_grad), query_grads = lax.scan(
        backward_block, (zero_heads, zero_heads), (starts, log_totals)
    )
    query_grad = query_grads.reshape(length, heads, HEAD_DIM)
    qkv_grad = (
        jnp.stack(
            [
                rotate_back(query_grad * query_scale, cosine, sine),
                rotate_back(key_grad, cosine, sine),
                value_grad,
            ],
            axis=1,
        )
        .reshape(length, 3 * width)
        .astype(jnp.bfloat16)
    )
    qkv_weight_grad = jnp.einsum("ld,le->de", normed, qkv_grad, preferred_element_type=jnp.float32)
    normed_one_grad = jnp.einsum(
        "le,de->ld", qkv_grad, qkv_back, preferred_element_type=jnp.float32
    )
    input_part, gain_one_grad = norm_backward(
        inputs, inverse_one, gain_one.astype(jnp.float32), normed_one_grad
    )
    tokens_grad = hidden_grad + input_part
    small_grad = jnp.concatenate(
        [gain_one_grad[:, None], gain_two_grad[:, None], mix_weight_grad, const_weight_grad, router_weight_grad], axis=1
    )
    rest_grad = jnp.concatenate(
        [out_weight_grad, jnp.pad(small_grad, ((0, 0), (0, 256 - small_grad.shape[1])))], axis=1
    )
    qkv_shard, rest_shard = reduce_dense(
        sizes, [qkv_weight_grad.astype(jnp.bfloat16), rest_grad.astype(jnp.bfloat16)], [3, 1]
    )
    small_shard = rest_shard[:, width:]
    return (
        layer_out,
        tokens_grad,
        prev_grad,
        small_shard[:, 0],
        qkv_shard,
        rest_shard[:, :width],
        small_shard[:, 1],
        small_shard[:, 8 : 8 + router_weight.shape[1]],
        small_shard[:, 2:6],
        small_shard[:, 6:8],
        gate_up_shard[None],
        down_shard[None],
    )


def grid_sizes(mesh):
    along_dp, along_expert = mesh.devices[:, 0], mesh.devices[0]
    nx = len({d.coords[0] for d in along_dp})
    ny = len({d.coords[1] for d in along_expert})
    return (len(along_dp) // nx, nx, ny, len(along_expert) // ny)


def solution(mesh):
    in_specs = (
        P(("dp", "expert"), None),
        P(("dp", "expert"), None),
        P(("dp", "expert"), None),
        P(("dp", "expert"), None),
        P(("dp", "expert"), None, None),
        P(("dp", "expert"), None),
        P(("dp", "expert"), None),
        P("dp"),
        P("dp", None),
        P("dp", None),
        P("dp"),
        P("dp", None),
        P("dp", None),
        P("dp", None),
        P("expert", "dp", None),
        P("expert", "dp", None),
    )
    out_specs = (
        P(("dp", "expert"), None),
        P(("dp", "expert"), None),
        P(("dp", "expert"), None),
        P("dp"),
        P("dp", None),
        P("dp", None),
        P("dp"),
        P("dp", None),
        P("dp", None),
        P("dp", None),
        P("expert", "dp", None),
        P("expert", "dp", None),
    )
    return jax.shard_map(
        functools.partial(per_device, grid_sizes(mesh)), mesh=mesh, in_specs=in_specs, out_specs=out_specs, check_vma=False
    )
```

```python
import functools
from types import SimpleNamespace
from typing import NamedTuple

import jax
import jax.numpy as jnp
from jax import lax
from jax.experimental import pallas as pl
from jax.experimental.pallas import tpu as pltpu
import numpy as np
from jax.sharding import PartitionSpec as P

HEAD_DIM = 64
BLOCK = 256
LONGEST = 384
LEVEL_STEP = 2.5
LEAD = 4.0
EARLY = 5
SHARE = 7
epsilon = 1e-06


MESH = pl.DeviceIdType.MESH


class Spot:
    def __init__(self, sizes):
        self.nz, self.nx, self.ny, self.nc = sizes
        self.dp, self.ex = lax.axis_index("dp"), lax.axis_index("expert")
        self.z, self.x = lax.div(self.dp, self.nx), lax.rem(self.dp, self.nx)
        self.y, self.core = lax.div(self.ex, self.nc), lax.rem(self.ex, self.nc)

    def device(self, z=None, x=None, y=None, core=None):
        z, x = self.z if z is None else z, self.x if x is None else x
        y, core = self.y if y is None else y, self.core if core is None else core
        return {"dp": z * self.nx + x, "expert": y * self.nc + core}


def between(value, size):
    return jnp.logical_and(value >= 0, value < size)


class Flood:
    def __init__(self, spot, number, own, view, sends, recvs, z_first, mate=None):
        self.s, self.n, self.own, self.view = spot, number, own, view
        self.sends, self.recvs, self.z_first, self.mate = sends, recvs, z_first, mate
        if z_first:
            self.na, self.nb, self.a, self.b = spot.nz, spot.nx, spot.z, spot.x
        else:
            self.na, self.nb, self.a, self.b = spot.nx, spot.nz, spot.x, spot.z
        self.drains = []

    def origin(self, a, b):
        return a * self.s.nx + b if self.z_first else b * self.s.nx + a

    def along(self, which, value):
        zed = (which == 0) == self.z_first
        return self.s.device(z=value) if zed else self.s.device(x=value)

    def push(self, cond, src, o, way, device, recvs=None):
        copy = pltpu.make_async_remote_copy(
            src_ref=src, dst_ref=self.view(o),
            send_sem=self.sends.at[way, self.n, o],
            recv_sem=(self.recvs if recvs is None else recvs).at[self.n, o],
            device_id=device, device_id_type=MESH)
        if cond is None:
            copy.start()
            self.drains.append(copy.wait_send)
        else:
            pl.when(cond)(lambda: copy.start())
            self.drains.append(lambda: pl.when(cond)(lambda: copy.wait_send()))

    def share(self, cond, src, o):
        if self.mate is not None:
            self.push(cond, src, o, 4, self.s.device(core=1 - self.s.core), self.mate)

    def mates(self, view):
        def one(o, carry):
            pltpu.make_async_remote_copy(
                src_ref=view(o), dst_ref=view(o), send_sem=self.sends.at[0, self.n, o], recv_sem=self.mate.at[self.n, o],
                device_id=self.s.device(), device_id_type=MESH).wait_recv()
            return carry
        lax.fori_loop(0, self.s.nz * self.s.nx, one, 0)

    def arrive(self, o):
        pltpu.make_async_remote_copy(
            src_ref=self.view(o), dst_ref=self.view(o),
            send_sem=self.sends.at[0, self.n, o], recv_sem=self.recvs.at[self.n, o],
            device_id=self.s.device(), device_id_type=MESH).wait_recv()

    def second(self, cond, src, o):
        for j, sign in enumerate((1, -1)):
            to = self.b + sign
            if self.nb > 1:
                ok = between(to, self.nb)
                self.push(ok if cond is None else jnp.logical_and(cond, ok), src, o, 2 + j, self.along(1, to))

    def levels(self):
        out = [[] for _ in range(self.na + self.nb - 1)]

        def begin():
            o = self.origin(self.a, self.b)
            for j, sign in enumerate((1, -1)):
                if self.na > 1:
                    self.push(between(self.a + sign, self.na), self.own, o, j, self.along(0, self.a + sign))
            self.second(None, self.own, o)
            self.share(None, self.own, o)

        out[0].append(begin)
        for k in range(1, self.na):
            for j, sign in enumerate((1, -1)):
                def step(k=k, j=j, sign=sign):
                    a = self.a - sign * k
                    here = between(a, self.na)
                    o = self.origin(a, self.b)
                    pl.when(here)(lambda: self.arrive(o))
                    on = jnp.logical_and(here, between(self.a + sign, self.na))
                    if self.na > 2 or k == 0:
                        self.push(on, self.view(o), o, j, self.along(0, self.a + sign))
                    self.second(here, self.view(o), o)
                    self.share(here, self.view(o), o)
                out[k].append(step)
        for d in range(1, self.nb):
            for da in range(-(self.na - 1), self.na):
                for j, sign in enumerate((1, -1)):
                    def step(d=d, da=da, j=j, sign=sign):
                        a, b = self.a + da, self.b - sign * d
                        here = jnp.logical_and(between(a, self.na), between(b, self.nb))
                        o = self.origin(a, b)
                        pl.when(here)(lambda: self.arrive(o))
                        if self.nb > 2:
                            on = jnp.logical_and(here, between(self.b + sign, self.nb))
                            self.push(on, self.view(o), o, 2 + j, self.along(1, self.b + sign))
                        self.share(here, self.view(o), o)
                    out[abs(da) + d].append(step)
        return out


def enter(spot, devices):
    barrier = pltpu.get_barrier_semaphore()
    count = jnp.int32(0)
    for cond, device in devices:
        def hail(device=device):
            pl.semaphore_signal(barrier, inc=1, device_id=device, device_id_type=MESH)
        if cond is None:
            hail()
            count = count + 1
        else:
            pl.when(cond)(hail)
            count = count + cond.astype(jnp.int32)
    pl.semaphore_wait(barrier, count)


def line_neighbours(spot):
    out = []
    for sign in (1, -1):
        out.append((between(spot.z + sign, spot.nz), spot.device(z=spot.z + sign)))
        out.append((between(spot.x + sign, spot.nx), spot.device(x=spot.x + sign)))
    return out


def dot(a, b, ca=1, cb=0):
    return lax.dot_general(a, b, (((ca,), (cb,)), ((), ())), preferred_element_type=jnp.float32)


def turned(columns):
    eye = lax.broadcasted_iota(jnp.int32, (128, 128), 0) == lax.broadcasted_iota(jnp.int32, (128, 128), 1)
    return dot(jnp.where(eye, 1.0, 0.0).astype(jnp.bfloat16), columns, 1, 1)


def spread(columns):
    lane = lax.broadcasted_iota(jnp.int32, (columns[0].shape[0], 128), 1)
    out = jnp.zeros(lane.shape, jnp.float32)
    for j, c in enumerate(columns):
        out = jnp.where(lane == j, c, out)
    return out


def swap_halves(v):
    half = HEAD_DIM // 2
    lane = lax.broadcasted_iota(jnp.int32, v.shape, 1)
    return jnp.where(lax.rem(lane, HEAD_DIM) < half, pltpu.roll(v, v.shape[1] - half, 1), pltpu.roll(v, half, 1))


def head_masks():
    lane = lax.broadcasted_iota(jnp.int32, (1, 128), 1)
    low = jnp.where(lane < HEAD_DIM, 1.0, 0.0).astype(jnp.bfloat16)
    high = jnp.where(lane < HEAD_DIM, 0.0, 1.0).astype(jnp.bfloat16)
    return low, high


def key_range(i):
    return max(0, i * BLOCK - LONGEST), (i + 1) * BLOCK


class Front:
    def __init__(self, spot, experts, chunks, r):
        self.spot, self.experts, self.r = spot, experts, r
        self.length, self.width = r.tokens.shape
        self.capacity = 2 * self.length // (experts + 4)
        self.blocks = self.length // BLOCK
        self.tall, self.wide = self.length // 2, r.dn.shape[0] // chunks

    def ranks(self):
        r, n = self.r, self.length
        order = [r.order[:, k : k + 1] for k in range(2)]
        route = [r.routes[:, k : k + 1] for k in range(2)]
        parts = []
        for k in range(2):
            parts += [lax.div(order[k], 256).astype(jnp.float32), lax.rem(order[k], 256).astype(jnp.float32)]
        parts += [route[k].astype(jnp.float32) for k in range(2)]
        side = turned(spread(parts).astype(jnp.bfloat16))
        order_row = [side[2 * k : 2 * k + 1] * 256.0 + side[2 * k + 1 : 2 * k + 2] for k in range(2)]
        route_row = [side[4 + k : 5 + k] for k in range(2)]
        out = []
        for k in range(2):
            for i in range(self.blocks):
                rows = slice(i * BLOCK, (i + 1) * BLOCK)
                mine, kind = order[k][rows].astype(jnp.float32), route[k][rows].astype(jnp.float32)
                ahead = jnp.zeros((BLOCK, n), jnp.float32)
                for other in range(2):
                    ahead += jnp.where(
                        jnp.logical_and(order_row[other] < mine, route_row[other] == kind), 1.0, 0.0)
                rank = jnp.sum(ahead, axis=1, keepdims=True)
                kept = jnp.logical_and(kind < self.experts, rank < self.capacity)
                r.scal[pl.ds(i * BLOCK, BLOCK), 8 + k : 9 + k] = jnp.where(
                    kept, kind * self.capacity + rank, float(self.experts * self.capacity))
                r.scal[pl.ds(i * BLOCK, BLOCK), 10 + k : 11 + k] = jnp.where(kept, kind, 255.0)
                r.scal[pl.ds(i * BLOCK, BLOCK), 12 + k : 13 + k] = jnp.where(kept, rank, 0.0)
                r.scal[pl.ds(i * BLOCK, BLOCK), 14 + k : 15 + k] = kind

    def flat_rows(self):
        r = self.r
        side = turned(r.scal[...].astype(jnp.bfloat16))
        for k in range(2):
            kind, rank = side[10 + k : 11 + k], side[12 + k : 13 + k]
            r.flat[k : k + 1] = jnp.where(
                kind < 255.0, kind * self.capacity + rank, float(self.experts * self.capacity))

    def first_norm(self):
        r = self.r
        for i in range(self.blocks):
            rows = pl.ds(i * BLOCK, BLOCK)
            x = r.tokens[rows].astype(jnp.float32)
            r.scal[rows, 0:1] = lax.rsqrt(jnp.mean(x * x, axis=1, keepdims=True) + epsilon)

    def masks(self):
        r, n = self.r, self.length
        segment = r.segments[...].astype(jnp.float32)
        padding = r.padding[...]
        column = jnp.transpose(jnp.broadcast_to(segment, (128, n)))[:, 0:1]
        for i in range(self.blocks):
            k0, k1 = key_range(i)
            row = lax.broadcasted_iota(jnp.int32, (BLOCK, k1 - k0), 0) + i * BLOCK
            col = lax.broadcasted_iota(jnp.int32, (BLOCK, k1 - k0), 1) + k0
            same = column[i * BLOCK : (i + 1) * BLOCK] == segment[:, k0:k1]
            real = jnp.broadcast_to(padding[:, k0:k1], row.shape) == 1
            fine = jnp.logical_and(jnp.logical_and(col <= row, same), jnp.logical_or(real, col == row))
            r.bias[pl.ds(i * BLOCK, BLOCK), pl.ds(0, k1 - k0)] = jnp.where(fine, 0.0, -1e30)

    def small_rows(self):
        r = self.r
        side = turned(r.rest[:, pl.ds(self.width, 128)])
        r.rows[...] = side[: r.rows.shape[0]]

    def project(self, i):
        r, w = self.r, self.width
        rows = pl.ds(i * BLOCK, BLOCK)
        x = r.tokens[rows].astype(jnp.float32)
        normed = (x * r.scal[rows, 0:1] * r.rows[0:1]).astype(jnp.bfloat16)
        r.normed[rows] = normed
        cosine, sine = r.cosine[rows], r.sine[rows]
        for part, to in enumerate((r.q, r.k)):
            full = dot(normed, r.qkv[:, pl.ds(part * w, w)])
            for pair in range(w // 128):
                v = full[:, pair * 128 : pair * 128 + 128]
                v = v * cosine + swap_halves(v) * sine
                if part == 0:
                    v = v * HEAD_DIM ** (-0.5)
                to[rows, pl.ds(pair * 128, 128)] = v.astype(jnp.bfloat16)
        r.v[rows] = dot(normed, r.qkv[:, pl.ds(2 * w, w)]).astype(jnp.bfloat16)

    def attend(self, i, pair):
        r = self.r
        k0, k1 = key_range(i)
        rows, keys, lanes = pl.ds(i * BLOCK, BLOCK), pl.ds(k0, k1 - k0), pl.ds(pair * 128, 128)
        q, k, v = r.q[rows, lanes], r.k[keys, lanes], r.v[keys, lanes]
        bias = r.bias[rows, pl.ds(0, k1 - k0)]
        out = jnp.zeros((BLOCK, 128), jnp.float32)
        for s, mask in enumerate(head_masks()):
            scores = dot(q * mask, k, 1, 1) + bias
            top = jnp.max(scores, axis=1, keepdims=True)
            e = jnp.exp(scores - top)
            total = jnp.sum(e, axis=1, keepdims=True)
            probs = (e * (1.0 / total)).astype(jnp.bfloat16)
            out = out + dot(probs, v * mask)
            r.lse[rows, 2 * pair + s : 2 * pair + s + 1] = top + jnp.log(total)
        r.attended[rows, lanes] = out.astype(jnp.bfloat16)

    def gate(self, i):
        r, w, e = self.r, self.width, self.experts
        rows = pl.ds(i * BLOCK, BLOCK)
        h = r.tokens[rows].astype(jnp.float32) + dot(r.attended[rows], r.rest[:, pl.ds(0, w)])
        r.h[rows] = h
        inverse = lax.rsqrt(jnp.mean(h * h, axis=1, keepdims=True) + epsilon)
        hn = (h * inverse * r.rows[1:2]).astype(jnp.bfloat16)
        r.hn[rows] = hn
        small = dot(hn, r.rest[:, pl.ds(w, 128)])
        lane = lax.broadcasted_iota(jnp.int32, small.shape, 1)
        prev = r.prev[rows].astype(jnp.float32)
        prev_lane = lax.broadcasted_iota(jnp.int32, prev.shape, 1)
        picked = []
        for k in range(2):
            route = r.routes[rows, k : k + 1]
            picked.append(jnp.sum(jnp.where(lane == route + 8, small, 0.0), axis=1, keepdims=True)
                          + jnp.sum(jnp.where(prev_lane == route, prev, 0.0), axis=1, keepdims=True))
        def soft(a, b):
            top = jnp.maximum(a, b)
            ea, eb = jnp.exp(a - top), jnp.exp(b - top)
            return ea / (ea + eb), eb / (ea + eb)
        gates = soft(*picked)
        mix = soft(small[:, 2:3], small[:, 3:4]) + soft(small[:, 4:5], small[:, 5:6])
        r.scal[rows, 1:2] = inverse
        for j, c in enumerate(gates + mix):
            r.scal[rows, 2 + j : 3 + j] = c
        cot = r.cot[rows].astype(jnp.float32)
        for k in range(2):
            r.gcot[k, rows] = (gates[k] * cot).astype(jnp.bfloat16)

    def slots(self, d):
        r, n = self.r, self.length
        e = lax.rem(self.spot.ex + d, self.experts)
        slot = (lax.broadcasted_iota(jnp.int32, (self.capacity, n), 0) + e * self.capacity).astype(jnp.float32)
        at = [jnp.where(r.flat[k : k + 1] == slot, 1.0, 0.0) for k in range(2)]
        x = dot((at[0] + at[1]).astype(jnp.bfloat16), r.hn[...]).astype(jnp.bfloat16)
        g = (dot(at[0].astype(jnp.bfloat16), r.gcot[0]) + dot(at[1].astype(jnp.bfloat16), r.gcot[1]))
        g = g.astype(jnp.bfloat16)
        if d == 0:
            rows = pl.ds(pl.multiple_of(e * self.capacity, 16), self.capacity)
            r.xin[rows], r.gin[rows] = x, g
        else:
            r.sendx[d - 1], r.sendg[d - 1] = x, g


    def side_rows(self):
        self.r.xt[...] = jnp.transpose(self.r.xin[...])

    def hidden(self, j, part):
        r, w = self.r, self.wide
        ff = r.gu.shape[1] // 2
        rows = pl.ds(part * self.tall, self.tall)
        x, g = r.xin[rows], r.gin[rows]
        gate = dot(x, r.gu[:, pl.ds(j * w, w)])
        up = dot(x, r.gu[:, pl.ds(ff + j * w, w)])
        back = dot(g, r.dn[pl.ds(j * w, w)], 1, 1)
        sigmoid = 1.0 / (1.0 + jnp.exp(-gate))
        silu = gate * sigmoid
        r.act[rows, pl.ds(j * w, w)] = (silu * up).astype(jnp.bfloat16)
        r.pg[rows, pl.ds(j * w, w)] = (back * up * sigmoid * (1.0 + gate * (1.0 - sigmoid))).astype(jnp.bfloat16)
        r.pg[rows, pl.ds(ff + j * w, w)] = (back * silu).astype(jnp.bfloat16)

    def outward(self, part):
        rows = pl.ds(part * self.tall, self.tall)
        self.r.yall[rows] = dot(self.r.act[rows], self.r.dn[...]).astype(jnp.bfloat16)

    def inward(self, part):
        rows = pl.ds(part * self.tall, self.tall)
        self.r.dxall[rows] = dot(self.r.pg[rows], self.r.gu[...], 1, 1).astype(jnp.bfloat16)

    def down_grad(self, j):
        r, w = self.r, self.wide
        r.dn[pl.ds(j * w, w)] = dot(r.act[:, pl.ds(j * w, w)], r.gin[...], 0, 0).astype(jnp.bfloat16)

    def up_grad(self, j):
        r, w = self.r, self.wide
        r.gu[:, pl.ds(j * w, w)] = dot(r.xt[...], r.pg[:, pl.ds(j * w, w)]).astype(jnp.bfloat16)


def expert_device(spot, e):
    return {"dp": spot.dp, "expert": e}


def slots_of(ref, capacity):
    return lambda e: ref.at[pl.ds(pl.multiple_of(e * capacity, 16), capacity)]


class Exchange:
    def __init__(self, spot, experts, number, out, into, sems):
        self.spot, self.experts, self.n, self.out, self.into, self.sems = spot, experts, number, out, into, sems

    def copy(self, d):
        e = lax.rem(self.spot.ex + d, self.experts)
        return pltpu.make_async_remote_copy(
            src_ref=self.out(d), dst_ref=self.into(self.spot.ex), send_sem=self.sems.at[0, self.n, d],
            recv_sem=self.sems.at[1, self.n, self.spot.ex], device_id=expert_device(self.spot, e),
            device_id_type=MESH)

    def send(self, d):
        self.copy(d).start()

    def drain(self, d):
        self.copy(d).wait_send()

    def receive(self, d):
        e = lax.rem(self.spot.ex + d, self.experts)
        pltpu.make_async_remote_copy(
            src_ref=self.into(e), dst_ref=self.into(e), send_sem=self.sems.at[0, self.n, d],
            recv_sem=self.sems.at[1, self.n, e], device_id=expert_device(self.spot, e),
            device_id_type=MESH).wait_recv()


def woven(work, events):
    done = 0
    for j, piece in enumerate(work):
        piece()
        upto = (j + 1) * len(events) // len(work)
        for event in events[done:upto]:
            event()
        done = upto


class FrontIns(NamedTuple):
    tokens: object
    prev: object
    segments: object
    padding: object
    routes: object
    order: object
    cot: object
    cosine: object
    sine: object
    qkv_own: object
    rest_own: object
    gu_own: object
    dn_own: object


class FrontOuts(NamedTuple):
    gu_grad: object
    dn_grad: object
    qkv_hbm: object
    rest_hbm: object
    q_hbm: object
    k_hbm: object
    v_hbm: object
    normed_hbm: object
    attended_hbm: object
    hn_hbm: object
    h_hbm: object
    lse_hbm: object
    scal_hbm: object
    rows_hbm: object
    y_hbm: object
    dx_hbm: object


class FrontScratch(NamedTuple):
    qkv: object
    rest: object
    q: object
    k: object
    v: object
    normed: object
    attended: object
    hn: object
    h: object
    lse: object
    scal: object
    rows: object
    gu: object
    dn: object
    xin: object
    gin: object
    xt: object
    act: object
    pg: object
    yall: object
    dxall: object
    flat: object
    bias: object
    gcot: object
    sendx: object
    sendg: object
    sends: object
    recvs: object
    mates: object
    local: object
    trade: object


def front_kernel(sizes, experts, chunks, *refs):
    r = SimpleNamespace(**dict(zip(FrontIns._fields + FrontOuts._fields + FrontScratch._fields, refs)))
    spot = Spot(sizes)
    front = Front(spot, experts, chunks, r)
    enter(spot, line_neighbours(spot)
          + [(None, expert_device(spot, lax.rem(spot.ex + d, experts))) for d in range(1, experts)])
    rows = r.qkv_own.shape[0]
    rows_d = r.dn_own.shape[0]
    ff = r.dn.shape[0]
    first, later = [], []
    for src, out in ((r.qkv_own, r.qkv), (r.rest_own, r.rest)):
        part = src.shape[1] // 2
        def half(o, core, out=out, part=part):
            return out.at[pl.ds(pl.multiple_of(o * rows, 8), rows), pl.ds(pl.multiple_of(core * part, 128), part)]
        first.append((src.at[:, pl.ds(pl.multiple_of(spot.core * part, 128), part)],
                      lambda o, half=half: half(o, spot.core), True, lambda o, half=half: half(o, 1 - spot.core)))
    part = rows_d // 2
    for p, zf in ((0, True), (1, False)):
        later.append((r.dn_own.at[pl.ds(p * part, part)],
                      lambda o, p=p: r.dn.at[pl.ds(pl.multiple_of(o * rows_d + p * part, 8), part)], zf, None))
    wide = ff // chunks
    for c in range(chunks):
        for side in range(2):
            cols = pl.ds(side * ff + c * wide, wide)
            later.append((r.gu_own.at[:, cols],
                          lambda o, cols=cols: r.gu.at[pl.ds(pl.multiple_of(o * rows, 8), rows), cols], True, None))
    floods = [Flood(spot, n, own, view, r.sends, r.recvs, zf, None if other is None else r.mates)
              for n, (own, view, zf, other) in enumerate(first + later)]
    levels = [f.levels() for f in floods]
    dense = levels[:2]
    keeps = [pltpu.make_async_copy(own, view(spot.dp), r.local.at[n])
             for n, (own, view, zf, other) in enumerate(first + later)]
    for ls in dense:
        for step in ls[0]:
            step()
    for keep in keeps:
        keep.start()
    front.ranks()
    front.flat_rows()
    front.first_norm()
    front.masks()
    depth = max(map(len, levels))
    keyed = []
    for n, ls in enumerate(levels[2:]):
        for level, steps in enumerate(ls):
            keyed += [(n + LEVEL_STEP * level if level else n - LEAD, n, level, step) for step in steps]
    keyed.sort(key=lambda t: t[:3])
    ahead = [t for t in keyed if t[0] <= 0]
    keyed = keyed[len(ahead):]
    for level in range(1, depth):
        if level == depth - 1:
            for t in ahead:
                t[3]()
        for ls in dense:
            if level < len(ls):
                for step in ls[level]:
                    step()
    for keep in keeps[:2]:
        keep.wait()
    for f, (own, view, zf, other) in zip(floods, first):
        f.mates(other)
    trades = [Exchange(spot, experts, n, lambda d, out=out: out.at[d - 1], slots_of(into, front.capacity), r.trade)
              for n, (out, into) in enumerate(((r.sendx, r.xin), (r.sendg, r.gin)))]
    work = [front.small_rows]
    work += [functools.partial(front.project, i) for i in range(front.blocks)]
    for pair in range(front.width // 128):
        work += [functools.partial(front.attend, i, pair) for i in range(front.blocks)]
    work += [functools.partial(front.gate, i) for i in range(front.blocks)]
    def dispatch(d):
        front.slots(d)
        if d:
            for t in trades:
                t.send(d)
    work += [functools.partial(dispatch, d) for d in list(range(1, experts)) + [0]]
    def upto(item):
        out = []
        while keyed and keyed[0][1] <= item:
            out.append(keyed.pop(0)[3])
        last = max((j for j, t in enumerate(keyed) if t[1] <= item), default=-1)
        out += [t[3] for t in keyed[: last + 1]]
        del keyed[: last + 1]
        return out
    saves = []
    def save(src, dst):
        copy = pltpu.make_async_copy(src, dst, r.local.at[len(keeps) + len(saves)])
        copy.start()
        saves.append(copy)
    def save_dense():
        for src, dst in ((r.qkv, r.qkv_hbm), (r.rest, r.rest_hbm), (r.q, r.q_hbm), (r.k, r.k_hbm), (r.v, r.v_hbm),
                         (r.normed, r.normed_hbm), (r.attended, r.attended_hbm), (r.lse, r.lse_hbm), (r.rows, r.rows_hbm),
                         (r.hn, r.hn_hbm), (r.h, r.h_hbm), (r.scal, r.scal_hbm)):
            save(src, dst)
    events = []
    early = len(keyed) * SHARE // 16
    events, keyed[:early] = [t[3] for t in keyed[:early]], []
    woven(work, events)
    save_dense()
    for event in upto(1 + 2):
        event()
    for d in range(1, experts):
        for t in trades:
            t.receive(d)
    keeps[2].wait()
    keeps[3].wait()
    front.side_rows()
    for c in range(chunks):
        for event in upto(2 + 2 * c + 1):
            event()
        keeps[4 + 2 * c].wait()
        keeps[5 + 2 * c].wait()
        for p in range(2):
            front.hidden(c, p)
    for p in range(2):
        front.outward(p)
    save(r.yall, r.y_hbm)
    for p in range(2):
        front.inward(p)
    save(r.dxall, r.dx_hbm)
    for f in floods:
        for drain in f.drains:
            drain()
    for c in range(chunks):
        front.down_grad(c)
        save(r.dn.at[pl.ds(c * wide, wide)], r.dn_grad.at[pl.ds(c * wide, wide)])
    for c in range(2 * chunks):
        front.up_grad(c)
        save(r.gu.at[:, pl.ds(c * wide, wide)], r.gu_grad.at[:, pl.ds(c * wide, wide)])
    for d in range(1, experts):
        for t in trades:
            t.drain(d)
    for copy in saves:
        copy.wait()


def run_front(sizes, experts, ins, chunks=4):
    tokens, qkv, rest, gu, dn = ins[0], ins[9], ins[10], ins[11], ins[12]
    length, width = tokens.shape
    n_dp = sizes[0] * sizes[1]
    capacity = 2 * length // (experts + 4)
    slots = experts * capacity
    bf, f4 = jnp.bfloat16, jnp.float32
    S, V = jax.ShapeDtypeStruct, pltpu.VMEM
    token = S((length, width), bf)
    gu_all, dn_all = (gu.shape[0] * n_dp, gu.shape[1]), (dn.shape[0] * n_dp, dn.shape[1])
    outs = [S(gu_all, bf), S(dn_all, bf)] + [S((a.shape[0] * n_dp, a.shape[1]), bf) for a in (qkv, rest)]
    outs += [token] * 6 + [S((length, width), f4), S((length, 128), f4), S((length, 128), f4), S((16, width), f4)]
    outs += [S((slots, width), bf)] * 2
    items = 4 + 2 * chunks
    dma = pltpu.SemaphoreType.DMA
    vmem = pl.BlockSpec(memory_space=pltpu.VMEM)
    hbm = pl.BlockSpec(memory_space=pl.ANY)
    send = V((experts - 1, capacity, width), bf)
    return pl.pallas_call(
        functools.partial(front_kernel, sizes, experts, chunks),
        out_shape=tuple(outs),
        in_specs=[vmem] * 13,
        out_specs=(hbm,) * len(outs),
        scratch_shapes=[V(o.shape, o.dtype) for o in outs[2:14]] + [
            V(gu_all, bf), V(dn_all, bf), V((slots, width), bf), V((slots, width), bf), V((width, slots), bf),
            V((slots, dn_all[0]), bf), V((slots, gu_all[1]), bf), V((slots, width), bf), V((slots, width), bf),
            V((8, length), f4), V((length, BLOCK + LONGEST), f4), V((2, length, width), bf), send, send,
            dma((5, items, n_dp)), dma((items, n_dp)), dma((2, n_dp)), dma((items + 16 + 3 * chunks,)),
            dma((2, 4, experts))],
        compiler_params=pltpu.CompilerParams(collective_id=1, has_side_effects=True, vmem_limit_bytes=63 << 20),
        name="front",
    )(*ins)


def add_into(view, more):
    view[...] = (view[...].astype(jnp.float32) + more[...].astype(jnp.float32)).astype(view.dtype)


class Reduce:
    def __init__(self, spot, number, view, one, two, sends, recv_one, recv_two, x_first):
        self.s, self.n, self.view, self.one, self.two = spot, number, view, one, two
        self.sends, self.recv_one, self.recv_two, self.x_first = sends, recv_one, recv_two, x_first
        if x_first:
            self.np, self.nq, self.p, self.q = spot.nx, spot.nz, spot.x, spot.z
        else:
            self.np, self.nq, self.p, self.q = spot.nz, spot.nx, spot.z, spot.x
        self.drains = []

    @staticmethod
    def slots(n):
        return 1 if n == 2 else n + 1

    @staticmethod
    def slot(n, place, above):
        if n == 2:
            return 0
        return jnp.where(above, n, place)

    def owner(self, p, q):
        return q * self.s.nx + p if self.x_first else p * self.s.nx + q

    def along(self, first, value):
        return self.s.device(x=value) if first == self.x_first else self.s.device(z=value)

    def push(self, cond, o, dst, recv, device):
        copy = pltpu.make_async_remote_copy(
            src_ref=self.view(o), dst_ref=dst, send_sem=self.sends.at[self.n, o], recv_sem=recv,
            device_id=device, device_id_type=MESH)
        pl.when(cond)(lambda: copy.start())
        self.drains.append(lambda: pl.when(cond)(lambda: copy.wait_send()))

    def take(self, cond, o, slot, recv):
        def run():
            pltpu.make_async_remote_copy(
                src_ref=slot, dst_ref=slot, send_sem=self.sends.at[self.n, o], recv_sem=recv,
                device_id=self.s.device(), device_id_type=MESH).wait_recv()
            add_into(self.view(o), slot)
        pl.when(cond)(run)

    def order(self):
        return sorted(range(-(self.nq - 1), self.nq), key=lambda d: (-abs(d), d))

    def phase_one(self):
        steps = []
        for turn in range(2):
            sign = jnp.where(self.p * 2 < self.np, 1, -1) * (1 if turn == 0 else -1)
            for k in range(self.np - 1, 0, -1):
                for dq in self.order():
                    def step(sign=sign, k=k, dq=dq):
                        p, q = self.p + sign * k, self.q + dq
                        here = jnp.logical_and(between(p, self.np), between(q, self.nq))
                        o = self.owner(p, q)
                        if self.np > 2:
                            behind = jnp.logical_and(here, between(self.p - sign, self.np))
                            self.take(behind, o, self.one.at[p, q], self.recv_one.at[self.n, p, q])
                        slot = self.slot(self.np, p, jnp.logical_and(k == 1, sign < 0))
                        self.push(here, o, self.one.at[slot, q], self.recv_one.at[self.n, slot, q],
                                  self.along(True, self.p + sign))
                    steps.append(step)
        return steps

    def settle(self, cond, q):
        o = self.owner(self.p, q)
        below = self.p > 0
        above = self.p < self.np - 1
        if cond is not None:
            below, above = jnp.logical_and(cond, below), jnp.logical_and(cond, above)
        for cond, top in ((below, False), (above, True)):
            slot = self.slot(self.np, self.p, top)
            self.take(cond, o, self.one.at[slot, q], self.recv_one.at[self.n, slot, q])

    def phase_two(self):
        steps = []
        for turn in range(2):
            sign = jnp.where(self.q * 2 < self.nq, 1, -1) * (1 if turn == 0 else -1)
            for k in range(self.nq - 1, 0, -1):
                def step(sign=sign, k=k):
                    q = self.q + sign * k
                    here = between(q, self.nq)
                    o = self.owner(self.p, q)
                    self.settle(here, q)
                    behind = jnp.logical_and(here, between(self.q - sign, self.nq))
                    if self.nq > 2:
                        self.take(behind, o, self.two.at[q], self.recv_two.at[self.n, q])
                    slot = self.slot(self.nq, q, jnp.logical_and(k == 1, sign < 0))
                    self.push(here, o, self.two.at[slot], self.recv_two.at[self.n, slot], self.along(False, self.q + sign))
                steps.append(step)
        return steps

    def finish(self, out):
        o = self.owner(self.p, self.q)
        self.settle(None, self.q)
        out[...] = self.view(o)[...].astype(jnp.float32)
        for cond, top in ((self.q > 0, False), (self.q < self.nq - 1, True)):
            def run(slot=self.slot(self.nq, self.q, top)):
                two = self.two.at[slot]
                pltpu.make_async_remote_copy(
                    src_ref=two, dst_ref=two, send_sem=self.sends.at[self.n, o], recv_sem=self.recv_two.at[self.n, slot],
                    device_id=self.s.device(), device_id_type=MESH).wait_recv()
                out[...] += two[...].astype(jnp.float32)
            pl.when(cond)(run)


def column_of(row):
    return jnp.transpose(jnp.broadcast_to(row, (128, row.shape[1])))


class Dense:
    def __init__(self, spot, number, own, bufs, sems, done):
        self.spot, self.n, self.own, self.done = spot, number, own, done
        self.mine, self.one, self.two, self.ybuf, self.final, self.other = bufs
        self.sends, self.recv_one, self.recv_two, self.mate, self.ys, self.outs = sems
        self.reduce = Reduce(spot, number, lambda o: self.mine.at[o], self.one, self.two, self.sends, self.recv_one,
                             self.recv_two, True)
        self.drains = []

    def swap(self):
        return pltpu.make_async_remote_copy(
            src_ref=self.own.at[1 - self.spot.core], dst_ref=self.mine, send_sem=self.mate.at[0, self.n],
            recv_sem=self.mate.at[1, self.n], device_id=self.spot.device(core=1 - self.spot.core), device_id_type=MESH)

    def begin(self):
        self.swap().start()

    def merge(self):
        self.swap().wait()
        def add(o, carry):
            add_into(self.mine.at[o], self.own.at[self.spot.core, o])
            return carry
        lax.fori_loop(0, self.mine.shape[0], add, 0)
        for step in self.reduce.phase_one():
            step()

    def across(self, d):
        y = lax.rem(self.spot.y + d, self.spot.ny)
        return pltpu.make_async_remote_copy(
            src_ref=self.ybuf.at[self.spot.y], dst_ref=self.ybuf.at[self.spot.y], send_sem=self.ys.at[0, self.n, d],
            recv_sem=self.ys.at[1, self.n, self.spot.y], device_id=self.spot.device(y=y), device_id_type=MESH)

    def settle(self):
        self.reduce.finish(self.final)
        self.ybuf[self.spot.y] = self.final[...].astype(self.ybuf.dtype)
        for d in range(1, self.spot.ny):
            copy = self.across(d)
            copy.start()
            self.drains.append(copy.wait_send)

    def hand(self):
        return pltpu.make_async_remote_copy(
            src_ref=self.final, dst_ref=self.other, send_sem=self.outs.at[0, self.n], recv_sem=self.outs.at[1, self.n],
            device_id=self.spot.device(core=1 - self.spot.core), device_id_type=MESH)

    def total(self):
        for d in range(1, self.spot.ny):
            y = lax.rem(self.spot.y + d, self.spot.ny)
            pltpu.make_async_remote_copy(
                src_ref=self.ybuf.at[y], dst_ref=self.ybuf.at[y], send_sem=self.ys.at[0, self.n, d],
                recv_sem=self.ys.at[1, self.n, y], device_id=self.spot.device(y=y), device_id_type=MESH).wait_recv()
        sum_ = self.ybuf[0].astype(jnp.float32)
        for y in range(1, self.spot.ny):
            sum_ = sum_ + self.ybuf[y].astype(jnp.float32)
        self.final[...] = sum_
        self.hand().start()

    def end(self):
        self.hand().wait()
        for half in range(2):
            pl.when(self.spot.core == half)(lambda half=half: self.done(half, self.final[...]))
            pl.when(self.spot.core != half)(lambda half=half: self.done(half, self.other[...]))

    def steps(self):
        return [self.merge] + self.reduce.phase_two() + [self.settle, self.total, self.end]


class Tail:
    def __init__(self, spot, experts, r):
        self.spot, self.experts, self.r = spot, experts, r
        self.length, self.width = r.cot.shape
        self.blocks = self.length // BLOCK
        self.pairs = self.width // 128

    def prepare(self):
        r, n = self.r, self.length
        r.lse_rows[...] = jnp.transpose(r.lse[...])[: r.lse_rows.shape[0]]
        segment = r.segments[...].astype(jnp.float32)
        seg_col = column_of(segment)[:, 0:1]
        pad_col = column_of(r.padding[...].astype(jnp.float32))[:, 0:1]
        at = 0
        for i in range(self.blocks):
            k0, k1 = key_range(i)
            key = lax.broadcasted_iota(jnp.int32, (k1 - k0, BLOCK), 0) + k0
            query = lax.broadcasted_iota(jnp.int32, (k1 - k0, BLOCK), 1) + i * BLOCK
            same = seg_col[k0:k1] == segment[:, i * BLOCK : (i + 1) * BLOCK]
            fine = jnp.logical_and(jnp.logical_and(key <= query, same),
                                   jnp.logical_or(pad_col[k0:k1] == 1.0, key == query))
            r.bias[pl.ds(at, k1 - k0)] = jnp.where(fine, 0.0, -1e30).astype(jnp.bfloat16)
            at += k1 - k0
        r.gain_rows[...] = jnp.zeros(r.gain_rows.shape, jnp.float32)

    def combine(self, i):
        r, w, e = self.r, self.width, self.experts
        rows = pl.ds(i * BLOCK, BLOCK)
        col = lambda j: r.scal[rows, j : j + 1]
        slot = lax.broadcasted_iota(jnp.int32, (BLOCK, r.y.shape[0]), 1).astype(jnp.float32)
        at = [jnp.where(col(8 + k) == slot, 1.0, 0.0).astype(jnp.bfloat16) for k in range(2)]
        pair = [dot(at[k], r.y[...]) for k in range(2)]
        routed = dot(at[0] + at[1], r.dx[...])
        cot, hn = r.cot[rows].astype(jnp.float32), r.hn[rows].astype(jnp.float32)
        h = r.tg[rows]
        gates, mix = [col(2), col(3)], [[col(4), col(5)], [col(6), col(7)]]
        route = [col(14 + k) for k in range(2)]
        one = lambda c: jnp.where(c, 1.0, 0.0)
        fixed = [[one(route[k] == e + 2 + j) for j in range(2)] for k in range(2)]
        share = [one(route[k] == e + 1) + fixed[k][0] * mix[0][0] + fixed[k][1] * mix[1][0] for k in range(2)]
        copy = gates[0] * share[0] + gates[1] * share[1]
        chosen = [gates[0] * fixed[0][j] + gates[1] * fixed[1][j] for j in range(2)]
        coef = [chosen[j] * mix[j][1] for j in range(2)]
        const = [r.rows[6 + j : 7 + j] for j in range(2)]
        branch = gates[0] * pair[0] + gates[1] * pair[1] + copy * hn + (coef[0] * const[0] + coef[1] * const[1])
        r.layer_out[rows] = (h + branch).astype(jnp.bfloat16)
        total = lambda v: jnp.sum(v, axis=1, keepdims=True)
        with_hn = total(cot * hn)
        with_const = [total(cot * const[j]) for j in range(2)]
        grads = [total(cot * pair[k]) + share[k] * with_hn
                 + fixed[k][0] * mix[0][1] * with_const[0] + fixed[k][1] * mix[1][1] * with_const[1] for k in range(2)]
        mean = gates[0] * grads[0] + gates[1] * grads[1]
        picked = [gates[k] * (grads[k] - mean) for k in range(2)]
        lane = lax.broadcasted_iota(jnp.int32, (BLOCK, r.prev_grad.shape[1]), 1).astype(jnp.float32)
        r.prev_grad[rows] = jnp.where(lane == route[0], picked[0], 0.0) + jnp.where(lane == route[1], picked[1], 0.0)
        lane = lax.broadcasted_iota(jnp.int32, (BLOCK, 128), 1).astype(jnp.float32)
        low = jnp.where(lane == route[0] + 8, picked[0], 0.0) + jnp.where(lane == route[1] + 8, picked[1], 0.0)
        for j in range(2):
            g = [chosen[j] * with_hn, chosen[j] * with_const[j]]
            m = mix[j][0] * g[0] + mix[j][1] * g[1]
            for q in range(2):
                low = jnp.where(lane == 2 + 2 * j + q, mix[j][q] * (g[q] - m), low)
        low = low.astype(jnp.bfloat16)
        r.low[rows] = low
        high = [c.astype(jnp.bfloat16).astype(jnp.float32) for c in coef]
        both = jnp.zeros(lane.shape, jnp.float32)
        for j in range(2):
            both = jnp.where(lane == 6 + j, high[j], jnp.where(lane == 70 + j, coef[j] - high[j], both))
        r.coef[rows] = both.astype(jnp.bfloat16)
        grad = routed + copy * cot + dot(low, r.rest[:, pl.ds(w, 128)], 1, 1)
        dh = cot + self.unnorm(grad, h, col(1), 1)
        r.tg[rows] = dh
        dh = dh.astype(jnp.bfloat16)
        r.dh[rows] = dh

    def unnorm(self, grad, v, inverse, gain):
        r = self.r
        scaled = r.rows[gain : gain + 1] * grad
        mean = jnp.sum(scaled * v, axis=1, keepdims=True) / v.shape[1]
        r.gain_rows[gain : gain + 1] += jnp.sum(grad * v * inverse, axis=0, keepdims=True)
        return inverse * scaled - v * (inverse * inverse * inverse * mean)

    def unproject(self, i):
        r = self.r
        rows = pl.ds(i * BLOCK, BLOCK)
        r.ag[rows] = dot(r.dh[rows], r.rest[:, pl.ds(0, self.width)], 1, 1).astype(jnp.bfloat16)

    def blocked(self, v):
        n = self.spot.nz * self.spot.nx
        return v.reshape(n, v.shape[0] // n, v.shape[1])

    def out_grad(self):
        r = self.r
        half = self.width // 2
        for c in range(2):
            g = dot(r.attended[...], r.dh[:, pl.ds(c * half, half)], 0, 0)
            r.own[self.pairs // 2, c] = self.blocked(g).astype(jnp.bfloat16)

    def small_grad(self):
        r = self.r
        g = dot(r.cot[...], r.coef[...], 0, 0)
        lane = lax.broadcasted_iota(jnp.int32, g.shape, 1)
        g = jnp.where(lane < 64, g + pltpu.roll(g, 64, 1), 0.0) + dot(r.hn[...], r.low[...], 0, 0)
        r.own_small[0] = self.blocked(g).astype(jnp.bfloat16)
        r.own_small[1] = jnp.zeros(r.own_small.shape[1:], jnp.bfloat16)

    def small_end(self):
        r = self.r
        g = r.own_small[0].astype(jnp.float32)
        lane = lax.broadcasted_iota(jnp.int32, g.shape, 2)
        for j in range(2):
            g = jnp.where(lane == j, self.blocked(column_of(r.gain_rows[j : j + 1])), g)
        r.own_small[0] = g.astype(jnp.bfloat16)

    def normed_side(self):
        self.r.nt[...] = jnp.transpose(self.r.normed[...])

    def pair_begin(self, pair):
        r = self.r
        r.kt[...] = jnp.transpose(r.k[:, pl.ds(pair * 128, 128)])
        r.dk[...] = jnp.zeros(r.dk.shape, jnp.float32)
        r.dv[...] = jnp.zeros(r.dv.shape, jnp.float32)

    def attend(self, pair, i):
        r = self.r
        k0, k1 = key_range(i)
        at = sum(key_range(j)[1] - key_range(j)[0] for j in range(i))
        rows, keys, lanes = pl.ds(i * BLOCK, BLOCK), pl.ds(k0, k1 - k0), pl.ds(pair * 128, 128)
        q, k, v, g = r.q[rows, lanes], r.k[keys, lanes], r.v[keys, lanes], r.ag[rows, lanes]
        bias = r.bias[pl.ds(at, k1 - k0)].astype(jnp.float32)
        dq = []
        for s, mask in enumerate(head_masks()):
            qs, gs = q * mask, g * mask
            head = 2 * pair + s
            probs = jnp.exp(dot(k, qs, 1, 1) + bias - r.lse_rows[head : head + 1, rows])
            grad = dot(v, gs, 1, 1)
            mean = jnp.sum(probs * grad, axis=0, keepdims=True)
            ds = (probs * (grad - mean)).astype(jnp.bfloat16)
            r.dv[keys] += dot(probs.astype(jnp.bfloat16), gs)
            r.dk[keys] += dot(ds, qs)
            dq.append(dot(r.kt[pl.ds(s * HEAD_DIM, HEAD_DIM), keys], ds))
        r.dq[rows] = jnp.transpose(jnp.concatenate(dq, axis=0))

    def pair_end(self, pair):
        r = self.r
        lanes = pl.ds(pair * 128, 128)
        cosine, sine = r.cosine[...], r.sine[...]
        dq = r.dq[...] * HEAD_DIM ** (-0.5)
        dk = r.dk[...]
        dq = (dq * cosine - swap_halves(dq) * sine).astype(jnp.bfloat16)
        dk = (dk * cosine - swap_halves(dk) * sine).astype(jnp.bfloat16)
        dv = r.dv[...].astype(jnp.bfloat16)
        r.q[:, lanes], r.k[:, lanes], r.v[:, lanes] = dq, dk, dv
        half = self.pairs // 2
        for part, d in enumerate((dq, dk, dv)):
            g = dot(r.nt[...], d)
            r.own[pair % half, pair // half, :, :, pl.ds(part * 128, 128)] = self.blocked(g).astype(jnp.bfloat16)

    def last(self, i):
        r, w = self.r, self.width
        rows = pl.ds(i * BLOCK, BLOCK)
        grad = (dot(r.q[rows], r.qkv[:, pl.ds(0, w)], 1, 1) + dot(r.k[rows], r.qkv[:, pl.ds(w, w)], 1, 1)
                + dot(r.v[rows], r.qkv[:, pl.ds(2 * w, w)], 1, 1))
        x = r.tokens[rows].astype(jnp.float32)
        r.tg[rows] += self.unnorm(grad, x, r.scal[rows, 0:1], 0)


class TailIns(NamedTuple):
    gu_hbm: object
    dn_hbm: object
    y_hbm: object
    dx_hbm: object
    h_hbm: object
    attended_hbm: object
    normed_hbm: object
    q_hbm: object
    k_hbm: object
    v_hbm: object
    hn_hbm: object
    tokens_hbm: object
    lse_hbm: object
    cot_hbm: object
    qkv_hbm: object
    rest_hbm: object
    scal_hbm: object
    rows_hbm: object
    segments: object
    padding: object
    cosine: object
    sine: object


class TailOuts(NamedTuple):
    layer_hbm: object
    gu_hbm_out: object
    dn_hbm_out: object
    tg: object
    prev_grad: object
    qkv_out: object
    out_out: object
    small_out: object


def expert_items(spot, chunks, r):
    wide, half = r.gu_src.shape[2] // chunks, r.dn_src.shape[1] // 2
    items, outs = [], []
    for p, xf in ((0, True), (1, False)):
        one, two = (r.d1a, r.d2a) if p == 0 else (r.d1b, r.d2b)
        items.append(Reduce(spot, p, lambda o, p=p: r.dn_src.at[o, pl.ds(p * half, half)], one, two,
                            r.e_sends, r.e_r1, r.e_r2, xf))
        outs.append((r.dn_out, r.dn_hbm_out.at[pl.ds(p * half, half)]))
    for c in range(chunks):
        cut = pl.ds(c * wide, wide)
        items.append(Reduce(spot, 2 + c, lambda o, cut=cut: r.gu_src.at[o, :, cut], r.g1.at[c], r.g2.at[c],
                            r.e_sends, r.e_r1, r.e_r2, True))
        outs.append((r.gu_out, r.gu_hbm_out.at[:, cut]))
    stored = {}
    def finish(n):
        stage, out = outs[n]
        kind = min(n, 2) // 2
        if kind in stored:
            stored[kind].wait()
        items[n].finish(stage)
        stored[kind] = pltpu.make_async_copy(stage, out, r.local.at[kind])
        stored[kind].start()
    lists = [item.phase_two() for item in items]
    events = []
    for n in range(len(items) + 1):
        if n < len(items):
            events += lists[n][: len(lists[n]) // 2]
        if n > 0:
            events += lists[n - 1][len(lists[n - 1]) // 2 :]
        if n > 1:
            events.append(functools.partial(finish, n - 2))
    events.append(functools.partial(finish, len(items) - 1))
    return items, events, stored


class ExpertIns(NamedTuple):
    gu_hbm: object
    dn_hbm: object


class ExpertOuts(NamedTuple):
    gu_hbm_out: object
    dn_hbm_out: object


class ExpertScratch(NamedTuple):
    gu_src: object
    dn_src: object
    gu_out: object
    dn_out: object
    g1: object
    g2: object
    d1a: object
    d2a: object
    d1b: object
    d2b: object
    e_sends: object
    e_r1: object
    e_r2: object
    local: object


def load_experts(chunks, r):
    loads = [pltpu.make_async_copy(r.dn_hbm, r.dn_src, r.local.at[3])]
    wide = r.gu_src.shape[2] // chunks
    for c in range(chunks):
        cut = pl.ds(c * wide, wide)
        loads.append(pltpu.make_async_copy(r.gu_hbm.at[:, :, cut], r.gu_src.at[:, :, cut], r.local.at[4 + c]))
    for l in loads:
        l.start()
    return loads


def start_experts(items, loads):
    for n, item in enumerate(items):
        if n != 1:
            loads[max(n - 1, 0)].wait()
        for step in item.phase_one():
            step()


def expert_kernel(sizes, chunks, *refs):
    r = SimpleNamespace(**dict(zip(ExpertIns._fields + ExpertOuts._fields + ExpertScratch._fields, refs)))
    spot = Spot(sizes)
    loads = load_experts(chunks, r)
    enter(spot, line_neighbours(spot))
    items, events, stored = expert_items(spot, chunks, r)
    start_experts(items, loads)
    for event in events:
        event()
    for copy in stored.values():
        copy.wait()
    for item in items:
        for drain in item.drains:
            drain()


def expert_scratch(sizes, gu, dn, chunks):
    nz, nx = sizes[:2]
    n_dp, big = nz * nx, max(nz, nx)
    bf, f4 = jnp.bfloat16, jnp.float32
    V, dma = pltpu.VMEM, pltpu.SemaphoreType.DMA
    rows, rows_d, width = gu.shape[1], dn.shape[1], dn.shape[2]
    wide, tall = gu.shape[2] // chunks, rows_d // 2
    sx, sz = Reduce.slots(nx), Reduce.slots(nz)
    items = 2 + chunks
    out = dict(gu_src=V(gu.shape, bf), dn_src=V(dn.shape, bf), gu_out=V((rows, wide), f4), dn_out=V((tall, width), f4),
               g1=V((chunks, sx, nz, rows, wide), bf), g2=V((chunks, sz, rows, wide), bf),
               d1a=V((sx, nz, tall, width), bf), d2a=V((sz, tall, width), bf),
               d1b=V((sz, nx, tall, width), bf), d2b=V((sx, tall, width), bf),
               e_sends=dma((items, n_dp)), e_r1=dma((items, big + 1, big)), e_r2=dma((items, big + 1)))
    shapes = (jax.ShapeDtypeStruct((rows, gu.shape[2]), f4), jax.ShapeDtypeStruct((rows_d, width), f4))
    return out, shapes


def reduce_experts(sizes, gu, dn, chunks=4):
    scratch, shapes = expert_scratch(sizes, gu, dn, chunks)
    scratch["local"] = pltpu.SemaphoreType.DMA((4 + chunks,))
    hbm = pl.BlockSpec(memory_space=pl.ANY)
    return pl.pallas_call(
        functools.partial(expert_kernel, sizes, chunks),
        out_shape=shapes, in_specs=[hbm] * 2, out_specs=(hbm,) * 2,
        scratch_shapes=[scratch[n] for n in ExpertScratch._fields],
        compiler_params=pltpu.CompilerParams(collective_id=3, has_side_effects=True, vmem_limit_bytes=60 << 20),
        name="experts",
    )(gu, dn)


def tail_kernel(sizes, experts, chunks, together, names, *refs):
    r = SimpleNamespace(**dict(zip(names, refs)))
    first = pl.ds(0, r.cot.shape[0])
    r.ag, r.dh, r.normed = r.y.at[first], r.ag_, r.dx.at[first]
    r.attended = r.nt = r.layer_out
    r.tokens, r.lse = r.hn, r.dq
    spot = Spot(sizes)
    tail = Tail(spot, experts, r)
    loads = {}
    def load(src, dst):
        copy = pltpu.make_async_copy(src, dst, r.local.at[4 + chunks + len(loads)])
        copy.start()
        loads[id(dst)] = copy
        return copy
    if together:
        loads_e = load_experts(chunks, r)
    capacity = r.y.shape[0] // experts
    own = slots_of(r.y_hbm, capacity), slots_of(r.dx_hbm, capacity)
    mine = slots_of(r.y, capacity)(spot.ex), slots_of(r.dx, capacity)(spot.ex)
    firsts = [load(own[n](spot.ex), mine[n]) for n in range(2)]
    firsts += [load(*p) for p in ((r.lse_hbm, r.lse), (r.h_hbm, r.tg), (r.hn_hbm, r.hn), (r.cot_hbm, r.cot),
                                  (r.rest_hbm, r.rest), (r.scal_hbm, r.scal), (r.rows_hbm, r.rows))]
    seconds = [load(*p) for p in ((r.q_hbm, r.q), (r.k_hbm, r.k), (r.v_hbm, r.v), (r.qkv_hbm, r.qkv))]
    enter(spot, line_neighbours(spot)
          + [(None, expert_device(spot, lax.rem(spot.ex + d, experts))) for d in range(1, experts)])
    target = lambda at: lambda d: at(lax.rem(spot.ex + d, experts))
    returns = [Exchange(spot, experts, n, target(own[n]), slots_of(into, capacity), r.trade)
               for n, into in enumerate((r.y, r.dx))]
    for t in returns:
        for d in range(1, experts):
            t.send(d)
    items, events, stored = [], [], {}
    if together:
        items, events, stored = expert_items(spot, chunks, r)
        start_experts(items, loads_e)
    sems = (r.sends, r.r1, r.r2, r.mates, r.ys, r.outs)
    dense = []
    rounds = tail.pairs // 2
    for j in range(rounds + 1):
        def done(h, v, j=j):
            if j == rounds:
                r.out_out[:, pl.ds(h * v.shape[1], v.shape[1])] = v
            else:
                for part in range(3):
                    cols = pl.ds(part * tail.width + (h * rounds + j) * 128, 128)
                    r.qkv_out[:, cols] = v[:, part * 128 : part * 128 + 128]
        bufs = [b.at[j] for b in (r.mine, r.one, r.two, r.ybuf, r.final, r.other)]
        dense.append(Dense(spot, j, r.own.at[j], bufs, sems, done))
    def done(h, v):
        r.small_out[:, pl.ds(h * 128, 128)] = v
    bufs = [r.mine_s, r.one_s, r.two_s, r.ybuf_s, r.final_s, r.other_s]
    dense.append(Dense(spot, rounds + 1, r.own_small, bufs, sems, done))
    part = functools.partial
    def arrived():
        for copy in firsts:
            copy.wait()
    def returned():
        for t in returns:
            for d in range(1, experts):
                t.receive(d)
    work = [arrived, tail.prepare, returned]
    work += [part(tail.combine, i) for i in range(tail.blocks)]
    thirds = []
    def load_more():
        seconds.append(load(r.normed_hbm, r.normed))
        copy = pltpu.make_async_copy(r.layer_out, r.layer_hbm, r.local.at[2])
        copy.start()
        copy.wait()
        thirds.append(load(r.attended_hbm, r.attended))
    work.append(load_more)
    work += [part(tail.unproject, i) for i in range(tail.blocks)]
    def outs_of():
        thirds.pop().wait()
        tail.out_grad()
        dense[rounds].begin()
    work.append(outs_of)
    def smalls():
        tail.small_grad()
        thirds.append(load(r.tokens_hbm, r.tokens))
    work.append(smalls)
    def ready():
        for copy in seconds:
            copy.wait()
        tail.normed_side()
    work.append(ready)
    later = {0: [dense[rounds].merge], }
    for j in range(rounds):
        for pair in (j, rounds + j):
            work.append(part(tail.pair_begin, pair))
            work += [part(tail.attend, pair, i) for i in range(tail.blocks)]
            work.append(part(tail.pair_end, pair))
        work.append(dense[j].begin)
        if j < rounds - 1:
            work.append(dense[j].merge)
        if j == 0:
            work.append(dense[rounds].merge)
    woven(work, events[: len(events) * EARLY // 8])
    rest = events[len(events) * EARLY // 8 :]
    thirds.pop().wait()
    woven([dense[rounds - 1].merge] + [part(tail.last, i) for i in range(tail.blocks)] + [tail.small_end, dense[-1].begin, dense[-1].merge], rest)
    stages = [d.steps()[1:] for d in dense]
    for level in range(max(map(len, stages))):
        for st in stages:
            if level < len(st):
                st[level]()
    for copy in stored.values():
        copy.wait()
    for t in returns:
        for d in range(1, experts):
            t.drain(d)
    for item in items + dense + [d.reduce for d in dense]:
        for drain in item.drains:
            drain()


def run_tail(sizes, experts, ins, routes_width, chunks=4):
    by = TailIns(*ins)
    nz, nx, ny = sizes[:3]
    n_dp = nz * nx
    length, width = by.cot_hbm.shape
    rows = by.gu_hbm.shape[1]
    slots = by.y_hbm.shape[0]
    assert length == width
    together = n_dp <= 8
    bf, f4 = jnp.bfloat16, jnp.float32
    S, V, dma = jax.ShapeDtypeStruct, pltpu.VMEM, pltpu.SemaphoreType.DMA
    e_scratch, e_shapes = expert_scratch(sizes, by.gu_hbm, by.dn_hbm, chunks)
    shapes = dict(layer_hbm=S((length, width), bf), tg=S((length, width), f4), prev_grad=S((length, routes_width), f4),
                  qkv_out=S((rows, 3 * width), f4), out_out=S((rows, width), f4), small_out=S((rows, 256), f4))
    shapes.update(zip(ExpertOuts._fields, e_shapes))
    kinds = width // 256 + 1
    token, back, pair = V((length, width), bf), V((slots, width), bf), V((length, 128), f4)
    keys = sum(key_range(i)[1] - key_range(i)[0] for i in range(length // BLOCK))
    sx, sz = Reduce.slots(nx), Reduce.slots(nz)
    big = max(nz, nx)
    def buffers(end, lead, cols):
        block = (rows, cols)
        sizes_ = ((n_dp,), (sx, nz), (sz,), (ny,), (), ())
        names = ("mine", "one", "two", "ybuf", "final", "other")
        return {n + end: V(lead + s + block, f4 if j > 3 else bf) for j, (n, s) in enumerate(zip(names, sizes_))}
    scratch = dict(y=back, dx=back, ag_=token, hn=token, q=token, k=token, v=token, layer_out=token,
                   low=V((length, 128), bf), coef=V((length, 128), bf), gain_rows=V((8, width), f4),
                   lse_rows=V((16, length), f4), bias=V((keys, BLOCK), bf), kt=V((128, length), bf), dq=pair, dk=pair,
                   dv=pair, own=V((kinds, 2, n_dp, rows, width // 2), bf), own_small=V((2, n_dp, rows, 128), bf),
                   cot=token, qkv=V(by.qkv_hbm.shape, bf), rest=V(by.rest_hbm.shape, bf), scal=pair,
                   rows=V(by.rows_hbm.shape, f4), trade=dma((2, 2, experts)))
    scratch.update(buffers("", (kinds,), width // 2))
    scratch.update(buffers("_s", (), 128))
    scratch.update(sends=dma((kinds + 1, n_dp)), r1=dma((kinds + 1, big + 1, big)), r2=dma((kinds + 1, big + 1)),
                   mates=dma((2, kinds + 1)), ys=dma((2, kinds + 1, ny)), outs=dma((2, kinds + 1)), local=dma((24 + chunks,)))
    if together:
        scratch.update(e_scratch)
    in_names = [n for n in TailIns._fields if together or n not in ExpertIns._fields]
    out_names = [n for n in TailOuts._fields if together or n not in ExpertOuts._fields]
    vmem = pl.BlockSpec(memory_space=pltpu.VMEM)
    hbm = pl.BlockSpec(memory_space=pl.ANY)
    place = lambda names: [hbm if "hbm" in n else vmem for n in names]
    outs = pl.pallas_call(
        functools.partial(tail_kernel, sizes, experts, chunks, together, in_names + out_names + list(scratch)),
        out_shape=tuple(shapes[n] for n in out_names),
        in_specs=place(in_names),
        out_specs=tuple(place(out_names)),
        scratch_shapes=list(scratch.values()),
        compiler_params=pltpu.CompilerParams(collective_id=2, has_side_effects=True, vmem_limit_bytes=67_000_000),
        name="tail",
    )(*(getattr(by, n) for n in in_names))
    out = dict(zip(out_names, outs))
    if not together:
        out.update(zip(ExpertOuts._fields, reduce_experts(sizes, by.gu_hbm, by.dn_hbm, chunks)))
    return [out[n] for n in TailOuts._fields]


def pair_tables(length):
    half = HEAD_DIM // 2
    inverse = np.float32(10000.0) ** (-(np.arange(half, dtype=np.float32) / np.float32(half)))
    angles = (np.arange(length, dtype=np.float32)[:, None] * inverse[None]).astype(np.float64)
    cosine, sine = np.cos(angles).astype(np.float32), np.sin(angles).astype(np.float32)
    return jnp.asarray(np.tile(cosine, (1, 4))), jnp.asarray(np.tile(np.concatenate([-sine, sine], 1), (1, 2)))


def per_device(
    sizes,
    tokens,
    prev_logits,
    segment_ids,
    pad_mask,
    routes,
    slot_order,
    cotangent,
    attn_gain,
    qkv_weight,
    out_weight,
    ffn_gain,
    router_weight,
    mix_weight,
    const_weight,
    gate_up_weight,
    down_weight,
):
    length, width = tokens.shape
    experts = lax.axis_size("expert") * gate_up_weight.shape[0]
    choices = router_weight.shape[1]
    n_dp = sizes[0] * sizes[1]
    small = jnp.concatenate(
        [attn_gain[:, None], ffn_gain[:, None], mix_weight, const_weight, router_weight], axis=1
    )
    rest = jnp.concatenate([out_weight, jnp.pad(small, ((0, 0), (0, 256 - small.shape[1])))], axis=1)
    cosine, sine = pair_tables(length)
    pairs = routes[0]
    f = FrontOuts(*run_front(
        sizes, experts,
        (tokens, prev_logits, segment_ids, pad_mask, pairs, slot_order.reshape(length, 2), cotangent,
         cosine, sine, qkv_weight, rest, gate_up_weight[0], down_weight[0])))
    by_owner = lambda g: g.reshape(n_dp, g.shape[0] // n_dp, g.shape[1])
    layer_out, gu_shard, dn_shard, tokens_grad, prev_grad, qkv_grad, out_grad, small_grad = run_tail(
        sizes, experts,
        (by_owner(f.gu_grad), by_owner(f.dn_grad), f.y_hbm, f.dx_hbm, f.h_hbm, f.attended_hbm, f.normed_hbm, f.q_hbm, f.k_hbm,
         f.v_hbm, f.hn_hbm, tokens, f.lse_hbm, cotangent, f.qkv_hbm, f.rest_hbm, f.scal_hbm, f.rows_hbm, segment_ids,
         pad_mask, cosine, sine), choices)
    return (
        layer_out,
        tokens_grad,
        prev_grad,
        small_grad[:, 0],
        qkv_grad,
        out_grad,
        small_grad[:, 1],
        small_grad[:, 8 : 8 + choices],
        small_grad[:, 2:6],
        small_grad[:, 6:8],
        gu_shard[None],
        dn_shard[None],
    )


def grid_sizes(mesh):
    along_dp, along_expert = mesh.devices[:, 0], mesh.devices[0]
    nx = len({d.coords[0] for d in along_dp})
    ny = len({d.coords[1] for d in along_expert})
    return (len(along_dp) // nx, nx, ny, len(along_expert) // ny)


def solution(mesh):
    in_specs = (
        P(("dp", "expert"), None),
        P(("dp", "expert"), None),
        P(("dp", "expert"), None),
        P(("dp", "expert"), None),
        P(("dp", "expert"), None, None),
        P(("dp", "expert"), None),
        P(("dp", "expert"), None),
        P("dp"),
        P("dp", None),
        P("dp", None),
        P("dp"),
        P("dp", None),
        P("dp", None),
        P("dp", None),
        P("expert", "dp", None),
        P("expert", "dp", None),
    )
    out_specs = (
        P(("dp", "expert"), None),
        P(("dp", "expert"), None),
        P(("dp", "expert"), None),
        P("dp"),
        P("dp", None),
        P("dp", None),
        P("dp"),
        P("dp", None),
        P("dp", None),
        P("dp", None),
        P("expert", "dp", None),
        P("expert", "dp", None),
    )
    return jax.shard_map(
        functools.partial(per_device, grid_sizes(mesh)), mesh=mesh, in_specs=in_specs, out_specs=out_specs, check_vma=False
    )
```

```python
import functools
from types import SimpleNamespace
from typing import NamedTuple

import jax
import jax.numpy as jnp
from jax import lax
from jax.experimental import pallas as pl
from jax.experimental.pallas import tpu as pltpu
import numpy as np
from jax.sharding import PartitionSpec as P

HEAD_DIM = 64
BLOCK = 256
LONGEST = 384
LEVEL_STEP = 2.5
LEAD = 4.0
FIRST, EACH, LEVEL_GAP, PAIR, DENSE_EACH, HOP = 8.0, 17.0, 7.0, 8.0, 6.0, 4.0
SHARE = 7
epsilon = 1e-06


MESH = pl.DeviceIdType.MESH


class Spot:
    def __init__(self, sizes):
        self.nz, self.nx, self.ny, self.nc = sizes
        self.dp, self.ex = lax.axis_index("dp"), lax.axis_index("expert")
        self.z, self.x = lax.div(self.dp, self.nx), lax.rem(self.dp, self.nx)
        self.y, self.core = lax.div(self.ex, self.nc), lax.rem(self.ex, self.nc)

    def device(self, z=None, x=None, y=None, core=None):
        z, x = self.z if z is None else z, self.x if x is None else x
        y, core = self.y if y is None else y, self.core if core is None else core
        return {"dp": z * self.nx + x, "expert": y * self.nc + core}


def between(value, size):
    return jnp.logical_and(value >= 0, value < size)


class Flood:
    def __init__(self, spot, number, own, view, sends, recvs, z_first, mate=None):
        self.s, self.n, self.own, self.view = spot, number, own, view
        self.sends, self.recvs, self.z_first, self.mate = sends, recvs, z_first, mate
        if z_first:
            self.na, self.nb, self.a, self.b = spot.nz, spot.nx, spot.z, spot.x
        else:
            self.na, self.nb, self.a, self.b = spot.nx, spot.nz, spot.x, spot.z
        self.drains = []

    def origin(self, a, b):
        return a * self.s.nx + b if self.z_first else b * self.s.nx + a

    def along(self, which, value):
        zed = (which == 0) == self.z_first
        return self.s.device(z=value) if zed else self.s.device(x=value)

    def push(self, cond, src, o, way, device, recvs=None):
        copy = pltpu.make_async_remote_copy(
            src_ref=src, dst_ref=self.view(o),
            send_sem=self.sends.at[way, self.n, o],
            recv_sem=(self.recvs if recvs is None else recvs).at[self.n, o],
            device_id=device, device_id_type=MESH)
        if cond is None:
            copy.start()
            self.drains.append(copy.wait_send)
        else:
            pl.when(cond)(lambda: copy.start())
            self.drains.append(lambda: pl.when(cond)(lambda: copy.wait_send()))

    def share(self, cond, src, o):
        if self.mate is not None:
            self.push(cond, src, o, 4, self.s.device(core=1 - self.s.core), self.mate)

    def mates(self, view):
        def one(o, carry):
            pltpu.make_async_remote_copy(
                src_ref=view(o), dst_ref=view(o), send_sem=self.sends.at[0, self.n, o], recv_sem=self.mate.at[self.n, o],
                device_id=self.s.device(), device_id_type=MESH).wait_recv()
            return carry
        lax.fori_loop(0, self.s.nz * self.s.nx, one, 0)

    def arrive(self, o):
        pltpu.make_async_remote_copy(
            src_ref=self.view(o), dst_ref=self.view(o),
            send_sem=self.sends.at[0, self.n, o], recv_sem=self.recvs.at[self.n, o],
            device_id=self.s.device(), device_id_type=MESH).wait_recv()

    def second(self, cond, src, o):
        for j, sign in enumerate((1, -1)):
            to = self.b + sign
            if self.nb > 1:
                ok = between(to, self.nb)
                self.push(ok if cond is None else jnp.logical_and(cond, ok), src, o, 2 + j, self.along(1, to))

    def levels(self):
        out = [[] for _ in range(self.na + self.nb - 1)]

        def begin():
            o = self.origin(self.a, self.b)
            for j, sign in enumerate((1, -1)):
                if self.na > 1:
                    self.push(between(self.a + sign, self.na), self.own, o, j, self.along(0, self.a + sign))
            self.second(None, self.own, o)
            self.share(None, self.own, o)

        out[0].append(begin)
        for k in range(1, self.na):
            for j, sign in enumerate((1, -1)):
                def step(k=k, j=j, sign=sign):
                    a = self.a - sign * k
                    here = between(a, self.na)
                    o = self.origin(a, self.b)
                    pl.when(here)(lambda: self.arrive(o))
                    on = jnp.logical_and(here, between(self.a + sign, self.na))
                    if self.na > 2 or k == 0:
                        self.push(on, self.view(o), o, j, self.along(0, self.a + sign))
                    self.second(here, self.view(o), o)
                    self.share(here, self.view(o), o)
                out[k].append(step)
        for d in range(1, self.nb):
            for da in range(-(self.na - 1), self.na):
                for j, sign in enumerate((1, -1)):
                    def step(d=d, da=da, j=j, sign=sign):
                        a, b = self.a + da, self.b - sign * d
                        here = jnp.logical_and(between(a, self.na), between(b, self.nb))
                        o = self.origin(a, b)
                        pl.when(here)(lambda: self.arrive(o))
                        if self.nb > 2:
                            on = jnp.logical_and(here, between(self.b + sign, self.nb))
                            self.push(on, self.view(o), o, 2 + j, self.along(1, self.b + sign))
                        self.share(here, self.view(o), o)
                    out[abs(da) + d].append(step)
        return out


def enter(spot, devices):
    barrier = pltpu.get_barrier_semaphore()
    count = jnp.int32(0)
    for cond, device in devices:
        def hail(device=device):
            pl.semaphore_signal(barrier, inc=1, device_id=device, device_id_type=MESH)
        if cond is None:
            hail()
            count = count + 1
        else:
            pl.when(cond)(hail)
            count = count + cond.astype(jnp.int32)
    pl.semaphore_wait(barrier, count)


def line_neighbours(spot):
    out = []
    for sign in (1, -1):
        out.append((between(spot.z + sign, spot.nz), spot.device(z=spot.z + sign)))
        out.append((between(spot.x + sign, spot.nx), spot.device(x=spot.x + sign)))
    return out


def dot(a, b, ca=1, cb=0):
    return lax.dot_general(a, b, (((ca,), (cb,)), ((), ())), preferred_element_type=jnp.float32)


def turned(columns):
    eye = lax.broadcasted_iota(jnp.int32, (128, 128), 0) == lax.broadcasted_iota(jnp.int32, (128, 128), 1)
    return dot(jnp.where(eye, 1.0, 0.0).astype(jnp.bfloat16), columns, 1, 1)


def spread(columns):
    lane = lax.broadcasted_iota(jnp.int32, (columns[0].shape[0], 128), 1)
    out = jnp.zeros(lane.shape, jnp.float32)
    for j, c in enumerate(columns):
        out = jnp.where(lane == j, c, out)
    return out


def swap_halves(v):
    half = HEAD_DIM // 2
    lane = lax.broadcasted_iota(jnp.int32, v.shape, 1)
    return jnp.where(lax.rem(lane, HEAD_DIM) < half, pltpu.roll(v, v.shape[1] - half, 1), pltpu.roll(v, half, 1))


def head_masks():
    lane = lax.broadcasted_iota(jnp.int32, (1, 128), 1)
    low = jnp.where(lane < HEAD_DIM, 1.0, 0.0).astype(jnp.bfloat16)
    high = jnp.where(lane < HEAD_DIM, 0.0, 1.0).astype(jnp.bfloat16)
    return low, high


def key_range(i):
    return max(0, i * BLOCK - LONGEST), (i + 1) * BLOCK


class Front:
    def __init__(self, spot, experts, chunks, r):
        self.spot, self.experts, self.r = spot, experts, r
        self.length, self.width = r.tokens.shape
        self.capacity = 2 * self.length // (experts + 4)
        self.blocks = self.length // BLOCK
        self.tall, self.wide = self.length // 2, r.dn.shape[0] // chunks

    def ranks(self):
        r, n = self.r, self.length
        order = [r.order[:, k : k + 1] for k in range(2)]
        route = [r.routes[:, k : k + 1] for k in range(2)]
        parts = []
        for k in range(2):
            parts += [lax.div(order[k], 256).astype(jnp.float32), lax.rem(order[k], 256).astype(jnp.float32)]
        parts += [route[k].astype(jnp.float32) for k in range(2)]
        side = turned(spread(parts).astype(jnp.bfloat16))
        order_row = [side[2 * k : 2 * k + 1] * 256.0 + side[2 * k + 1 : 2 * k + 2] for k in range(2)]
        route_row = [side[4 + k : 5 + k] for k in range(2)]
        out = []
        for k in range(2):
            for i in range(self.blocks):
                rows = slice(i * BLOCK, (i + 1) * BLOCK)
                mine, kind = order[k][rows].astype(jnp.float32), route[k][rows].astype(jnp.float32)
                ahead = jnp.zeros((BLOCK, n), jnp.float32)
                for other in range(2):
                    ahead += jnp.where(
                        jnp.logical_and(order_row[other] < mine, route_row[other] == kind), 1.0, 0.0)
                rank = jnp.sum(ahead, axis=1, keepdims=True)
                kept = jnp.logical_and(kind < self.experts, rank < self.capacity)
                r.scal[pl.ds(i * BLOCK, BLOCK), 8 + k : 9 + k] = jnp.where(
                    kept, kind * self.capacity + rank, float(self.experts * self.capacity))
                r.scal[pl.ds(i * BLOCK, BLOCK), 10 + k : 11 + k] = jnp.where(kept, kind, 255.0)
                r.scal[pl.ds(i * BLOCK, BLOCK), 12 + k : 13 + k] = jnp.where(kept, rank, 0.0)
                r.scal[pl.ds(i * BLOCK, BLOCK), 14 + k : 15 + k] = kind

    def flat_rows(self):
        r = self.r
        side = turned(r.scal[...].astype(jnp.bfloat16))
        for k in range(2):
            kind, rank = side[10 + k : 11 + k], side[12 + k : 13 + k]
            r.flat[k : k + 1] = jnp.where(
                kind < 255.0, kind * self.capacity + rank, float(self.experts * self.capacity))

    def first_norm(self):
        r = self.r
        for i in range(self.blocks):
            rows = pl.ds(i * BLOCK, BLOCK)
            x = r.tokens[rows].astype(jnp.float32)
            r.scal[rows, 0:1] = lax.rsqrt(jnp.mean(x * x, axis=1, keepdims=True) + epsilon)

    def masks(self):
        r, n = self.r, self.length
        segment = r.segments[...].astype(jnp.float32)
        padding = r.padding[...]
        column = jnp.transpose(jnp.broadcast_to(segment, (128, n)))[:, 0:1]
        for i in range(self.blocks):
            k0, k1 = key_range(i)
            row = lax.broadcasted_iota(jnp.int32, (BLOCK, k1 - k0), 0) + i * BLOCK
            col = lax.broadcasted_iota(jnp.int32, (BLOCK, k1 - k0), 1) + k0
            same = column[i * BLOCK : (i + 1) * BLOCK] == segment[:, k0:k1]
            real = jnp.broadcast_to(padding[:, k0:k1], row.shape) == 1
            fine = jnp.logical_and(jnp.logical_and(col <= row, same), jnp.logical_or(real, col == row))
            r.bias[pl.ds(i * BLOCK, BLOCK), pl.ds(0, k1 - k0)] = jnp.where(fine, 0.0, -1e30)

    def small_rows(self):
        r = self.r
        side = turned(r.rest[:, pl.ds(self.width, 128)])
        r.rows[...] = side[: r.rows.shape[0]]

    def project(self, i):
        r, w = self.r, self.width
        rows = pl.ds(i * BLOCK, BLOCK)
        x = r.tokens[rows].astype(jnp.float32)
        normed = (x * r.scal[rows, 0:1] * r.rows[0:1]).astype(jnp.bfloat16)
        r.normed[rows] = normed
        cosine, sine = r.cosine[rows], r.sine[rows]
        for part, to in enumerate((r.q, r.k)):
            full = dot(normed, r.qkv[:, pl.ds(part * w, w)])
            for pair in range(w // 128):
                v = full[:, pair * 128 : pair * 128 + 128]
                v = v * cosine + swap_halves(v) * sine
                if part == 0:
                    v = v * HEAD_DIM ** (-0.5)
                to[rows, pl.ds(pair * 128, 128)] = v.astype(jnp.bfloat16)
        r.v[rows] = dot(normed, r.qkv[:, pl.ds(2 * w, w)]).astype(jnp.bfloat16)

    def attend(self, i, pair):
        r = self.r
        k0, k1 = key_range(i)
        rows, keys, lanes = pl.ds(i * BLOCK, BLOCK), pl.ds(k0, k1 - k0), pl.ds(pair * 128, 128)
        q, k, v = r.q[rows, lanes], r.k[keys, lanes], r.v[keys, lanes]
        bias = r.bias[rows, pl.ds(0, k1 - k0)]
        out = jnp.zeros((BLOCK, 128), jnp.float32)
        for s, mask in enumerate(head_masks()):
            scores = dot(q * mask, k, 1, 1) + bias
            top = jnp.max(scores, axis=1, keepdims=True)
            e = jnp.exp(scores - top)
            total = jnp.sum(e, axis=1, keepdims=True)
            probs = (e * (1.0 / total)).astype(jnp.bfloat16)
            out = out + dot(probs, v * mask)
            r.lse[rows, 2 * pair + s : 2 * pair + s + 1] = top + jnp.log(total)
        r.attended[rows, lanes] = out.astype(jnp.bfloat16)

    def gate(self, i):
        r, w, e = self.r, self.width, self.experts
        rows = pl.ds(i * BLOCK, BLOCK)
        h = r.tokens[rows].astype(jnp.float32) + dot(r.attended[rows], r.rest[:, pl.ds(0, w)])
        r.h[rows] = h
        inverse = lax.rsqrt(jnp.mean(h * h, axis=1, keepdims=True) + epsilon)
        hn = (h * inverse * r.rows[1:2]).astype(jnp.bfloat16)
        r.hn[rows] = hn
        small = dot(hn, r.rest[:, pl.ds(w, 128)])
        lane = lax.broadcasted_iota(jnp.int32, small.shape, 1)
        prev = r.prev[rows].astype(jnp.float32)
        prev_lane = lax.broadcasted_iota(jnp.int32, prev.shape, 1)
        picked = []
        for k in range(2):
            route = r.routes[rows, k : k + 1]
            picked.append(jnp.sum(jnp.where(lane == route + 8, small, 0.0), axis=1, keepdims=True)
                          + jnp.sum(jnp.where(prev_lane == route, prev, 0.0), axis=1, keepdims=True))
        def soft(a, b):
            top = jnp.maximum(a, b)
            ea, eb = jnp.exp(a - top), jnp.exp(b - top)
            return ea / (ea + eb), eb / (ea + eb)
        gates = soft(*picked)
        mix = soft(small[:, 2:3], small[:, 3:4]) + soft(small[:, 4:5], small[:, 5:6])
        r.scal[rows, 1:2] = inverse
        for j, c in enumerate(gates + mix):
            r.scal[rows, 2 + j : 3 + j] = c
        cot = r.cot[rows].astype(jnp.float32)
        for k in range(2):
            r.gcot[k, rows] = (gates[k] * cot).astype(jnp.bfloat16)

    def slots(self, d):
        r, n = self.r, self.length
        e = lax.rem(self.spot.ex + d, self.experts)
        slot = (lax.broadcasted_iota(jnp.int32, (self.capacity, n), 0) + e * self.capacity).astype(jnp.float32)
        at = [jnp.where(r.flat[k : k + 1] == slot, 1.0, 0.0) for k in range(2)]
        x = dot((at[0] + at[1]).astype(jnp.bfloat16), r.hn[...]).astype(jnp.bfloat16)
        g = (dot(at[0].astype(jnp.bfloat16), r.gcot[0]) + dot(at[1].astype(jnp.bfloat16), r.gcot[1]))
        g = g.astype(jnp.bfloat16)
        if d == 0:
            rows = pl.ds(pl.multiple_of(e * self.capacity, 16), self.capacity)
            r.xin[rows], r.gin[rows] = x, g
        else:
            r.sendx[d - 1], r.sendg[d - 1] = x, g


    def side_rows(self):
        self.r.xt[...] = jnp.transpose(self.r.xin[...])

    def hidden(self, j, part):
        r, w = self.r, self.wide
        ff = r.gu.shape[1] // 2
        rows = pl.ds(part * self.tall, self.tall)
        x, g = r.xin[rows], r.gin[rows]
        gate = dot(x, r.gu[:, pl.ds(j * w, w)])
        up = dot(x, r.gu[:, pl.ds(ff + j * w, w)])
        back = dot(g, r.dn[pl.ds(j * w, w)], 1, 1)
        sigmoid = 1.0 / (1.0 + jnp.exp(-gate))
        silu = gate * sigmoid
        r.act[rows, pl.ds(j * w, w)] = (silu * up).astype(jnp.bfloat16)
        r.pg[rows, pl.ds(j * w, w)] = (back * up * sigmoid * (1.0 + gate * (1.0 - sigmoid))).astype(jnp.bfloat16)
        r.pg[rows, pl.ds(ff + j * w, w)] = (back * silu).astype(jnp.bfloat16)

    def outward(self, part):
        rows = pl.ds(part * self.tall, self.tall)
        self.r.yall[rows] = dot(self.r.act[rows], self.r.dn[...]).astype(jnp.bfloat16)

    def inward(self, part):
        rows = pl.ds(part * self.tall, self.tall)
        self.r.dxall[rows] = dot(self.r.pg[rows], self.r.gu[...], 1, 1).astype(jnp.bfloat16)

    def down_grad(self, j):
        r, w = self.r, self.wide
        r.dn_stage[j % 2] = dot(r.act[:, pl.ds(j * w, w)], r.gin[...], 0, 0).astype(jnp.bfloat16)

    def up_grad(self, j, n):
        r, w = self.r, self.wide
        r.gu_stage[n] = dot(r.xt[...], r.pg[:, pl.ds(j * w, w)]).astype(jnp.bfloat16)


def expert_device(spot, e):
    return {"dp": spot.dp, "expert": e}


def slots_of(ref, capacity):
    return lambda e: ref.at[pl.ds(pl.multiple_of(e * capacity, 16), capacity)]


class Exchange:
    def __init__(self, spot, experts, number, out, into, sems):
        self.spot, self.experts, self.n, self.out, self.into, self.sems = spot, experts, number, out, into, sems

    def copy(self, d):
        e = lax.rem(self.spot.ex + d, self.experts)
        return pltpu.make_async_remote_copy(
            src_ref=self.out(d), dst_ref=self.into(self.spot.ex), send_sem=self.sems.at[0, self.n, d],
            recv_sem=self.sems.at[1, self.n, self.spot.ex], device_id=expert_device(self.spot, e),
            device_id_type=MESH)

    def send(self, d):
        self.copy(d).start()

    def drain(self, d):
        self.copy(d).wait_send()

    def receive(self, d):
        e = lax.rem(self.spot.ex + d, self.experts)
        pltpu.make_async_remote_copy(
            src_ref=self.into(e), dst_ref=self.into(e), send_sem=self.sems.at[0, self.n, d],
            recv_sem=self.sems.at[1, self.n, e], device_id=expert_device(self.spot, e),
            device_id_type=MESH).wait_recv()


def woven(work, events):
    done = 0
    for j, piece in enumerate(work):
        piece()
        upto = (j + 1) * len(events) // len(work)
        for event in events[done:upto]:
            event()
        done = upto


class FrontIns(NamedTuple):
    tokens: object
    prev: object
    segments: object
    padding: object
    routes: object
    order: object
    cot: object
    cosine: object
    sine: object
    qkv_own: object
    rest_own: object
    gu_own: object
    dn_own: object


class FrontOuts(NamedTuple):
    gu_grad: object
    dn_grad: object
    qkv_hbm: object
    rest_hbm: object
    q_hbm: object
    k_hbm: object
    v_hbm: object
    normed_hbm: object
    attended_hbm: object
    hn_hbm: object
    h_hbm: object
    lse_hbm: object
    scal_hbm: object
    rows_hbm: object
    y_hbm: object
    dx_hbm: object


class FrontScratch(NamedTuple):
    dn_stage: object
    gu_stage: object
    qkv: object
    rest: object
    q: object
    k: object
    v: object
    normed: object
    attended: object
    hn: object
    h: object
    lse: object
    scal: object
    rows: object
    gu: object
    dn: object
    xin: object
    gin: object
    xt: object
    act: object
    pg: object
    yall: object
    dxall: object
    flat: object
    bias: object
    gcot: object
    sendx: object
    sendg: object
    sends: object
    recvs: object
    mates: object
    local: object
    trade: object


def front_kernel(sizes, experts, chunks, *refs):
    r = SimpleNamespace(**dict(zip(FrontIns._fields + FrontOuts._fields + FrontScratch._fields, refs)))
    spot = Spot(sizes)
    front = Front(spot, experts, chunks, r)
    enter(spot, line_neighbours(spot)
          + [(None, expert_device(spot, lax.rem(spot.ex + d, experts))) for d in range(1, experts)])
    rows = r.qkv_own.shape[0]
    rows_d = r.dn_own.shape[0]
    ff = r.dn.shape[0]
    first, later = [], []
    for src, out in ((r.qkv_own, r.qkv), (r.rest_own, r.rest)):
        part = src.shape[1] // 2
        def half(o, core, out=out, part=part):
            return out.at[pl.ds(pl.multiple_of(o * rows, 8), rows), pl.ds(pl.multiple_of(core * part, 128), part)]
        first.append((src.at[:, pl.ds(pl.multiple_of(spot.core * part, 128), part)],
                      lambda o, half=half: half(o, spot.core), True, lambda o, half=half: half(o, 1 - spot.core)))
    part = rows_d // 2
    for p, zf in ((0, True), (1, False)):
        later.append((r.dn_own.at[pl.ds(p * part, part)],
                      lambda o, p=p: r.dn.at[pl.ds(pl.multiple_of(o * rows_d + p * part, 8), part)], zf, None))
    wide = ff // chunks
    for c in range(chunks):
        for side in range(2):
            cols = pl.ds(side * ff + c * wide, wide)
            later.append((r.gu_own.at[:, cols],
                          lambda o, cols=cols: r.gu.at[pl.ds(pl.multiple_of(o * rows, 8), rows), cols], True, None))
    floods = [Flood(spot, n, own, view, r.sends, r.recvs, zf, None if other is None else r.mates)
              for n, (own, view, zf, other) in enumerate(first + later)]
    levels = [f.levels() for f in floods]
    dense = levels[:2]
    keeps = [pltpu.make_async_copy(own, view(spot.dp), r.local.at[n])
             for n, (own, view, zf, other) in enumerate(first + later)]
    for ls in dense:
        for step in ls[0]:
            step()
    for keep in keeps:
        keep.start()
    front.ranks()
    front.flat_rows()
    front.first_norm()
    front.masks()
    depth = max(map(len, levels))
    keyed = []
    for n, ls in enumerate(levels[2:]):
        for level, steps in enumerate(ls):
            keyed += [(n + LEVEL_STEP * level if level else n - LEAD, n, level, step) for step in steps]
    keyed.sort(key=lambda t: t[:3])
    ahead = [t for t in keyed if t[0] <= 0]
    keyed = keyed[len(ahead):]
    for level in range(1, depth):
        if level == depth - 1:
            for t in ahead:
                t[3]()
        for ls in dense:
            if level < len(ls):
                for step in ls[level]:
                    step()
    for keep in keeps[:2]:
        keep.wait()
    for f, (own, view, zf, other) in zip(floods, first):
        f.mates(other)
    trades = [Exchange(spot, experts, n, lambda d, out=out: out.at[d - 1], slots_of(into, front.capacity), r.trade)
              for n, (out, into) in enumerate(((r.sendx, r.xin), (r.sendg, r.gin)))]
    work = [front.small_rows]
    work += [functools.partial(front.project, i) for i in range(front.blocks)]
    for pair in range(front.width // 128):
        work += [functools.partial(front.attend, i, pair) for i in range(front.blocks)]
    work += [functools.partial(front.gate, i) for i in range(front.blocks)]
    def dispatch(d):
        front.slots(d)
        if d:
            for t in trades:
                t.send(d)
    work += [functools.partial(dispatch, d) for d in list(range(1, experts)) + [0]]
    def upto(item):
        out = []
        while keyed and keyed[0][1] <= item:
            out.append(keyed.pop(0)[3])
        last = max((j for j, t in enumerate(keyed) if t[1] <= item), default=-1)
        out += [t[3] for t in keyed[: last + 1]]
        del keyed[: last + 1]
        return out
    saves, number = [], []
    def save(src, dst):
        number.append(0)
        copy = pltpu.make_async_copy(src, dst, r.local.at[len(keeps) + len(number)])
        copy.start()
        saves.append(copy)
        return copy
    def save_dense():
        for src, dst in ((r.qkv, r.qkv_hbm), (r.rest, r.rest_hbm), (r.q, r.q_hbm), (r.k, r.k_hbm), (r.v, r.v_hbm),
                         (r.normed, r.normed_hbm), (r.attended, r.attended_hbm), (r.lse, r.lse_hbm), (r.rows, r.rows_hbm),
                         (r.hn, r.hn_hbm), (r.h, r.h_hbm), (r.scal, r.scal_hbm)):
            save(src, dst)
    events = []
    early = len(keyed) * SHARE // 16
    events, keyed[:early] = [t[3] for t in keyed[:early]], []
    woven(work, events)
    save_dense()
    for event in upto(1 + 2):
        event()
    for d in range(1, experts):
        for t in trades:
            t.receive(d)
    keeps[2].wait()
    keeps[3].wait()
    front.side_rows()
    staged = {}
    def stage(key, src, dst):
        staged[key] = save(src, dst)
    def grads(c):
        for key in (c % 2, 2 + (c % 2) * 2, 3 + (c % 2) * 2):
            if key in staged:
                old = staged.pop(key)
                saves[:] = [s for s in saves if s is not old]
                old.wait()
        front.down_grad(c)
        stage(c % 2, r.dn_stage.at[c % 2], r.dn_grad.at[pl.ds(c * wide, wide)])
        for j in (c, chunks + c):
            n = (c % 2) * 2 + j // chunks
            front.up_grad(j, n)
            stage(2 + n, r.gu_stage.at[n], r.gu_grad.at[:, pl.ds(j * wide, wide)])
    for c in range(chunks):
        for event in upto(2 + 2 * c + 1):
            event()
        keeps[4 + 2 * c].wait()
        keeps[5 + 2 * c].wait()
        for p in range(2):
            front.hidden(c, p)
        grads(c)
    for p in range(2):
        front.outward(p)
    save(r.yall, r.y_hbm)
    for p in range(2):
        front.inward(p)
    save(r.dxall, r.dx_hbm)
    for f in floods:
        for drain in f.drains:
            drain()
    for d in range(1, experts):
        for t in trades:
            t.drain(d)
    for copy in saves:
        copy.wait()


def run_front(sizes, experts, ins, chunks=4):
    tokens, qkv, rest, gu, dn = ins[0], ins[9], ins[10], ins[11], ins[12]
    length, width = tokens.shape
    n_dp = sizes[0] * sizes[1]
    capacity = 2 * length // (experts + 4)
    slots, ff = experts * capacity, gu.shape[1] // 2
    bf, f4 = jnp.bfloat16, jnp.float32
    S, V = jax.ShapeDtypeStruct, pltpu.VMEM
    token = S((length, width), bf)
    gu_all, dn_all = (gu.shape[0] * n_dp, gu.shape[1]), (dn.shape[0] * n_dp, dn.shape[1])
    outs = [S(gu_all, bf), S(dn_all, bf)] + [S((a.shape[0] * n_dp, a.shape[1]), bf) for a in (qkv, rest)]
    outs += [token] * 6 + [S((length, width), f4), S((length, 128), f4), S((length, 128), f4), S((16, width), f4)]
    outs += [S((slots, width), bf)] * 2
    items = 4 + 2 * chunks
    dma = pltpu.SemaphoreType.DMA
    vmem = pl.BlockSpec(memory_space=pltpu.VMEM)
    hbm = pl.BlockSpec(memory_space=pl.ANY)
    send = V((experts - 1, capacity, width), bf)
    return pl.pallas_call(
        functools.partial(front_kernel, sizes, experts, chunks),
        out_shape=tuple(outs),
        in_specs=[vmem] * 13,
        out_specs=(hbm,) * len(outs),
        scratch_shapes=[V((2, ff // chunks, width), bf), V((4, width, ff // chunks), bf)] + [V(o.shape, o.dtype) for o in outs[2:14]] + [
            V(gu_all, bf), V(dn_all, bf), V((slots, width), bf), V((slots, width), bf), V((width, slots), bf),
            V((slots, dn_all[0]), bf), V((slots, gu_all[1]), bf), V((slots, width), bf), V((slots, width), bf),
            V((8, length), f4), V((length, BLOCK + LONGEST), f4), V((2, length, width), bf), send, send,
            dma((5, items, n_dp)), dma((items, n_dp)), dma((2, n_dp)), dma((items + 16 + 3 * chunks,)),
            dma((2, 4, experts))],
        compiler_params=pltpu.CompilerParams(collective_id=1, has_side_effects=True, vmem_limit_bytes=63 << 20),
        name="front",
    )(*ins)


def add_into(view, more):
    view[...] = (view[...].astype(jnp.float32) + more[...].astype(jnp.float32)).astype(view.dtype)


class Reduce:
    def __init__(self, spot, number, view, one, two, sends, recv_one, recv_two, x_first):
        self.s, self.n, self.view, self.one, self.two = spot, number, view, one, two
        self.sends, self.recv_one, self.recv_two, self.x_first = sends, recv_one, recv_two, x_first
        if x_first:
            self.np, self.nq, self.p, self.q = spot.nx, spot.nz, spot.x, spot.z
        else:
            self.np, self.nq, self.p, self.q = spot.nz, spot.nx, spot.z, spot.x
        self.drains = []

    @staticmethod
    def slots(n):
        return 1 if n == 2 else n + 1

    @staticmethod
    def slot(n, place, above):
        if n == 2:
            return 0
        return jnp.where(above, n, place)

    def owner(self, p, q):
        return q * self.s.nx + p if self.x_first else p * self.s.nx + q

    def along(self, first, value):
        return self.s.device(x=value) if first == self.x_first else self.s.device(z=value)

    def push(self, cond, o, dst, recv, device):
        copy = pltpu.make_async_remote_copy(
            src_ref=self.view(o), dst_ref=dst, send_sem=self.sends.at[self.n, o], recv_sem=recv,
            device_id=device, device_id_type=MESH)
        pl.when(cond)(lambda: copy.start())
        self.drains.append(lambda: pl.when(cond)(lambda: copy.wait_send()))

    def take(self, cond, o, slot, recv):
        def run():
            pltpu.make_async_remote_copy(
                src_ref=slot, dst_ref=slot, send_sem=self.sends.at[self.n, o], recv_sem=recv,
                device_id=self.s.device(), device_id_type=MESH).wait_recv()
            add_into(self.view(o), slot)
        pl.when(cond)(run)

    def order(self):
        return sorted(range(-(self.nq - 1), self.nq), key=lambda d: (-abs(d), d))

    def phase_one(self):
        steps = []
        for turn in range(2):
            sign = jnp.where(self.p * 2 < self.np, 1, -1) * (1 if turn == 0 else -1)
            for k in range(self.np - 1, 0, -1):
                for dq in self.order():
                    def step(sign=sign, k=k, dq=dq):
                        p, q = self.p + sign * k, self.q + dq
                        here = jnp.logical_and(between(p, self.np), between(q, self.nq))
                        o = self.owner(p, q)
                        if self.np > 2:
                            behind = jnp.logical_and(here, between(self.p - sign, self.np))
                            self.take(behind, o, self.one.at[p, q], self.recv_one.at[self.n, p, q])
                        slot = self.slot(self.np, p, jnp.logical_and(k == 1, sign < 0))
                        self.push(here, o, self.one.at[slot, q], self.recv_one.at[self.n, slot, q],
                                  self.along(True, self.p + sign))
                    steps.append(step)
        return steps

    def settle(self, cond, q):
        o = self.owner(self.p, q)
        below = self.p > 0
        above = self.p < self.np - 1
        if cond is not None:
            below, above = jnp.logical_and(cond, below), jnp.logical_and(cond, above)
        for cond, top in ((below, False), (above, True)):
            slot = self.slot(self.np, self.p, top)
            self.take(cond, o, self.one.at[slot, q], self.recv_one.at[self.n, slot, q])

    def phase_two(self):
        def step(sign, k, now):
            q = self.q + sign * k
            here = jnp.logical_and(now, between(q, self.nq))
            o = self.owner(self.p, q)
            self.settle(here, q)
            behind = jnp.logical_and(here, between(self.q - sign, self.nq))
            if self.nq > 2:
                self.take(behind, o, self.two.at[q], self.recv_two.at[self.n, q])
            slot = self.slot(self.nq, q, jnp.logical_and(k == 1, sign < 0))
            self.push(here, o, self.two.at[slot], self.recv_two.at[self.n, slot], self.along(False, self.q + sign))
        levels = []
        for level in range(self.nq - 1):
            up, down = self.q == level, self.nq - 1 - self.q == level
            if self.nq % 2 == 0:
                ways = [(jnp.where(up, 1, -1), jnp.logical_or(up, down))]
            else:
                ways = [(jnp.int32(1), up), (jnp.int32(-1), down)]
            levels.append([functools.partial(step, sign, k, now) for sign, now in ways for k in range(self.nq - 1, 0, -1)])
        return levels

    def finish(self, out):
        o = self.owner(self.p, self.q)
        self.settle(None, self.q)
        out[...] = self.view(o)[...].astype(jnp.float32)
        for cond, top in ((self.q > 0, False), (self.q < self.nq - 1, True)):
            def run(slot=self.slot(self.nq, self.q, top)):
                two = self.two.at[slot]
                pltpu.make_async_remote_copy(
                    src_ref=two, dst_ref=two, send_sem=self.sends.at[self.n, o], recv_sem=self.recv_two.at[self.n, slot],
                    device_id=self.s.device(), device_id_type=MESH).wait_recv()
                out[...] += two[...].astype(jnp.float32)
            pl.when(cond)(run)


def column_of(row):
    return jnp.transpose(jnp.broadcast_to(row, (128, row.shape[1])))


class Dense:
    def __init__(self, spot, number, own, bufs, sems, done):
        self.spot, self.n, self.own, self.done = spot, number, own, done
        self.mine, self.one, self.two, self.ybuf, self.final, self.other = bufs
        self.sends, self.recv_one, self.recv_two, self.mate, self.ys, self.outs = sems
        self.reduce = Reduce(spot, number, lambda o: self.mine.at[o], self.one, self.two, self.sends, self.recv_one,
                             self.recv_two, True)
        self.drains = []

    def swap(self):
        return pltpu.make_async_remote_copy(
            src_ref=self.own.at[1 - self.spot.core], dst_ref=self.mine, send_sem=self.mate.at[0, self.n],
            recv_sem=self.mate.at[1, self.n], device_id=self.spot.device(core=1 - self.spot.core), device_id_type=MESH)

    def begin(self):
        self.swap().start()

    def merge(self):
        self.swap().wait()
        def add(o, carry):
            add_into(self.mine.at[o], self.own.at[self.spot.core, o])
            return carry
        lax.fori_loop(0, self.mine.shape[0], add, 0)
        for step in self.reduce.phase_one():
            step()

    def across(self, d):
        y = lax.rem(self.spot.y + d, self.spot.ny)
        return pltpu.make_async_remote_copy(
            src_ref=self.ybuf.at[self.spot.y], dst_ref=self.ybuf.at[self.spot.y], send_sem=self.ys.at[0, self.n, d],
            recv_sem=self.ys.at[1, self.n, self.spot.y], device_id=self.spot.device(y=y), device_id_type=MESH)

    def settle(self):
        self.reduce.finish(self.final)
        self.ybuf[self.spot.y] = self.final[...].astype(self.ybuf.dtype)
        for d in range(1, self.spot.ny):
            copy = self.across(d)
            copy.start()
            self.drains.append(copy.wait_send)

    def hand(self):
        return pltpu.make_async_remote_copy(
            src_ref=self.final, dst_ref=self.other, send_sem=self.outs.at[0, self.n], recv_sem=self.outs.at[1, self.n],
            device_id=self.spot.device(core=1 - self.spot.core), device_id_type=MESH)

    def total(self):
        for d in range(1, self.spot.ny):
            y = lax.rem(self.spot.y + d, self.spot.ny)
            pltpu.make_async_remote_copy(
                src_ref=self.ybuf.at[y], dst_ref=self.ybuf.at[y], send_sem=self.ys.at[0, self.n, d],
                recv_sem=self.ys.at[1, self.n, y], device_id=self.spot.device(y=y), device_id_type=MESH).wait_recv()
        sum_ = self.ybuf[0].astype(jnp.float32)
        for y in range(1, self.spot.ny):
            sum_ = sum_ + self.ybuf[y].astype(jnp.float32)
        self.final[...] = sum_
        self.hand().start()

    def end(self):
        self.hand().wait()
        for half in range(2):
            pl.when(self.spot.core == half)(lambda half=half: self.done(half, self.final[...]))
            pl.when(self.spot.core != half)(lambda half=half: self.done(half, self.other[...]))

    def steps(self):
        out = [(HOP * (n + 1), f) for n, fs in enumerate(self.reduce.phase_two()) for f in fs]
        end = HOP * self.reduce.nq
        return out + [(end, self.settle), (end + 3, self.total), (end + 5, self.end)]


class Tail:
    def __init__(self, spot, experts, r):
        self.spot, self.experts, self.r = spot, experts, r
        self.length, self.width = r.cot.shape
        self.blocks = self.length // BLOCK
        self.pairs = self.width // 128

    def prepare(self):
        r, n = self.r, self.length
        r.lse_rows[...] = jnp.transpose(r.lse[...])[: r.lse_rows.shape[0]]
        segment = r.segments[...].astype(jnp.float32)
        seg_col = column_of(segment)[:, 0:1]
        pad_col = column_of(r.padding[...].astype(jnp.float32))[:, 0:1]
        at = 0
        for i in range(self.blocks):
            k0, k1 = key_range(i)
            key = lax.broadcasted_iota(jnp.int32, (k1 - k0, BLOCK), 0) + k0
            query = lax.broadcasted_iota(jnp.int32, (k1 - k0, BLOCK), 1) + i * BLOCK
            same = seg_col[k0:k1] == segment[:, i * BLOCK : (i + 1) * BLOCK]
            fine = jnp.logical_and(jnp.logical_and(key <= query, same),
                                   jnp.logical_or(pad_col[k0:k1] == 1.0, key == query))
            r.bias[pl.ds(at, k1 - k0)] = jnp.where(fine, 0.0, -1e30).astype(jnp.bfloat16)
            at += k1 - k0
        r.gain_rows[...] = jnp.zeros(r.gain_rows.shape, jnp.float32)

    def combine(self, i):
        r, w, e = self.r, self.width, self.experts
        tile = BLOCK // 2
        rows = pl.ds(i * tile, tile)
        col = lambda j: r.scal[rows, j : j + 1]
        slot = lax.broadcasted_iota(jnp.int32, (tile, r.y.shape[0]), 1).astype(jnp.float32)
        at = [jnp.where(col(8 + k) == slot, 1.0, 0.0).astype(jnp.bfloat16) for k in range(2)]
        pair = [dot(at[k], r.y[...]) for k in range(2)]
        routed = dot(at[0] + at[1], r.dx[...])
        cot, hn = r.cot[rows].astype(jnp.float32), r.hn[rows].astype(jnp.float32)
        h = r.tg[rows]
        gates, mix = [col(2), col(3)], [[col(4), col(5)], [col(6), col(7)]]
        route = [col(14 + k) for k in range(2)]
        one = lambda c: jnp.where(c, 1.0, 0.0)
        fixed = [[one(route[k] == e + 2 + j) for j in range(2)] for k in range(2)]
        share = [one(route[k] == e + 1) + fixed[k][0] * mix[0][0] + fixed[k][1] * mix[1][0] for k in range(2)]
        copy = gates[0] * share[0] + gates[1] * share[1]
        chosen = [gates[0] * fixed[0][j] + gates[1] * fixed[1][j] for j in range(2)]
        coef = [chosen[j] * mix[j][1] for j in range(2)]
        const = [r.rows[6 + j : 7 + j] for j in range(2)]
        branch = gates[0] * pair[0] + gates[1] * pair[1] + copy * hn + (coef[0] * const[0] + coef[1] * const[1])
        r.layer_out[rows] = (h + branch).astype(jnp.bfloat16)
        total = lambda v: jnp.sum(v, axis=1, keepdims=True)
        with_hn = total(cot * hn)
        with_const = [total(cot * const[j]) for j in range(2)]
        grads = [total(cot * pair[k]) + share[k] * with_hn
                 + fixed[k][0] * mix[0][1] * with_const[0] + fixed[k][1] * mix[1][1] * with_const[1] for k in range(2)]
        mean = gates[0] * grads[0] + gates[1] * grads[1]
        picked = [gates[k] * (grads[k] - mean) for k in range(2)]
        lane = lax.broadcasted_iota(jnp.int32, (tile, r.prev_grad.shape[1]), 1).astype(jnp.float32)
        r.prev_grad[rows] = jnp.where(lane == route[0], picked[0], 0.0) + jnp.where(lane == route[1], picked[1], 0.0)
        lane = lax.broadcasted_iota(jnp.int32, (tile, 128), 1).astype(jnp.float32)
        low = jnp.where(lane == route[0] + 8, picked[0], 0.0) + jnp.where(lane == route[1] + 8, picked[1], 0.0)
        for j in range(2):
            g = [chosen[j] * with_hn, chosen[j] * with_const[j]]
            m = mix[j][0] * g[0] + mix[j][1] * g[1]
            for q in range(2):
                low = jnp.where(lane == 2 + 2 * j + q, mix[j][q] * (g[q] - m), low)
        low = low.astype(jnp.bfloat16)
        r.low[rows] = low
        high = [c.astype(jnp.bfloat16).astype(jnp.float32) for c in coef]
        both = jnp.zeros(lane.shape, jnp.float32)
        for j in range(2):
            both = jnp.where(lane == 6 + j, high[j], jnp.where(lane == 70 + j, coef[j] - high[j], both))
        r.coef[rows] = both.astype(jnp.bfloat16)
        grad = routed + copy * cot + dot(low, r.rest[:, pl.ds(w, 128)], 1, 1)
        dh = cot + self.unnorm(grad, h, col(1), 1)
        r.tg[rows] = dh
        dh = dh.astype(jnp.bfloat16)
        r.dh[rows] = dh

    def unnorm(self, grad, v, inverse, gain):
        r = self.r
        scaled = r.rows[gain : gain + 1] * grad
        mean = jnp.sum(scaled * v, axis=1, keepdims=True) / v.shape[1]
        r.gain_rows[gain : gain + 1] += jnp.sum(grad * v * inverse, axis=0, keepdims=True)
        return inverse * scaled - v * (inverse * inverse * inverse * mean)

    def unproject(self, i):
        r = self.r
        rows = pl.ds(i * BLOCK, BLOCK)
        r.ag[rows] = dot(r.dh[rows], r.rest[:, pl.ds(0, self.width)], 1, 1).astype(jnp.bfloat16)

    def blocked(self, v):
        n = self.spot.nz * self.spot.nx
        return v.reshape(n, v.shape[0] // n, v.shape[1])

    def out_grad(self):
        r = self.r
        half = self.width // 2
        for c in range(2):
            g = dot(r.attended[...], r.dh[:, pl.ds(c * half, half)], 0, 0)
            r.own[self.pairs // 2, c] = self.blocked(g).astype(jnp.bfloat16)

    def small_grad(self):
        r = self.r
        g = dot(r.cot[...], r.coef[...], 0, 0)
        lane = lax.broadcasted_iota(jnp.int32, g.shape, 1)
        g = jnp.where(lane < 64, g + pltpu.roll(g, 64, 1), 0.0) + dot(r.hn[...], r.low[...], 0, 0)
        r.own_small[0] = self.blocked(g).astype(jnp.bfloat16)
        r.own_small[1] = jnp.zeros(r.own_small.shape[1:], jnp.bfloat16)

    def small_end(self):
        r = self.r
        g = r.own_small[0].astype(jnp.float32)
        lane = lax.broadcasted_iota(jnp.int32, g.shape, 2)
        for j in range(2):
            g = jnp.where(lane == j, self.blocked(column_of(r.gain_rows[j : j + 1])), g)
        r.own_small[0] = g.astype(jnp.bfloat16)

    def normed_side(self):
        self.r.nt[...] = jnp.transpose(self.r.normed[...])

    def pair_begin(self, pair):
        r = self.r
        r.kt[...] = jnp.transpose(r.k[:, pl.ds(pair * 128, 128)])
        r.dk[...] = jnp.zeros(r.dk.shape, jnp.float32)
        r.dv[...] = jnp.zeros(r.dv.shape, jnp.float32)

    def attend(self, pair, i):
        r = self.r
        k0, k1 = key_range(i)
        at = sum(key_range(j)[1] - key_range(j)[0] for j in range(i))
        rows, keys, lanes = pl.ds(i * BLOCK, BLOCK), pl.ds(k0, k1 - k0), pl.ds(pair * 128, 128)
        q, k, v, g = r.q[rows, lanes], r.k[keys, lanes], r.v[keys, lanes], r.ag[rows, lanes]
        bias = r.bias[pl.ds(at, k1 - k0)].astype(jnp.float32)
        dq = []
        for s, mask in enumerate(head_masks()):
            qs, gs = q * mask, g * mask
            head = 2 * pair + s
            probs = jnp.exp(dot(k, qs, 1, 1) + bias - r.lse_rows[head : head + 1, rows])
            grad = dot(v, gs, 1, 1)
            mean = jnp.sum(probs * grad, axis=0, keepdims=True)
            ds = (probs * (grad - mean)).astype(jnp.bfloat16)
            r.dv[keys] += dot(probs.astype(jnp.bfloat16), gs)
            r.dk[keys] += dot(ds, qs)
            dq.append(dot(r.kt[pl.ds(s * HEAD_DIM, HEAD_DIM), keys], ds))
        r.dq[rows] = jnp.transpose(jnp.concatenate(dq, axis=0))

    def pair_end(self, pair):
        r = self.r
        lanes = pl.ds(pair * 128, 128)
        cosine, sine = r.cosine[...], r.sine[...]
        dq = r.dq[...] * HEAD_DIM ** (-0.5)
        dk = r.dk[...]
        dq = (dq * cosine - swap_halves(dq) * sine).astype(jnp.bfloat16)
        dk = (dk * cosine - swap_halves(dk) * sine).astype(jnp.bfloat16)
        dv = r.dv[...].astype(jnp.bfloat16)
        r.q[:, lanes], r.k[:, lanes], r.v[:, lanes] = dq, dk, dv
        half = self.pairs // 2
        for part, d in enumerate((dq, dk, dv)):
            g = dot(r.nt[...], d)
            r.own[pair % half, pair // half, :, :, pl.ds(part * 128, 128)] = self.blocked(g).astype(jnp.bfloat16)

    def last(self, i):
        r, w = self.r, self.width
        rows = pl.ds(i * BLOCK, BLOCK)
        grad = (dot(r.q[rows], r.qkv[:, pl.ds(0, w)], 1, 1) + dot(r.k[rows], r.qkv[:, pl.ds(w, w)], 1, 1)
                + dot(r.v[rows], r.qkv[:, pl.ds(2 * w, w)], 1, 1))
        x = r.tokens[rows].astype(jnp.float32)
        r.tg[rows] += self.unnorm(grad, x, r.scal[rows, 0:1], 0)


class TailIns(NamedTuple):
    gu_hbm: object
    dn_hbm: object
    y_hbm: object
    dx_hbm: object
    h_hbm: object
    attended_hbm: object
    normed_hbm: object
    q_hbm: object
    k_hbm: object
    v_hbm: object
    hn_hbm: object
    tokens_hbm: object
    lse_hbm: object
    cot_hbm: object
    qkv_hbm: object
    rest_hbm: object
    scal_hbm: object
    rows_hbm: object
    segments: object
    padding: object
    cosine: object
    sine: object


class TailOuts(NamedTuple):
    layer_hbm: object
    gu_hbm_out: object
    dn_hbm_out: object
    tg: object
    prev_grad: object
    qkv_out: object
    out_out: object
    small_out: object


def expert_items(spot, chunks, r):
    wide, half = r.gu_src.shape[2] // chunks, r.dn_src.shape[1] // 2
    items, outs = [], []
    for p, xf in ((0, True), (1, False)):
        one, two = (r.d1a, r.d2a) if p == 0 else (r.d1b, r.d2b)
        items.append(Reduce(spot, p, lambda o, p=p: r.dn_src.at[o, pl.ds(p * half, half)], one, two,
                            r.e_sends, r.e_r1, r.e_r2, xf))
        outs.append((r.dn_out, r.dn_hbm_out.at[pl.ds(p * half, half)]))
    for c in range(chunks):
        cut = pl.ds(c * wide, wide)
        items.append(Reduce(spot, 2 + c, lambda o, cut=cut: r.gu_src.at[o, :, cut], r.g1.at[c], r.g2.at[c],
                            r.e_sends, r.e_r1, r.e_r2, True))
        outs.append((r.gu_out, r.gu_hbm_out.at[:, cut]))
    stored = {}
    def finish(n):
        stage, out = outs[n]
        kind = min(n, 2) // 2
        if kind in stored:
            stored[kind].wait()
        items[n].finish(stage)
        stored[kind] = pltpu.make_async_copy(stage, out, r.local.at[kind])
        stored[kind].start()
    events = []
    place = 0
    for n, item in enumerate(items):
        if item.x_first:
            place += 1
        else:
            events += [(8 + 0.8 * j, step) for j, step in enumerate(item.phase_one())]
        at = FIRST + EACH * (place if item.x_first else len(items) - 1)
        levels = item.phase_two()
        for level, steps in enumerate(levels):
            events += [(at + LEVEL_GAP * level, step) for step in steps]
        events.append((at + LEVEL_GAP * len(levels), functools.partial(finish, n)))
    events.sort(key=lambda t: t[0])
    return items, events, stored


class ExpertIns(NamedTuple):
    gu_hbm: object
    dn_hbm: object


class ExpertOuts(NamedTuple):
    gu_hbm_out: object
    dn_hbm_out: object


class ExpertScratch(NamedTuple):
    gu_src: object
    dn_src: object
    gu_out: object
    dn_out: object
    g1: object
    g2: object
    d1a: object
    d2a: object
    d1b: object
    d2b: object
    e_sends: object
    e_r1: object
    e_r2: object
    local: object


def load_experts(chunks, r):
    loads = [pltpu.make_async_copy(r.dn_hbm, r.dn_src, r.local.at[3])]
    wide = r.gu_src.shape[2] // chunks
    for c in range(chunks):
        cut = pl.ds(c * wide, wide)
        loads.append(pltpu.make_async_copy(r.gu_hbm.at[:, :, cut], r.gu_src.at[:, :, cut], r.local.at[4 + c]))
    for l in loads:
        l.start()
    return loads


def start_experts(items, loads):
    for n, item in enumerate(items):
        if n != 1:
            loads[max(n - 1, 0)].wait()
        if item.x_first:
            for step in item.phase_one():
                step()


def expert_kernel(sizes, chunks, *refs):
    r = SimpleNamespace(**dict(zip(ExpertIns._fields + ExpertOuts._fields + ExpertScratch._fields, refs)))
    spot = Spot(sizes)
    loads = load_experts(chunks, r)
    enter(spot, line_neighbours(spot))
    items, events, stored = expert_items(spot, chunks, r)
    start_experts(items, loads)
    for _, event in events:
        event()
    for copy in stored.values():
        copy.wait()
    for item in items:
        for drain in item.drains:
            drain()


def expert_scratch(sizes, gu, dn, chunks):
    nz, nx = sizes[:2]
    n_dp, big = nz * nx, max(nz, nx)
    bf, f4 = jnp.bfloat16, jnp.float32
    V, dma = pltpu.VMEM, pltpu.SemaphoreType.DMA
    rows, rows_d, width = gu.shape[1], dn.shape[1], dn.shape[2]
    wide, tall = gu.shape[2] // chunks, rows_d // 2
    sx, sz = Reduce.slots(nx), Reduce.slots(nz)
    items = 2 + chunks
    out = dict(gu_src=V(gu.shape, bf), dn_src=V(dn.shape, bf), gu_out=V((rows, wide), f4), dn_out=V((tall, width), f4),
               g1=V((chunks, sx, nz, rows, wide), bf), g2=V((chunks, sz, rows, wide), bf),
               d1a=V((sx, nz, tall, width), bf), d2a=V((sz, tall, width), bf),
               d1b=V((sz, nx, tall, width), bf), d2b=V((sx, tall, width), bf),
               e_sends=dma((items, n_dp)), e_r1=dma((items, big + 1, big)), e_r2=dma((items, big + 1)))
    shapes = (jax.ShapeDtypeStruct((rows, gu.shape[2]), f4), jax.ShapeDtypeStruct((rows_d, width), f4))
    return out, shapes


def reduce_experts(sizes, gu, dn, chunks=4):
    scratch, shapes = expert_scratch(sizes, gu, dn, chunks)
    scratch["local"] = pltpu.SemaphoreType.DMA((4 + chunks,))
    hbm = pl.BlockSpec(memory_space=pl.ANY)
    return pl.pallas_call(
        functools.partial(expert_kernel, sizes, chunks),
        out_shape=shapes, in_specs=[hbm] * 2, out_specs=(hbm,) * 2,
        scratch_shapes=[scratch[n] for n in ExpertScratch._fields],
        compiler_params=pltpu.CompilerParams(collective_id=3, has_side_effects=True, vmem_limit_bytes=60 << 20),
        name="experts",
    )(gu, dn)


def tail_kernel(sizes, experts, chunks, together, names, *refs):
    r = SimpleNamespace(**dict(zip(names, refs)))
    first = pl.ds(0, r.cot.shape[0])
    r.ag, r.dh, r.normed = r.y.at[first], r.ag_, r.dx.at[first]
    r.attended = r.nt = r.layer_out
    r.tokens, r.lse, r.q = r.hn, r.dq, r.cot
    spot = Spot(sizes)
    tail = Tail(spot, experts, r)
    loads = []
    def load(src, dst):
        copy = pltpu.make_async_copy(src, dst, r.local.at[4 + chunks + len(loads)])
        copy.start()
        loads.append(copy)
        return copy
    if together:
        loads_e = load_experts(chunks, r)
    capacity = r.y.shape[0] // experts
    own = slots_of(r.y_hbm, capacity), slots_of(r.dx_hbm, capacity)
    mine = slots_of(r.y, capacity)(spot.ex), slots_of(r.dx, capacity)(spot.ex)
    firsts = [load(own[n](spot.ex), mine[n]) for n in range(2)]
    firsts += [load(*p) for p in ((r.lse_hbm, r.lse), (r.h_hbm, r.tg), (r.hn_hbm, r.hn), (r.cot_hbm, r.cot),
                                  (r.rest_hbm, r.rest), (r.scal_hbm, r.scal), (r.rows_hbm, r.rows))]
    seconds = [load(*p) for p in ((r.k_hbm, r.k), (r.v_hbm, r.v), (r.qkv_hbm, r.qkv))]
    enter(spot, line_neighbours(spot)
          + [(None, expert_device(spot, lax.rem(spot.ex + d, experts))) for d in range(1, experts)])
    target = lambda at: lambda d: at(lax.rem(spot.ex + d, experts))
    returns = [Exchange(spot, experts, n, target(own[n]), slots_of(into, capacity), r.trade)
               for n, into in enumerate((r.y, r.dx))]
    for t in returns:
        for d in range(1, experts):
            t.send(d)
    items, events, stored = [], [], {}
    if together:
        items, events, stored = expert_items(spot, chunks, r)
        start_experts(items, loads_e)
    sems = (r.sends, r.r1, r.r2, r.mates, r.ys, r.outs)
    dense = []
    rounds = tail.pairs // 2
    for j in range(rounds + 1):
        def done(h, v, j=j):
            if j == rounds:
                r.out_out[:, pl.ds(h * v.shape[1], v.shape[1])] = v
            else:
                for part in range(3):
                    cols = pl.ds(part * tail.width + (h * rounds + j) * 128, 128)
                    r.qkv_out[:, cols] = v[:, part * 128 : part * 128 + 128]
        bufs = [b.at[j] for b in (r.mine, r.one, r.two, r.ybuf, r.final, r.other)]
        dense.append(Dense(spot, j, r.own.at[j], bufs, sems, done))
    def done(h, v):
        r.small_out[:, pl.ds(h * 128, 128)] = v
    bufs = [r.mine_s, r.one_s, r.two_s, r.ybuf_s, r.final_s, r.other_s]
    dense.append(Dense(spot, rounds + 1, r.own_small, bufs, sems, done))
    part = functools.partial
    def arrived():
        for copy in firsts:
            copy.wait()
    def returned():
        for t in returns:
            for d in range(1, experts):
                t.receive(d)
    thirds, lasts = [], []
    def smalls():
        tail.small_grad()
        seconds.append(load(r.q_hbm, r.q))
        lasts.append(load(r.tokens_hbm, r.tokens))
    def load_more():
        seconds.append(load(r.normed_hbm, r.normed))
        copy = pltpu.make_async_copy(r.layer_out, r.layer_hbm, r.local.at[2])
        copy.start()
        copy.wait()
        thirds.append(load(r.attended_hbm, r.attended))
    def outs_of():
        thirds.pop().wait()
        tail.out_grad()
        dense[rounds].begin()
    def lasts_ready():
        lasts.pop().wait()
    def ready():
        for copy in seconds:
            copy.wait()
        tail.normed_side()
    plan = []
    def at(time, *pieces):
        plan.extend((time, p) for p in pieces)
    at(4, arrived, tail.prepare)
    at(27, returned)
    at(28, *[part(tail.combine, i) for i in range(2 * tail.blocks)])
    at(37, smalls, load_more)
    at(38, *[part(tail.unproject, i) for i in range(tail.blocks)])
    at(40, outs_of, ready)
    now = 42.0
    at(now + 5, dense[rounds].merge)
    due = [(now + 50, dense[rounds])]
    for j in range(rounds):
        for pair in (j, rounds + j):
            at(now, part(tail.pair_begin, pair))
            for i in range(tail.blocks):
                at(now + 1 + 2 * i, part(tail.attend, pair, i))
            at(now + PAIR - 0.5, part(tail.pair_end, pair))
            now += PAIR
        at(now - 0.4, dense[j].begin)
        at(now + 3, dense[j].merge)
        due.append((now + 3, dense[j]))
    at(now, lasts_ready, *[part(tail.last, i) for i in range(tail.blocks)])
    at(now + 7, tail.small_end, dense[-1].begin)
    at(now + 9, dense[-1].merge)
    due.append((now + 9, dense[-1]))
    busy = FIRST + EACH * (len(items) - 1) if together else 0
    for time, d in due:
        busy = max(busy, time) + DENSE_EACH
        plan += [(busy + after, step) for after, step in d.steps()]
    plan += events
    for _, piece in sorted(plan, key=lambda t: t[0]):
        piece()
    for copy in stored.values():
        copy.wait()
    for t in returns:
        for d in range(1, experts):
            t.drain(d)
    for item in items + dense + [d.reduce for d in dense]:
        for drain in item.drains:
            drain()


def run_tail(sizes, experts, ins, routes_width, chunks=4):
    by = TailIns(*ins)
    nz, nx, ny = sizes[:3]
    n_dp = nz * nx
    length, width = by.cot_hbm.shape
    rows = by.gu_hbm.shape[1]
    slots = by.y_hbm.shape[0]
    assert length == width
    together = n_dp <= 8
    bf, f4 = jnp.bfloat16, jnp.float32
    S, V, dma = jax.ShapeDtypeStruct, pltpu.VMEM, pltpu.SemaphoreType.DMA
    e_scratch, e_shapes = expert_scratch(sizes, by.gu_hbm, by.dn_hbm, chunks)
    shapes = dict(layer_hbm=S((length, width), bf), tg=S((length, width), f4), prev_grad=S((length, routes_width), f4),
                  qkv_out=S((rows, 3 * width), f4), out_out=S((rows, width), f4), small_out=S((rows, 256), f4))
    shapes.update(zip(ExpertOuts._fields, e_shapes))
    kinds = width // 256 + 1
    token, back, pair = V((length, width), bf), V((slots, width), bf), V((length, 128), f4)
    keys = sum(key_range(i)[1] - key_range(i)[0] for i in range(length // BLOCK))
    sx, sz = Reduce.slots(nx), Reduce.slots(nz)
    big = max(nz, nx)
    def buffers(end, lead, cols):
        block = (rows, cols)
        sizes_ = ((n_dp,), (sx, nz), (sz,), (ny,), (), ())
        names = ("mine", "one", "two", "ybuf", "final", "other")
        return {n + end: V(lead + s + block, f4 if j > 3 else bf) for j, (n, s) in enumerate(zip(names, sizes_))}
    scratch = dict(y=back, dx=back, ag_=token, hn=token, k=token, v=token, layer_out=token,
                   low=V((length, 128), bf), coef=V((length, 128), bf), gain_rows=V((8, width), f4),
                   lse_rows=V((16, length), f4), bias=V((keys, BLOCK), bf), kt=V((128, length), bf), dq=pair, dk=pair,
                   dv=pair, own=V((kinds, 2, n_dp, rows, width // 2), bf), own_small=V((2, n_dp, rows, 128), bf),
                   cot=token, qkv=V(by.qkv_hbm.shape, bf), rest=V(by.rest_hbm.shape, bf), scal=pair,
                   rows=V(by.rows_hbm.shape, f4), trade=dma((2, 2, experts)))
    scratch.update(buffers("", (kinds,), width // 2))
    scratch.update(buffers("_s", (), 128))
    scratch.update(sends=dma((kinds + 1, n_dp)), r1=dma((kinds + 1, big + 1, big)), r2=dma((kinds + 1, big + 1)),
                   mates=dma((2, kinds + 1)), ys=dma((2, kinds + 1, ny)), outs=dma((2, kinds + 1)), local=dma((24 + chunks,)))
    if together:
        scratch.update(e_scratch)
    in_names = [n for n in TailIns._fields if together or n not in ExpertIns._fields]
    out_names = [n for n in TailOuts._fields if together or n not in ExpertOuts._fields]
    vmem = pl.BlockSpec(memory_space=pltpu.VMEM)
    hbm = pl.BlockSpec(memory_space=pl.ANY)
    place = lambda names: [hbm if "hbm" in n else vmem for n in names]
    outs = pl.pallas_call(
        functools.partial(tail_kernel, sizes, experts, chunks, together, in_names + out_names + list(scratch)),
        out_shape=tuple(shapes[n] for n in out_names),
        in_specs=place(in_names),
        out_specs=tuple(place(out_names)),
        scratch_shapes=list(scratch.values()),
        compiler_params=pltpu.CompilerParams(collective_id=2, has_side_effects=True, vmem_limit_bytes=67_000_000),
        name="tail",
    )(*(getattr(by, n) for n in in_names))
    out = dict(zip(out_names, outs))
    if not together:
        out.update(zip(ExpertOuts._fields, reduce_experts(sizes, by.gu_hbm, by.dn_hbm, chunks)))
    return [out[n] for n in TailOuts._fields]


def release_kernel(whole, *refs):
    n = len(whole)
    ins, small_ref, outs = refs[:n], refs[n], refs[n + 1 : 2 * n + 1]
    gain_one, gain_two, router, mix, const = refs[2 * n + 1 : 2 * n + 6]
    bufs, sems = refs[2 * n + 6 : 3 * n + 6], refs[3 * n + 6]
    loads = [pltpu.make_async_copy(ins[j], bufs[j], sems.at[0, j]) for j in range(n)]
    stores = [pltpu.make_async_copy(bufs[j], outs[j], sems.at[1, j]) for j in range(n)]
    for l in loads:
        l.start()
    small = small_ref[...]
    rows = small.shape[0]
    eye = lax.broadcasted_iota(jnp.int32, (rows, rows), 0) == lax.broadcasted_iota(jnp.int32, (rows, rows), 1)
    for j, out in enumerate((gain_one, gain_two)):
        out[...] = jnp.sum(jnp.where(eye, small[:, j : j + 1], 0.0), axis=0, keepdims=True)
    mix[...] = small[:, 2:6]
    const[...] = small[:, 6:8]
    router[...] = small[:, 8 : 8 + router.shape[1]]
    for l, s in zip(loads, stores):
        l.wait()
        s.start()
    for s in stores:
        s.wait()


def release(whole, small, choices):
    n, rows = len(whole), small.shape[0]
    S = lambda *shape: jax.ShapeDtypeStruct(shape, jnp.float32)
    hbm, vmem = pl.BlockSpec(memory_space=pl.ANY), pl.BlockSpec(memory_space=pltpu.VMEM)
    return pl.pallas_call(
        functools.partial(release_kernel, tuple(a.shape for a in whole)),
        out_shape=tuple(jax.ShapeDtypeStruct(a.shape, a.dtype) for a in whole)
        + (S(1, rows), S(1, rows), S(rows, choices), S(rows, 4), S(rows, 2)),
        in_specs=[hbm] * n + [vmem],
        out_specs=(hbm,) * n + (vmem,) * 5,
        scratch_shapes=[pltpu.VMEM(a.shape, a.dtype) for a in whole] + [pltpu.SemaphoreType.DMA((2, n))],
        name="release",
    )(*whole, small)


def pair_tables(length):
    half = HEAD_DIM // 2
    inverse = np.float32(10000.0) ** (-(np.arange(half, dtype=np.float32) / np.float32(half)))
    angles = (np.arange(length, dtype=np.float32)[:, None] * inverse[None]).astype(np.float64)
    cosine, sine = np.cos(angles).astype(np.float32), np.sin(angles).astype(np.float32)
    return jnp.asarray(np.tile(cosine, (1, 4))), jnp.asarray(np.tile(np.concatenate([-sine, sine], 1), (1, 2)))


def per_device(
    sizes,
    tokens,
    prev_logits,
    segment_ids,
    pad_mask,
    routes,
    slot_order,
    cotangent,
    attn_gain,
    qkv_weight,
    out_weight,
    ffn_gain,
    router_weight,
    mix_weight,
    const_weight,
    gate_up_weight,
    down_weight,
):
    length, width = tokens.shape
    experts = lax.axis_size("expert") * gate_up_weight.shape[0]
    choices = router_weight.shape[1]
    n_dp = sizes[0] * sizes[1]
    small = jnp.concatenate(
        [attn_gain[:, None], ffn_gain[:, None], mix_weight, const_weight, router_weight], axis=1
    )
    rest = jnp.concatenate([out_weight, jnp.pad(small, ((0, 0), (0, 256 - small.shape[1])))], axis=1)
    cosine, sine = pair_tables(length)
    pairs = routes[0]
    f = FrontOuts(*run_front(
        sizes, experts,
        (tokens, prev_logits, segment_ids, pad_mask, pairs, slot_order.reshape(length, 2), cotangent,
         cosine, sine, qkv_weight, rest, gate_up_weight[0], down_weight[0])))
    by_owner = lambda g: g.reshape(n_dp, g.shape[0] // n_dp, g.shape[1])
    layer_out, gu_shard, dn_shard, tokens_grad, prev_grad, qkv_grad, out_grad, small_grad = run_tail(
        sizes, experts,
        (by_owner(f.gu_grad), by_owner(f.dn_grad), f.y_hbm, f.dx_hbm, f.h_hbm, f.attended_hbm, f.normed_hbm, f.q_hbm, f.k_hbm,
         f.v_hbm, f.hn_hbm, tokens, f.lse_hbm, cotangent, f.qkv_hbm, f.rest_hbm, f.scal_hbm, f.rows_hbm, segment_ids,
         pad_mask, cosine, sine), choices)
    layer_out, tokens_grad, prev_grad, qkv_grad, out_grad, gu_shard, dn_shard, *smalls = release(
        (layer_out, tokens_grad, prev_grad, qkv_grad, out_grad, gu_shard, dn_shard), small_grad, choices)
    gain_one, gain_two, router, mix, const = smalls
    return (
        layer_out,
        tokens_grad,
        prev_grad,
        gain_one[0],
        qkv_grad,
        out_grad,
        gain_two[0],
        router,
        mix,
        const,
        gu_shard[None],
        dn_shard[None],
    )


def grid_sizes(mesh):
    along_dp, along_expert = mesh.devices[:, 0], mesh.devices[0]
    nx = len({d.coords[0] for d in along_dp})
    ny = len({d.coords[1] for d in along_expert})
    return (len(along_dp) // nx, nx, ny, len(along_expert) // ny)


def solution(mesh):
    in_specs = (
        P(("dp", "expert"), None),
        P(("dp", "expert"), None),
        P(("dp", "expert"), None),
        P(("dp", "expert"), None),
        P(("dp", "expert"), None, None),
        P(("dp", "expert"), None),
        P(("dp", "expert"), None),
        P("dp"),
        P("dp", None),
        P("dp", None),
        P("dp"),
        P("dp", None),
        P("dp", None),
        P("dp", None),
        P("expert", "dp", None),
        P("expert", "dp", None),
    )
    out_specs = (
        P(("dp", "expert"), None),
        P(("dp", "expert"), None),
        P(("dp", "expert"), None),
        P("dp"),
        P("dp", None),
        P("dp", None),
        P("dp"),
        P("dp", None),
        P("dp", None),
        P("dp", None),
        P("expert", "dp", None),
        P("expert", "dp", None),
    )
    return jax.shard_map(
        functools.partial(per_device, grid_sizes(mesh)), mesh=mesh, in_specs=in_specs, out_specs=out_specs, check_vma=False
    )
```
